32 devices in a mesh: row: 4 (over y, x), col: 4 (over z), cond: 2 (over core).
Axes of the slice: x: 2, y: 2, z: 4, core: 2. Of those that a mesh axis runs over, the one named last changes fastest.
Arguments:
- mask: float32 [512, 512], P('row', 'col'), may hold values from -1 to 1
- target: int32 [512, 512], P('row', 'col'), may hold values 0 or 1
- cond_index: int32 [4], P('cond'), may hold values from 0 to 7
- kernels: float32 [8, 2, 12, 576], replicated, may hold values from -6 to 6
- dose: float32 [8], replicated, may hold values from 0.7 to 1.4
Outputs:
- mask_grad: float32 [512, 512], P('row', 'col')
The draws below stay inside these ranges and needn't reach their ends.
All inputs are finite; a program needn't handle non-finite values. No bound on the sum of `target` on one device may be relied on, other than what follows from the above.
Results may differ from the reference program's by a relative error of at most 0.0003.
Values sent between devices are 32-bit elements; how exact they have to be, the bound alone decides.
No kernel may reach another device: no remote copies, remote signals or barrier semaphores. Data moves between devices by JAX's collectives and lax.ppermute only.
A program may use at most 64 MiB of HBM per device.

```python
import math
import jax
import jax.numpy as jnp
from jax import lax

TILE = 128
MARGIN = 128
KERNELS = 12
CONDS = 4
SETTINGS = 8
BAND = 24
NR = 512
NC = 512
N_ROW = 4
N_COL = 4


def plant(entries, own_key, smallest, high):
    index_at = [jax.random.randint(jax.random.fold_in(own_key, axis), (), 0, length) for axis, length in enumerate(entries.shape)]
    widest = entries.shape.index(max(entries.shape))
    neighbour = index_at[:widest] + [(index_at[widest] + 1) % entries.shape[widest]] + index_at[widest + 1:]
    return entries.at[tuple(index_at)].set(smallest).at[tuple(neighbour)].set(high)


def shard_levels(key, shape, pieces, low, top_value):
    def one(axis_at, parts):
        steps = jax.random.uniform(jax.random.fold_in(jax.random.fold_in(key, 6), axis_at), (parts,), jnp.float32, low / len(pieces), top_value / len(pieces))
        return jnp.repeat(jnp.exp(steps), shape[axis_at] // parts).reshape((-1,) + (1,) * (len(shape) - axis_at - 1))

    factor_of = one(*pieces[0])
    for cut in pieces[1:]:
        factor_of = factor_of * one(*cut)
    return factor_of


def centred(key, dims, spread, bound, held_as=jnp.bfloat16):
    values = spread * jax.random.normal(key, dims, jnp.float32)
    return jnp.clip(values, min=-bound, max=bound).astype(held_as)


def setup_inputs(seed: int = 0) -> dict:
    arg_keys = jax.random.split(jax.random.key(seed), 6)
    return {
        "mask": jnp.clip(jax.random.uniform(arg_keys[0], (NR, NC), jnp.float32, -1.0, 1.0) * shard_levels(arg_keys[0], (NR, NC), ((0, 4), (1, 4)), -0.4, 0.0), -1.0, 1.0),
        "target": plant((jax.random.randint(arg_keys[1], (NR, NC), 0, 2) < 1).astype(jnp.int32), jax.random.fold_in(arg_keys[1], 1), 0, 1),
        "cond_index": plant(jax.random.randint(arg_keys[2], (CONDS,), 0, SETTINGS), jax.random.fold_in(arg_keys[2], 1), 0, SETTINGS - 1).astype(jnp.int32),
        "kernels": centred(arg_keys[3], (SETTINGS, 2, KERNELS, BAND * BAND), 1.0, 6.0, jnp.float32),
        "dose": jnp.clip(jnp.exp(jax.random.uniform(arg_keys[4], (SETTINGS,), jnp.float32, math.log(0.7), math.log(1.4))), 0.7, 1.4),
    }


STEEP = 4.0
THRESH = 0.6

def highest(left_side, right_side):
    return jnp.dot(left_side, right_side, precision=lax.Precision.HIGHEST, preferred_element_type=jnp.float32)

def tables(length, start, window_size, band_size):
    frequency = jnp.arange(band_size, dtype=jnp.int32) - band_size // 2
    positions = jnp.arange(length, dtype=jnp.int32) + start
    phases = frequency[:, None] * positions[None, :] % window_size
    angles = phases.astype(jnp.float32) * (2.0 * math.pi / window_size)
    return (jnp.cos(angles), jnp.sin(angles))

def row_product(segment, row_start, window_size, band_size):
    cosine_table, sine_table = tables(segment.shape[0], row_start, window_size, band_size)
    return highest(jnp.concatenate([cosine_table, sine_table], axis=0), segment)

def col_product(partial_rows, col_start, window_size, band_size):
    cosine_table, sine_table = tables(partial_rows.shape[1], col_start, window_size, band_size)
    products = highest(partial_rows, jnp.concatenate([cosine_table, sine_table], axis=0).T)
    upper_cos = products[:band_size, :band_size]
    upper_sin = products[:band_size, band_size:]
    lower_cos = products[band_size:, :band_size]
    lower_sin = products[band_size:, band_size:]
    return jnp.stack([upper_cos - lower_sin, -lower_cos - upper_sin]) / window_size

def tile_loss(spectrum, kernel, dose_value, goal_map):
    tile_size = goal_map.shape[0]
    band_size = spectrum.shape[1]
    window_size = tile_size + 2 * MARGIN
    kernel_real = kernel[0].reshape(-1, band_size, band_size)
    kernel_imag = kernel[1].reshape(-1, band_size, band_size)
    kernel_count = kernel_real.shape[0]
    product_real = kernel_real * spectrum[0] - kernel_imag * spectrum[1]
    product_imag = kernel_real * spectrum[1] + kernel_imag * spectrum[0]
    stacked = jnp.concatenate([product_real, product_imag], axis=1)
    stacked = jnp.transpose(stacked, (1, 0, 2)).reshape(2 * band_size, kernel_count * band_size)
    cosine_table, sine_table = tables(tile_size, MARGIN, window_size, band_size)
    cosine_cols = cosine_table.T
    sine_cols = sine_table.T
    inverse_left = jnp.concatenate([jnp.concatenate([cosine_cols, -sine_cols], 1), jnp.concatenate([sine_cols, cosine_cols], 1)], 0)
    partial_rows = highest(inverse_left, stacked)
    rows_real = partial_rows[:tile_size].reshape(tile_size, kernel_count, band_size)
    rows_imag = partial_rows[tile_size:].reshape(tile_size, kernel_count, band_size)
    rows_both = jnp.concatenate([rows_real, rows_imag], axis=2)
    rows_both = jnp.transpose(rows_both, (1, 0, 2)).reshape(kernel_count * tile_size, 2 * band_size)
    inverse_right = jnp.concatenate([jnp.concatenate([cosine_table, sine_table], 1), jnp.concatenate([-sine_table, cosine_table], 1)], 0)
    fields = highest(rows_both, inverse_right)
    squared = (fields * fields).reshape(kernel_count, tile_size, 2, tile_size)
    intensity = lax.optimization_barrier(jnp.sum(squared, axis=(0, 2))) / (kernel_count * band_size * band_size)
    resist = jax.nn.sigmoid(STEEP * (dose_value * intensity - THRESH))
    return jnp.sum(jnp.square(resist - goal_map))

def interior_adjoint(cotangent, tile_size, window_size):
    band_size = cotangent.shape[1]
    cosine_table, sine_table = tables(tile_size, MARGIN, window_size, band_size)
    joined = jnp.concatenate([cotangent[0], cotangent[1]], axis=1)
    right_side = jnp.concatenate([jnp.concatenate([cosine_table, -sine_table], 1), jnp.concatenate([-sine_table, -cosine_table], 1)], 0)
    halves = highest(joined, right_side)
    stacked = jnp.concatenate([halves[:, :tile_size], halves[:, tile_size:]], axis=0)
    left_side = jnp.concatenate([cosine_table, sine_table], axis=0).T
    return highest(left_side, stacked) / window_size

def reference(mask, target, cond_index, kernels, dose):
    window_size = TILE + 2 * MARGIN
    padded = jnp.pad(mask, MARGIN)

    def tile_gradient(position):
        tile_row = position // N_COL
        tile_col = position % N_COL
        window = lax.dynamic_slice(padded, (tile_row * TILE, tile_col * TILE), (window_size, window_size))
        goal_map = lax.dynamic_slice(target, (tile_row * TILE, tile_col * TILE), (TILE, TILE)).astype(jnp.float32)
        spectrum = col_product(row_product(window, 0, window_size, BAND), 0, window_size, BAND)
        summed = jnp.zeros((2, BAND, BAND), jnp.float32)
        for ordinal in range(CONDS):
            setting = cond_index[ordinal]
            kernel = lax.dynamic_index_in_dim(kernels, setting, 0, keepdims=False)
            dose_value = lax.dynamic_index_in_dim(dose, setting, 0, keepdims=False)
            summed = summed + jax.grad(tile_loss)(spectrum, kernel, dose_value, goal_map)
        return interior_adjoint(summed, TILE, window_size)
    gradients = lax.map(tile_gradient, jnp.arange(N_ROW * N_COL, dtype=jnp.int32))
    return gradients.reshape(N_ROW, N_COL, TILE, TILE).transpose(0, 2, 1, 3).reshape(N_ROW * TILE, N_COL * TILE)
```

```python
import functools
import math

import jax
import jax.numpy as jnp
import numpy as np
from jax import lax
from jax.experimental import pallas as pl
from jax.experimental.pallas import tpu as pltpu
from jax.sharding import PartitionSpec as P

MARGIN = 128
BAND = 24
STEEP = 4.0
THRESH = 0.6

HALF = 64
AXES = ("row", "col", "cond")
BF = jnp.bfloat16
F32 = jnp.float32


def pieces(table, count):
    out, rest = [], np.asarray(table, np.float32)
    for _ in range(count):
        part = rest.astype(BF)
        out.append(part)
        rest = rest - part.astype(np.float32)
    return out


def angles(left, right, period):
    left, right = np.asarray(left, np.int64), np.asarray(right, np.int64)
    return (left[:, None] * right[None, :] % period) * (2.0 * math.pi / period)


def frequencies():
    return np.arange(BAND) - BAND // 2


def lanes(*blocks):
    rows = blocks[0][1].shape[0]
    width = -(-max(at + block.shape[1] for at, block in blocks) // 128) * 128
    out = np.zeros((rows, width))
    for at, block in blocks:
        out[:, at : at + block.shape[1]] = block
    return out


def rows_at(height, *blocks):
    out = np.zeros((height, blocks[0][1].shape[1]))
    for at, block in blocks:
        out[at : at + block.shape[0]] = block
    return out


def six(table):
    high, mid, low = pieces(table, 3)
    return np.concatenate([high, high, high, mid, mid, low], 1)


def three(table):
    high, low = pieces(table, 2)
    return np.concatenate([high, high, low], 1)


def stacked(table, count):
    return np.concatenate(pieces(table, count), 0)


def local_tables(tile, window):
    places = np.arange(tile)
    cols = []
    for at, shift in ((0, 0), (HALF, 2 * MARGIN), (2 * HALF, MARGIN), (3 * HALF, MARGIN)):
        phase = angles(places + shift, frequencies(), window)
        cols += [(at, np.cos(phase)), (at + BAND, -np.sin(phase))]
    col_table = lanes(*cols) / window
    real, imag = [], []
    for shift in (MARGIN, 0, 2 * MARGIN):
        phase = angles(frequencies(), places + shift, window)
        real.append(np.cos(phase))
        imag.append(-np.sin(phase))
    row_table = np.concatenate(real + imag, 0)
    return stacked(col_table, 3), six(row_table)


def field_tables(tile, window):
    count = 2 * BAND
    points = np.arange(count)
    phase = angles(frequencies(), points, count)
    cos, sin = np.cos(phase), np.sin(phase)
    real_rows = lanes((0, cos), (HALF, sin), (2 * HALF, -sin), (3 * HALF, cos))
    imag_rows = lanes((0, -sin), (HALF, cos), (2 * HALF, -cos), (3 * HALF, -sin))
    to_cols = rows_at(HALF, (0, real_rows), (BAND, imag_rows))
    to_rows = np.concatenate([cos.T, sin.T], 1)
    where = (np.arange(tile)[:, None] + MARGIN) / window - points[None, :] / count
    spread = np.ones((tile, count))
    for order in range(1, BAND):
        spread += 2.0 * np.cos(2.0 * math.pi * order * where)
    spread /= count
    spread_cols = rows_at(HALF, (0, spread.T))
    gather_cols = lanes((0, spread), (HALF, spread))
    from_rows = np.concatenate([cos, sin], 0)
    pad = np.zeros((HALF - count, BAND))
    c, s = cos.T, sin.T

    def both(real_part, imag_part):
        block = np.concatenate([real_part, imag_part], 1)
        return lanes((0, block), (HALF, block))

    blocks = [both(c, -s), both(s, c), both(-s, -c), both(c, -s)]
    empty = np.zeros((HALF - count, 2 * HALF))
    from_cols = np.concatenate([part for block in blocks for part in (block, empty)], 0)
    return (
        stacked(to_cols, 3),
        six(to_rows),
        stacked(spread_cols, 3),
        six(spread),
        three(spread.T),
        stacked(gather_cols, 2),
        three(from_rows),
        np.concatenate(pieces(from_cols, 2), 1),
    )


def adjoint_tables(tile, window):
    places = np.arange(tile) + MARGIN
    phase = angles(frequencies(), places, window)
    cos, sin = np.cos(phase), np.sin(phase)
    first = np.concatenate([cos, -sin], 1)
    second = np.concatenate([-sin, -cos], 1)
    cols = rows_at(
        2 * HALF, (0, first), (BAND, first), (HALF, second), (HALF + BAND, second)
    )
    rows = np.concatenate([cos.T, sin.T], 1) / window
    return stacked(cols, 2), three(rows)


def dot(left, right):
    return jnp.dot(left, right, preferred_element_type=F32)


def split(value, count):
    out, rest = [], value
    for step in range(count):
        part = rest.astype(BF)
        out.append(part)
        if step + 1 < count:
            rest = rest - part.astype(F32)
    return out


def lane_ids(shape):
    return lax.broadcasted_iota(jnp.int32, shape, len(shape) - 1)


def doubled(value):
    low_half = lane_ids(value.shape) < HALF
    high = value.astype(BF).astype(F32)
    rest = value - high
    mid = rest.astype(BF).astype(F32)
    first = jnp.where(low_half, high, rest).astype(BF)
    second = jnp.where(low_half, rest - mid, high).astype(BF)
    return jnp.concatenate([first, first, second], 1)


def doubled_weights(ref):
    size = ref.shape[0] // 3
    high, mid, low = ref[:size], ref[size : 2 * size], ref[2 * size :]
    return jnp.concatenate([high, high, mid, mid, high, low], 0)


def six_right(value):
    high, mid, low = split(value, 3)
    return jnp.concatenate([high, mid, low, high, mid, high], 0)


def three_right(value):
    high, low = split(value, 2)
    return jnp.concatenate([high, low, high], 0)


def local_kernel(where_ref, mask_ref, col_ref, row_ref, own_ref, send_ref):
    tile = mask_ref.shape[0]
    high, mid, low = split(mask_ref[...], 3)
    left = jnp.concatenate([high, mid, low, high, mid, high], 1)
    ch, cm, cl = col_ref[:tile], col_ref[tile : 2 * tile], col_ref[2 * tile :]
    right = jnp.concatenate([ch, ch, ch, cm, cm, cl], 0)
    partial = dot(left, right)
    both = dot(row_ref[...], six_right(partial))
    top, bottom = both[: 3 * BAND], both[3 * BAND :]
    lane = lane_ids(top.shape) % HALF
    width = top.shape[1]
    turned = jnp.where(
        lane < BAND,
        -pltpu.roll(bottom, width - BAND, 1),
        jnp.where(lane < 2 * BAND, pltpu.roll(bottom, BAND, 1), 0.0),
    )
    result = top + turned
    own = result[:BAND]
    below = result[BAND : 2 * BAND]
    above = result[2 * BAND :]
    down, valid = where_ref[0], where_ref[1]
    chosen = jnp.where(down == 1, below, above)
    chosen = jnp.where(valid == 1, chosen, 0.0)
    own_ref[:BAND] = own[:, : 2 * HALF]
    own_ref[BAND:] = own[:, 2 * HALF :]
    send_ref[:BAND] = chosen[:, : 2 * HALF]
    send_ref[BAND:] = chosen[:, 2 * HALF :]


def field_kernel(
    where_ref, cond_ref, dose_ref, own_ref, near_ref, far_ref, side_ref, other_ref, ker_a_ref,
    ker_b_ref, target_ref, to_cols_ref, to_rows_ref, spread_cols_ref, spread_ref,
    gather_rows_ref, gather_cols_ref, from_rows_ref, from_cols_ref, out_ref, cols_ref, field_ref,
):
    conds = cond_ref.shape[0]
    count = 2 * BAND
    total = ker_a_ref.shape[0] // BAND
    per = total // conds
    tile = target_ref.shape[0]

    def half(value, first, valid):
        keep = (lane_ids(value.shape) < HALF) == (first == 1)
        kept = jnp.where(keep & (valid == 1), value, 0.0)
        return kept + pltpu.roll(kept, HALF, 1)

    spectrum = own_ref[BAND:] + near_ref[BAND:] + far_ref[BAND:]
    spectrum += half(side_ref[...], where_ref[2], where_ref[3])
    spectrum += half(other_ref[...], where_ref[4], where_ref[5])
    lane = lane_ids(spectrum.shape) % HALF
    real = jnp.where(lane < BAND, spectrum, 0.0)
    imag = jnp.where(lane >= BAND, spectrum, 0.0)
    real = real + pltpu.roll(real, BAND, 1)
    imag = imag + pltpu.roll(imag, 2 * HALF - BAND, 1)

    ker_a = ker_a_ref[...].reshape(total, BAND, 2 * HALF)
    ker_b = ker_b_ref[...].reshape(total, BAND, 2 * HALF)
    product = (ker_a * real[None] + ker_b * imag[None]).reshape(total * BAND, 2 * HALF)
    cols_ref[...] = dot(doubled(product), doubled_weights(to_cols_ref))

    sums = [jnp.zeros((count, 2 * HALF), F32) for _ in range(conds)]
    to_rows = to_rows_ref[...]
    for pair in range(total // 2):
        rights = []
        for k in (2 * pair, 2 * pair + 1):
            block = cols_ref[k * BAND : (k + 1) * BAND, :]
            block = jnp.concatenate([block[:, : 2 * HALF], block[:, 2 * HALF :]], 0)
            rights.append(six_right(block))
        both = dot(to_rows, jnp.concatenate(rights, 1))
        field_ref[pair] = both
        squares = both * both
        for part in range(2):
            c = (2 * pair + part) // per
            sums[c] = sums[c] + squares[:, part * 2 * HALF : (part + 1) * 2 * HALF]

    coarse = jnp.concatenate([value + pltpu.roll(value, HALF, 1) for value in sums], 0)
    wide = dot(doubled(coarse), doubled_weights(spread_cols_ref))
    right = jnp.concatenate(
        [six_right(wide[c * count : (c + 1) * count]) for c in range(conds)], 1
    )
    image = dot(spread_ref[...], right)

    goal = target_ref[...].astype(F32)
    norm = 1.0 / (per * BAND * BAND)
    slopes = []
    for c in range(conds):
        strength = dose_ref[cond_ref[c]]
        intensity = image[:, c * tile : (c + 1) * tile] * norm
        resist = jax.nn.sigmoid(STEEP * (strength * intensity - THRESH))
        slope = (resist - goal) * resist * (1.0 - resist)
        slopes.append(slope * (4.0 * STEEP * norm * strength))
    back = dot(gather_rows_ref[...], three_right(jnp.concatenate(slopes, 1)))
    high, low = split(
        jnp.concatenate([back[:, c * tile : (c + 1) * tile] for c in range(conds)], 0), 2
    )
    gh, gl = gather_cols_ref[:tile], gather_cols_ref[tile:]
    slope = dot(
        jnp.concatenate([high, low, high], 1), jnp.concatenate([gh, gh, gl], 0)
    )

    from_rows = from_rows_ref[...]
    for pair in range(total // 2):
        weight = [
            slope[((2 * pair + part) // per) * count : ((2 * pair + part) // per + 1) * count]
            for part in range(2)
        ]
        scaled = field_ref[pair] * jnp.concatenate(weight, 1)
        back = dot(from_rows, three_right(scaled))
        for part in range(2):
            block = back[:, part * 2 * HALF : (part + 1) * 2 * HALF]
            k = 2 * pair + part
            cols_ref[k * BAND : (k + 1) * BAND, :] = jnp.concatenate(
                [block[:BAND], block[BAND:]], 1
            )
    high, low = split(cols_ref[...], 2)
    weights = from_cols_ref[...]
    first = dot(high, weights)
    back = first[:, : 2 * HALF] + first[:, 2 * HALF :] + dot(low, weights[:, : 2 * HALF])
    back = back.reshape(total, BAND, 2 * HALF)
    sum_a = jnp.sum(ker_a_ref[...].reshape(total, BAND, 2 * HALF) * back, axis=0)
    sum_b = jnp.sum(ker_b_ref[...].reshape(total, BAND, 2 * HALF) * back, axis=0)
    out_ref[...] = jnp.where(lane_ids(sum_a.shape) < HALF, sum_a, sum_b)


def adjoint_kernel(mine_ref, theirs_ref, cols_ref, rows_ref, out_ref):
    tile = out_ref.shape[1]
    high, low = split(mine_ref[...] + theirs_ref[...], 2)
    size = cols_ref.shape[0] // 2
    ch, cl = cols_ref[:size], cols_ref[size:]
    halves = dot(jnp.concatenate([high, low, high], 1), jnp.concatenate([ch, ch, cl], 0))
    joined = jnp.concatenate([halves[:, :tile], halves[:, tile:]], 0)
    out_ref[...] = dot(rows_ref[...], three_right(joined))


VMEM = pl.BlockSpec(memory_space=pltpu.VMEM)
SMEM = pl.BlockSpec(memory_space=pltpu.SMEM)


def call(body, outs, specs, args, scratch=(), flops=1000000):
    shapes = [jax.ShapeDtypeStruct(shape, F32) for shape in outs]
    one = len(outs) == 1
    return pl.pallas_call(
        body,
        out_shape=shapes[0] if one else shapes,
        in_specs=specs,
        out_specs=VMEM if one else [VMEM] * len(outs),
        scratch_shapes=list(scratch),
        cost_estimate=pl.CostEstimate(flops=flops, bytes_accessed=1000000, transcendentals=0),
    )(*args)


def partner(at, core, size):
    other = at ^ 1 if core == 0 else ((at + 1) ^ 1) - 1
    return other if 0 <= other < size else None


def swaps(mesh_shape, along):
    rows, cols, cores = mesh_shape
    out = []
    for r in range(rows):
        for c in range(cols):
            for k in range(cores):
                at, size = (r, rows) if along == 0 else (c, cols)
                other = partner(at, k, size)
                if other is not None:
                    to = (other, c, k) if along == 0 else (r, other, k)
                elif along == 0:
                    to = (r, c ^ 1, k)
                else:
                    to = (r ^ 1, c, k)
                if to[0] < rows and to[1] < cols:
                    out.append((((r * cols) + c) * cores + k, ((to[0] * cols) + to[1]) * cores + to[2]))
    return out


def toward(at, core, size):
    onward = (at + core) % 2 == 0
    other = jnp.where(onward, at + 1, at - 1)
    valid = (other >= 0) & (other < size)
    return onward.astype(jnp.int32), valid.astype(jnp.int32)


def shards(mesh_shape, mask, target, cond_index, kernels, dose):
    tile = mask.shape[0]
    window = tile + 2 * MARGIN
    rows, cols, cores = mesh_shape
    row, col, core = (lax.axis_index(name) for name in AXES)
    down, valid = toward(row, core, rows)
    right, side_valid = toward(col, core, cols)
    other_right, other_valid = toward(col, 1 - core, cols)
    where = jnp.stack([down, valid, 1 - right, side_valid, 1 - other_right, other_valid])

    col_table, row_table = local_tables(tile, window)
    block = (2 * BAND, 2 * HALF)
    own, send = call(
        local_kernel, [block, block], [SMEM, VMEM, VMEM, VMEM], (where, mask, col_table, row_table)
    )
    swap = [(0, 1), (1, 0)]
    near = lax.ppermute(send, AXES, swaps(mesh_shape, 0))
    far = lax.ppermute(near, "cond", swap)
    message = own[:BAND] + near[:BAND] + far[:BAND]
    side = lax.ppermute(message, AXES, swaps(mesh_shape, 1))
    other = lax.ppermute(side, "cond", swap)

    conds = cond_index.shape[0]
    count = kernels.shape[2]
    chosen = [
        lax.dynamic_index_in_dim(kernels, cond_index[c], 0, keepdims=False).reshape(
            2, count * BAND, BAND
        )
        for c in range(conds)
    ]
    real = jnp.concatenate([value[0] for value in chosen], 0)
    imag = jnp.concatenate([value[1] for value in chosen], 0)
    gap = jnp.zeros((real.shape[0], HALF - 2 * BAND), F32)
    ker_a = jnp.concatenate([real, imag, gap] * 2, 1)
    ker_b = jnp.concatenate([-imag, real, gap] * 2, 1)

    total = conds * count
    cotangent = call(
        field_kernel,
        [(BAND, 2 * HALF)],
        [SMEM] * 3 + [VMEM] * 16,
        (where, cond_index, dose, own, near, far, side, other, ker_a, ker_b, target)
        + field_tables(tile, window),
        scratch=[
            pltpu.VMEM((total * BAND, 4 * HALF), F32),
            pltpu.VMEM((total // 2, 2 * BAND, 4 * HALF), F32),
        ],
    )
    theirs = lax.ppermute(cotangent, "cond", swap)
    return call(
        adjoint_kernel, [(tile, tile)], [VMEM] * 4, (cotangent, theirs) + adjoint_tables(tile, window)
    )


def solution(mesh):
    in_specs = (P("row", "col"), P("row", "col"), P("cond"), P(), P())
    out_specs = P("row", "col")
    shape = tuple(mesh.shape[name] for name in AXES)
    body = functools.partial(shards, shape)
    return jax.shard_map(body, mesh=mesh, in_specs=in_specs, out_specs=out_specs, check_vma=False)
```

```python
import functools
import math

import jax
import jax.numpy as jnp
import numpy as np
from jax import lax
from jax.experimental import pallas as pl
from jax.experimental.pallas import tpu as pltpu
from jax.sharding import PartitionSpec as P

MARGIN = 128
BAND = 24
STEEP = 4.0
THRESH = 0.6

HALF = 64
AXES = ("row", "col", "cond")
BF = jnp.bfloat16
F32 = jnp.float32


def pieces(table, count):
    out, rest = [], np.asarray(table, np.float32)
    for _ in range(count):
        part = rest.astype(BF)
        out.append(part)
        rest = rest - part.astype(np.float32)
    return out


def angles(left, right, period):
    left, right = np.asarray(left, np.int64), np.asarray(right, np.int64)
    return (left[:, None] * right[None, :] % period) * (2.0 * math.pi / period)


def frequencies():
    return np.arange(BAND) - BAND // 2


def lanes(*blocks):
    rows = blocks[0][1].shape[0]
    width = -(-max(at + block.shape[1] for at, block in blocks) // 128) * 128
    out = np.zeros((rows, width))
    for at, block in blocks:
        out[:, at : at + block.shape[1]] = block
    return out


def rows_at(height, *blocks):
    out = np.zeros((height, blocks[0][1].shape[1]))
    for at, block in blocks:
        out[at : at + block.shape[0]] = block
    return out


def six(table):
    high, mid, low = pieces(table, 3)
    return np.concatenate([high, high, high, mid, mid, low], 1)


def three(table):
    high, low = pieces(table, 2)
    return np.concatenate([high, high, low], 1)


def stacked(table, count):
    return np.concatenate(pieces(table, count), 0)


def local_tables(tile, window):
    places = np.arange(tile)
    cols = []
    for at, shift in ((0, 0), (HALF, 2 * MARGIN), (2 * HALF, MARGIN), (3 * HALF, MARGIN)):
        phase = angles(places + shift, frequencies(), window)
        cols += [(at, np.cos(phase)), (at + BAND, -np.sin(phase))]
    col_table = lanes(*cols) / window
    real, imag = [], []
    for shift in (MARGIN, 0, 2 * MARGIN):
        phase = angles(frequencies(), places + shift, window)
        real.append(np.cos(phase))
        imag.append(-np.sin(phase))
    row_table = np.concatenate(real + imag, 0)
    return stacked(col_table, 3), six(row_table)


def field_tables(tile, window):
    count = 2 * BAND
    points = np.arange(count)
    phase = angles(frequencies(), points, count)
    cos, sin = np.cos(phase), np.sin(phase)
    real_rows = lanes((0, cos), (HALF, sin), (2 * HALF, -sin), (3 * HALF, cos))
    imag_rows = lanes((0, -sin), (HALF, cos), (2 * HALF, -cos), (3 * HALF, -sin))
    to_cols = rows_at(HALF, (0, real_rows), (BAND, imag_rows))
    to_rows = np.concatenate([cos.T, sin.T], 1)
    where = (np.arange(tile)[:, None] + MARGIN) / window - points[None, :] / count
    spread = np.ones((tile, count))
    for order in range(1, BAND):
        spread += 2.0 * np.cos(2.0 * math.pi * order * where)
    spread /= count
    spread_cols = rows_at(HALF, (0, spread.T))
    gather_cols = lanes((0, spread), (HALF, spread))
    from_rows = np.concatenate([cos, sin], 0)
    pad = np.zeros((HALF - count, BAND))
    c, s = cos.T, sin.T

    def both(real_part, imag_part):
        block = np.concatenate([real_part, imag_part], 1)
        return lanes((0, block), (HALF, block))

    blocks = [both(c, -s), both(s, c), both(-s, -c), both(c, -s)]
    empty = np.zeros((HALF - count, 2 * HALF))
    from_cols = np.concatenate([part for block in blocks for part in (block, empty)], 0)
    return (
        stacked(to_cols, 3),
        six(to_rows),
        stacked(spread_cols, 3),
        six(spread),
        three(spread.T),
        stacked(gather_cols, 2),
        three(from_rows),
        np.concatenate(pieces(from_cols, 2), 1),
    )


def adjoint_tables(tile, window):
    places = np.arange(tile) + MARGIN
    phase = angles(frequencies(), places, window)
    cos, sin = np.cos(phase), np.sin(phase)
    first = np.concatenate([cos, -sin], 1)
    second = np.concatenate([-sin, -cos], 1)
    cols = rows_at(
        2 * HALF, (0, first), (BAND, first), (HALF, second), (HALF + BAND, second)
    )
    rows = np.concatenate([cos.T, sin.T], 1) / window
    return stacked(cols, 2), three(rows)


def toward(at, core, size):
    onward = lax.rem(at + core, 2) == 0
    other = jnp.where(onward, at + 1, at - 1)
    return onward, (other >= 0) & (other < size)


def dot(left, right):
    return jnp.dot(left, right, preferred_element_type=F32)


def split(value, count):
    out, rest = [], value
    for step in range(count):
        part = rest.astype(BF)
        out.append(part)
        if step + 1 < count:
            rest = rest - part.astype(F32)
    return out


def lane_ids(shape):
    return lax.broadcasted_iota(jnp.int32, shape, len(shape) - 1)


def doubled(value):
    low_half = lane_ids(value.shape) < HALF
    high = value.astype(BF).astype(F32)
    rest = value - high
    mid = rest.astype(BF).astype(F32)
    first = jnp.where(low_half, high, rest).astype(BF)
    second = jnp.where(low_half, rest - mid, high).astype(BF)
    return jnp.concatenate([first, first, second], 1)


def doubled_weights(ref):
    size = ref.shape[0] // 3
    high, mid, low = ref[:size], ref[size : 2 * size], ref[2 * size :]
    return jnp.concatenate([high, high, mid, mid, high, low], 0)


def six_right(value):
    high, mid, low = split(value, 3)
    return jnp.concatenate([high, mid, low, high, mid, high], 0)


def three_right(value):
    high, low = split(value, 2)
    return jnp.concatenate([high, low, high], 0)


def local_kernel(mesh_shape, mask_ref, col_ref, row_ref, own_ref, send_ref):
    tile = mask_ref.shape[0]
    high, mid, low = split(mask_ref[...], 3)
    left = jnp.concatenate([high, mid, low, high, mid, high], 1)
    ch, cm, cl = col_ref[:tile], col_ref[tile : 2 * tile], col_ref[2 * tile :]
    right = jnp.concatenate([ch, ch, ch, cm, cm, cl], 0)
    partial = dot(left, right)
    both = dot(row_ref[...], six_right(partial))
    top, bottom = both[: 3 * BAND], both[3 * BAND :]
    lane = lane_ids(top.shape) % HALF
    width = top.shape[1]
    turned = jnp.where(
        lane < BAND,
        -pltpu.roll(bottom, width - BAND, 1),
        jnp.where(lane < 2 * BAND, pltpu.roll(bottom, BAND, 1), 0.0),
    )
    result = top + turned
    own = result[:BAND]
    below = result[BAND : 2 * BAND]
    above = result[2 * BAND :]
    down, valid = toward(lax.axis_index("row"), lax.axis_index("cond"), mesh_shape[0])
    chosen = jnp.where(down, below, above)
    chosen = jnp.where(valid, chosen, 0.0)
    own_ref[:BAND] = own[:, : 2 * HALF]
    own_ref[BAND:] = own[:, 2 * HALF :]
    send_ref[:BAND] = chosen[:, : 2 * HALF]
    send_ref[BAND:] = chosen[:, 2 * HALF :]


def select_kernel(cond_ref, dose_ref, kernels_ref, out_ref, strength_ref, sems):
    conds = cond_ref.shape[0]
    copies = [
        pltpu.make_async_copy(kernels_ref.at[cond_ref[c]], out_ref.at[c], sems.at[c])
        for c in range(conds)
    ]
    for copy in copies:
        copy.start()
    for c in range(conds):
        strength_ref[c] = jnp.full(strength_ref.shape[1:], dose_ref[cond_ref[c]], F32)
    for copy in copies:
        copy.wait()


def field_kernel(
    mesh_shape, strength_ref, own_ref, near_ref, far_ref, side_ref, other_ref, ker_a_ref,
    ker_b_ref, target_ref, to_cols_ref, to_rows_ref, spread_cols_ref, spread_ref,
    gather_rows_ref, gather_cols_ref, from_rows_ref, from_cols_ref, out_ref, cols_ref, field_ref,
):
    conds = strength_ref.shape[0]
    count = 2 * BAND
    total = ker_a_ref.shape[0] // BAND
    per = total // conds
    tile = target_ref.shape[0]

    col, core = lax.axis_index("col"), lax.axis_index("cond")

    def half(value, core):
        onward, valid = toward(col, core, mesh_shape[1])
        low_half = lane_ids(value.shape) < HALF
        kept = jnp.where(onward, jnp.where(low_half, 0.0, value), jnp.where(low_half, value, 0.0))
        kept = jnp.where(valid, kept, 0.0)
        return kept + pltpu.roll(kept, HALF, 1)

    spectrum = own_ref[BAND:] + near_ref[BAND:] + far_ref[BAND:]
    spectrum += half(side_ref[...], core) + half(other_ref[...], 1 - core)
    lane = lane_ids(spectrum.shape) % HALF
    real = jnp.where(lane < BAND, spectrum, 0.0)
    imag = jnp.where(lane >= BAND, spectrum, 0.0)
    real = real + pltpu.roll(real, BAND, 1)
    imag = imag + pltpu.roll(imag, 2 * HALF - BAND, 1)

    ker_a = ker_a_ref[...].reshape(total, BAND, 2 * HALF)
    ker_b = ker_b_ref[...].reshape(total, BAND, 2 * HALF)
    product = (ker_a * real[None] + ker_b * imag[None]).reshape(total * BAND, 2 * HALF)
    cols_ref[...] = dot(doubled(product), doubled_weights(to_cols_ref))

    sums = [jnp.zeros((count, 2 * HALF), F32) for _ in range(conds)]
    to_rows = to_rows_ref[...]
    for pair in range(total // 2):
        rights = []
        for k in (2 * pair, 2 * pair + 1):
            block = cols_ref[k * BAND : (k + 1) * BAND, :]
            block = jnp.concatenate([block[:, : 2 * HALF], block[:, 2 * HALF :]], 0)
            rights.append(six_right(block))
        both = dot(to_rows, jnp.concatenate(rights, 1))
        field_ref[pair] = both
        squares = both * both
        for part in range(2):
            c = (2 * pair + part) // per
            sums[c] = sums[c] + squares[:, part * 2 * HALF : (part + 1) * 2 * HALF]

    coarse = jnp.concatenate([value + pltpu.roll(value, HALF, 1) for value in sums], 0)
    wide = dot(doubled(coarse), doubled_weights(spread_cols_ref))
    right = jnp.concatenate(
        [six_right(wide[c * count : (c + 1) * count]) for c in range(conds)], 1
    )
    image = dot(spread_ref[...], right)

    goal = target_ref[...].astype(F32)
    norm = 1.0 / (per * BAND * BAND)
    slopes = []
    for c in range(conds):
        strength = strength_ref[c][:1]
        intensity = image[:, c * tile : (c + 1) * tile] * norm
        resist = jax.nn.sigmoid(STEEP * (strength * intensity - THRESH))
        slope = (resist - goal) * resist * (1.0 - resist)
        slopes.append(slope * (4.0 * STEEP * norm * strength))
    back = dot(gather_rows_ref[...], three_right(jnp.concatenate(slopes, 1)))
    high, low = split(
        jnp.concatenate([back[:, c * tile : (c + 1) * tile] for c in range(conds)], 0), 2
    )
    gh, gl = gather_cols_ref[:tile], gather_cols_ref[tile:]
    slope = dot(
        jnp.concatenate([high, low, high], 1), jnp.concatenate([gh, gh, gl], 0)
    )

    from_rows = from_rows_ref[...]
    for pair in range(total // 2):
        weight = [
            slope[((2 * pair + part) // per) * count : ((2 * pair + part) // per + 1) * count]
            for part in range(2)
        ]
        scaled = field_ref[pair] * jnp.concatenate(weight, 1)
        back = dot(from_rows, three_right(scaled))
        for part in range(2):
            block = back[:, part * 2 * HALF : (part + 1) * 2 * HALF]
            k = 2 * pair + part
            cols_ref[k * BAND : (k + 1) * BAND, :] = jnp.concatenate(
                [block[:BAND], block[BAND:]], 1
            )
    high, low = split(cols_ref[...], 2)
    weights = from_cols_ref[...]
    first = dot(high, weights)
    back = first[:, : 2 * HALF] + first[:, 2 * HALF :] + dot(low, weights[:, : 2 * HALF])
    back = back.reshape(total, BAND, 2 * HALF)
    sum_a = jnp.sum(ker_a_ref[...].reshape(total, BAND, 2 * HALF) * back, axis=0)
    sum_b = jnp.sum(ker_b_ref[...].reshape(total, BAND, 2 * HALF) * back, axis=0)
    out_ref[...] = jnp.where(lane_ids(sum_a.shape) < HALF, sum_a, sum_b)


def adjoint_kernel(mine_ref, theirs_ref, cols_ref, rows_ref, out_ref):
    tile = out_ref.shape[1]
    high, low = split(mine_ref[...] + theirs_ref[...], 2)
    size = cols_ref.shape[0] // 2
    ch, cl = cols_ref[:size], cols_ref[size:]
    halves = dot(jnp.concatenate([high, low, high], 1), jnp.concatenate([ch, ch, cl], 0))
    joined = jnp.concatenate([halves[:, :tile], halves[:, tile:]], 0)
    out_ref[...] = dot(rows_ref[...], three_right(joined))


VMEM = pl.BlockSpec(memory_space=pltpu.VMEM)
SMEM = pl.BlockSpec(memory_space=pltpu.SMEM)


def call(body, outs, specs, args, scratch=(), flops=1000000, grant=8):
    shapes = [jax.ShapeDtypeStruct(shape, F32) for shape in outs]
    one = len(outs) == 1
    return pl.pallas_call(
        body,
        out_shape=shapes[0] if one else shapes,
        in_specs=specs,
        out_specs=VMEM if one else [VMEM] * len(outs),
        scratch_shapes=list(scratch),
        compiler_params=pltpu.CompilerParams(vmem_limit_bytes=grant * 2**20),
        cost_estimate=pl.CostEstimate(flops=flops, bytes_accessed=1000000, transcendentals=0),
    )(*args)


def partner(at, core, size):
    other = at ^ 1 if core == 0 else ((at + 1) ^ 1) - 1
    return other if 0 <= other < size else None


def swaps(mesh_shape, along):
    rows, cols, cores = mesh_shape
    out = []
    for r in range(rows):
        for c in range(cols):
            for k in range(cores):
                at, size = (r, rows) if along == 0 else (c, cols)
                other = partner(at, k, size)
                if other is not None:
                    to = (other, c, k) if along == 0 else (r, other, k)
                elif along == 0:
                    to = (r, c ^ 1, k)
                else:
                    to = (r ^ 1, c, k)
                if to[0] < rows and to[1] < cols:
                    out.append((((r * cols) + c) * cores + k, ((to[0] * cols) + to[1]) * cores + to[2]))
    return out


def shards(mesh_shape, mask, target, cond_index, kernels, dose):
    tile = mask.shape[0]
    window = tile + 2 * MARGIN
    col_table, row_table = local_tables(tile, window)
    block = (2 * BAND, 2 * HALF)
    own, send = call(
        functools.partial(local_kernel, mesh_shape), [block] * 2, [VMEM] * 3,
        (mask, col_table, row_table),
    )
    swap = [(0, 1), (1, 0)]
    near = lax.ppermute(send, AXES, swaps(mesh_shape, 0))
    far = lax.ppermute(near, "cond", swap)
    message = own[:BAND] + near[:BAND] + far[:BAND]
    side = lax.ppermute(message, AXES, swaps(mesh_shape, 1))
    other = lax.ppermute(side, "cond", swap)

    conds = cond_index.shape[0]
    count = kernels.shape[2]
    chosen, strength = call(
        select_kernel, [(conds, count, 2, BAND * BAND), (conds, 8, tile)],
        [SMEM, SMEM, pl.BlockSpec(memory_space=pl.ANY)],
        (cond_index, dose, jnp.transpose(kernels, (0, 2, 1, 3))),
        scratch=[pltpu.SemaphoreType.DMA((conds,))],
    )
    real = chosen[:, :, 0].reshape(conds * count * BAND, BAND)
    imag = chosen[:, :, 1].reshape(conds * count * BAND, BAND)
    gap = jnp.zeros((real.shape[0], HALF - 2 * BAND), F32)
    ker_a = jnp.concatenate([real, imag, gap] * 2, 1)
    ker_b = jnp.concatenate([-imag, real, gap] * 2, 1)

    total = conds * count
    cotangent = call(
        functools.partial(field_kernel, mesh_shape),
        [(BAND, 2 * HALF)],
        [VMEM] * 17,
        (strength, own, near, far, side, other, ker_a, ker_b, target)
        + field_tables(tile, window),
        scratch=[
            pltpu.VMEM((total * BAND, 4 * HALF), F32),
            pltpu.VMEM((total // 2, 2 * BAND, 4 * HALF), F32),
        ],
    )
    theirs = lax.ppermute(cotangent, "cond", swap)
    return call(
        adjoint_kernel, [(tile, tile)], [VMEM] * 4, (cotangent, theirs) + adjoint_tables(tile, window)
    )


def solution(mesh):
    in_specs = (P("row", "col"), P("row", "col"), P("cond"), P(), P())
    out_specs = P("row", "col")
    shape = tuple(mesh.shape[name] for name in AXES)
    body = functools.partial(shards, shape)
    return jax.shard_map(body, mesh=mesh, in_specs=in_specs, out_specs=out_specs, check_vma=False)
```

```python
import functools
import math

import jax
import jax.numpy as jnp
import numpy as np
from jax import lax
from jax.experimental import pallas as pl
from jax.experimental.pallas import tpu as pltpu
from jax.sharding import PartitionSpec as P

MARGIN = 128
BAND = 24
STEEP = 4.0
THRESH = 0.6

HALF = 64
AXES = ("row", "col", "cond")
BF = jnp.bfloat16
F32 = jnp.float32


def pieces(table, count):
    out, rest = [], np.asarray(table, np.float32)
    for _ in range(count):
        part = rest.astype(BF)
        out.append(part)
        rest = rest - part.astype(np.float32)
    return out


def angles(left, right, period):
    left, right = np.asarray(left, np.int64), np.asarray(right, np.int64)
    return (left[:, None] * right[None, :] % period) * (2.0 * math.pi / period)


def frequencies():
    return np.arange(BAND) - BAND // 2


def lanes(*blocks):
    rows = blocks[0][1].shape[0]
    width = -(-max(at + block.shape[1] for at, block in blocks) // 128) * 128
    out = np.zeros((rows, width))
    for at, block in blocks:
        out[:, at : at + block.shape[1]] = block
    return out


def rows_at(height, *blocks):
    out = np.zeros((height, blocks[0][1].shape[1]))
    for at, block in blocks:
        out[at : at + block.shape[0]] = block
    return out


def six(table):
    high, mid, low = pieces(table, 3)
    return np.concatenate([high, high, high, mid, mid, low], 1)


def three(table):
    high, low = pieces(table, 2)
    return np.concatenate([high, high, low], 1)


def stacked(table, count):
    return np.concatenate(pieces(table, count), 0)


def local_tables(tile, window):
    places = np.arange(tile)
    cols = []
    for at, shift in ((0, 0), (HALF, 2 * MARGIN), (2 * HALF, MARGIN), (3 * HALF, MARGIN)):
        phase = angles(places + shift, frequencies(), window)
        cols += [(at, np.cos(phase)), (at + BAND, -np.sin(phase))]
    col_table = lanes(*cols) / window
    real, imag = [], []
    for shift in (MARGIN, 0, 2 * MARGIN):
        phase = angles(frequencies(), places + shift, window)
        real.append(np.cos(phase))
        imag.append(-np.sin(phase))
    row_table = np.concatenate(real + imag, 0)
    return stacked(col_table, 3), six(row_table)


def field_tables(tile, window):
    count = 2 * BAND
    points = np.arange(count)
    phase = angles(frequencies(), points, count)
    cos, sin = np.cos(phase), np.sin(phase)
    real_rows = lanes((0, cos), (HALF, sin), (2 * HALF, -sin), (3 * HALF, cos))
    imag_rows = lanes((0, -sin), (HALF, cos), (2 * HALF, -cos), (3 * HALF, -sin))
    to_cols = rows_at(
        2 * HALF,
        (0, real_rows),
        (BAND, imag_rows),
        (HALF, imag_rows),
        (HALF + BAND, -real_rows),
    )
    to_rows = np.concatenate([cos.T, sin.T], 1)
    where = (np.arange(tile)[:, None] + MARGIN) / window - points[None, :] / count
    spread = np.ones((tile, count))
    for order in range(1, BAND):
        spread += 2.0 * np.cos(2.0 * math.pi * order * where)
    spread /= count
    spread_cols = rows_at(HALF, (0, spread.T))
    gather_cols = lanes((0, spread), (HALF, spread))
    from_rows = np.concatenate([cos, sin], 0)
    pad = np.zeros((HALF - count, BAND))
    c, s = cos.T, sin.T

    def both(real_part, imag_part):
        return lanes((0, real_part), (BAND, imag_part), (HALF, imag_part), (HALF + BAND, -real_part))

    blocks = [both(c, -s), both(s, c), both(-s, -c), both(c, -s)]
    empty = np.zeros((HALF - count, 2 * HALF))
    from_cols = np.concatenate([part for block in blocks for part in (block, empty)], 0)
    return (
        stacked(to_cols, 3),
        six(to_rows),
        stacked(spread_cols, 3),
        six(spread),
        three(spread.T),
        stacked(gather_cols, 2),
        three(from_rows),
        np.concatenate(pieces(from_cols, 2), 1),
    )


def adjoint_tables(tile, window):
    places = np.arange(tile) + MARGIN
    phase = angles(frequencies(), places, window)
    cos, sin = np.cos(phase), np.sin(phase)
    first = np.concatenate([cos, -sin], 1)
    second = np.concatenate([-sin, -cos], 1)
    cols = rows_at(
        2 * HALF, (0, first), (BAND, first), (HALF, second), (HALF + BAND, second)
    )
    rows = np.concatenate([cos.T, sin.T], 1) / window
    return stacked(cols, 2), three(rows)


def toward(at, core, size):
    onward = lax.rem(at + core, 2) == 0
    other = jnp.where(onward, at + 1, at - 1)
    return onward, (other >= 0) & (other < size)


def dot(left, right):
    return jnp.dot(left, right, preferred_element_type=F32)


def split(value, count):
    out, rest = [], value
    for step in range(count):
        part = rest.astype(BF)
        out.append(part)
        if step + 1 < count:
            rest = rest - part.astype(F32)
    return out


def lane_ids(shape):
    return lax.broadcasted_iota(jnp.int32, shape, len(shape) - 1)


def doubled(value):
    low_half = lane_ids(value.shape) < HALF
    high = value.astype(BF).astype(F32)
    rest = value - high
    mid = rest.astype(BF).astype(F32)
    first = jnp.where(low_half, high, rest).astype(BF)
    second = jnp.where(low_half, rest - mid, high).astype(BF)
    return jnp.concatenate([first, first, second], 1)


def doubled_weights(ref):
    size = ref.shape[0] // 3
    high, mid, low = ref[:size], ref[size : 2 * size], ref[2 * size :]
    return jnp.concatenate([high, high, mid, mid, high, low], 0)


def six_right(value):
    high, mid, low = split(value, 3)
    return jnp.concatenate([high, mid, low, high, mid, high], 0)


def three_right(value):
    high, low = split(value, 2)
    return jnp.concatenate([high, low, high], 0)


def fetch(sources, targets, sems):
    copies = [
        pltpu.make_async_copy(source, target, sems.at[at])
        for at, (source, target) in enumerate(zip(sources, targets))
    ]
    for copy in copies:
        copy.start()
    return copies


def local_kernel(
    mesh_shape, mask_hbm, col_hbm, row_hbm, own_ref, send_ref, mask_ref, col_ref, row_ref, sems
):
    tile = mask_ref.shape[0]
    for copy in fetch((mask_hbm, col_hbm, row_hbm), (mask_ref, col_ref, row_ref), sems):
        copy.wait()
    high, mid, low = split(mask_ref[...], 3)
    left = jnp.concatenate([high, mid, low, high, mid, high], 1)
    ch, cm, cl = col_ref[:tile], col_ref[tile : 2 * tile], col_ref[2 * tile :]
    right = jnp.concatenate([ch, ch, ch, cm, cm, cl], 0)
    partial = dot(left, right)
    both = dot(row_ref[...], six_right(partial))
    top, bottom = both[: 3 * BAND], both[3 * BAND :]
    lane = lane_ids(top.shape) % HALF
    width = top.shape[1]
    turned = jnp.where(
        lane < BAND,
        -pltpu.roll(bottom, width - BAND, 1),
        jnp.where(lane < 2 * BAND, pltpu.roll(bottom, BAND, 1), 0.0),
    )
    result = top + turned
    own = result[:BAND]
    below = result[BAND : 2 * BAND]
    above = result[2 * BAND :]
    down, valid = toward(lax.axis_index("row"), lax.axis_index("cond"), mesh_shape[0])
    chosen = jnp.where(down, below, above)
    chosen = jnp.where(valid, chosen, 0.0)
    own_ref[:BAND] = own[:, : 2 * HALF]
    own_ref[BAND:] = own[:, 2 * HALF :]
    send_ref[:BAND] = chosen[:, : 2 * HALF]
    send_ref[BAND:] = chosen[:, 2 * HALF :]


def fetch_kernel(cond_ref, dose_ref, kernels_hbm, *refs):
    sems = refs[-1]
    count = (len(refs) - 3) // 2
    chosen_ref, strength_ref = refs[count : count + 2]
    conds = cond_ref.shape[0]
    chosen = [kernels_hbm.at[cond_ref[c]] for c in range(conds)]
    copies = fetch(
        chosen + list(refs[:count]),
        [chosen_ref.at[c] for c in range(conds)] + list(refs[count + 2 : -1]),
        sems,
    )
    for c in range(conds):
        strength_ref[c] = jnp.full(strength_ref.shape[1:], dose_ref[cond_ref[c]], F32)
    for copy in copies:
        copy.wait()


def field_kernel(
    mesh_shape, strength_ref, own_ref, near_ref, far_ref, side_ref, other_ref,
    kernels_ref, target_ref, to_cols_ref, to_rows_ref, spread_cols_ref, spread_ref,
    gather_rows_ref, gather_cols_ref, from_rows_ref, from_cols_ref, out_ref, cols_ref, field_ref,
):
    conds = strength_ref.shape[0]
    count = 2 * BAND
    total = kernels_ref.shape[0] // BAND
    per = total // conds
    tile = target_ref.shape[0]

    col, core = lax.axis_index("col"), lax.axis_index("cond")

    def half(value, core):
        onward, valid = toward(col, core, mesh_shape[1])
        low_half = lane_ids(value.shape) < HALF
        kept = jnp.where(onward, jnp.where(low_half, 0.0, value), jnp.where(low_half, value, 0.0))
        kept = jnp.where(valid, kept, 0.0)
        return kept + pltpu.roll(kept, HALF, 1)

    spectrum = own_ref[BAND:] + near_ref[BAND:] + far_ref[BAND:]
    spectrum += half(side_ref[...], core) + half(other_ref[...], 1 - core)
    lane = lane_ids(spectrum.shape) % HALF
    onto_next = jnp.where(lane < BAND, spectrum, 0.0)
    onto_last = jnp.where(lane >= BAND, spectrum, 0.0)
    spectrum = jnp.where(
        lane_ids(spectrum.shape) < HALF,
        onto_next + pltpu.roll(onto_next, BAND, 1),
        onto_last + pltpu.roll(onto_last, 2 * HALF - BAND, 1),
    )

    kernels = kernels_ref[...].reshape(total, BAND, 2 * HALF)
    product = (kernels * spectrum[None]).reshape(total * BAND, 2 * HALF)
    high, mid, low = split(product, 3)
    size = 2 * HALF
    wh, wm, wl = to_cols_ref[:size], to_cols_ref[size : 2 * size], to_cols_ref[2 * size :]
    cols_ref[...] = dot(
        jnp.concatenate([high, mid, low, high, mid, high], 1),
        jnp.concatenate([wh, wh, wh, wm, wm, wl], 0),
    )

    sums = [jnp.zeros((count, 2 * HALF), F32) for _ in range(conds)]
    to_rows = to_rows_ref[...]
    for pair in range(total // 2):
        rights = []
        for k in (2 * pair, 2 * pair + 1):
            block = cols_ref[k * BAND : (k + 1) * BAND, :]
            block = jnp.concatenate([block[:, : 2 * HALF], block[:, 2 * HALF :]], 0)
            rights.append(six_right(block))
        both = dot(to_rows, jnp.concatenate(rights, 1))
        field_ref[pair] = both
        squares = both * both
        for part in range(2):
            c = (2 * pair + part) // per
            sums[c] = sums[c] + squares[:, part * 2 * HALF : (part + 1) * 2 * HALF]

    coarse = jnp.concatenate([value + pltpu.roll(value, HALF, 1) for value in sums], 0)
    wide = dot(doubled(coarse), doubled_weights(spread_cols_ref))
    right = jnp.concatenate(
        [six_right(wide[c * count : (c + 1) * count]) for c in range(conds)], 1
    )
    image = dot(spread_ref[...], right)

    goal = target_ref[...].astype(F32)
    norm = 1.0 / (per * BAND * BAND)
    slopes = []
    for c in range(conds):
        strength = strength_ref[c][:1]
        intensity = image[:, c * tile : (c + 1) * tile] * norm
        resist = jax.nn.sigmoid(STEEP * (strength * intensity - THRESH))
        slope = (resist - goal) * resist * (1.0 - resist)
        slopes.append(slope * (4.0 * STEEP * norm * strength))
    back = dot(gather_rows_ref[...], three_right(jnp.concatenate(slopes, 1)))
    high, low = split(
        jnp.concatenate([back[:, c * tile : (c + 1) * tile] for c in range(conds)], 0), 2
    )
    gh, gl = gather_cols_ref[:tile], gather_cols_ref[tile:]
    slope = dot(
        jnp.concatenate([high, low, high], 1), jnp.concatenate([gh, gh, gl], 0)
    )

    from_rows = from_rows_ref[...]
    for pair in range(total // 2):
        weight = [
            slope[((2 * pair + part) // per) * count : ((2 * pair + part) // per + 1) * count]
            for part in range(2)
        ]
        scaled = field_ref[pair] * jnp.concatenate(weight, 1)
        back = dot(from_rows, three_right(scaled))
        for part in range(2):
            block = back[:, part * 2 * HALF : (part + 1) * 2 * HALF]
            k = 2 * pair + part
            cols_ref[k * BAND : (k + 1) * BAND, :] = jnp.concatenate(
                [block[:BAND], block[BAND:]], 1
            )
    high, low = split(cols_ref[...], 2)
    weights = from_cols_ref[...]
    first = dot(high, weights)
    back = first[:, : 2 * HALF] + first[:, 2 * HALF :] + dot(low, weights[:, : 2 * HALF])
    back = back.reshape(total, BAND, 2 * HALF)
    out_ref[...] = jnp.sum(kernels_ref[...].reshape(total, BAND, 2 * HALF) * back, axis=0)


def adjoint_kernel(mine_ref, theirs_ref, cols_ref, rows_ref, out_ref):
    tile = out_ref.shape[1]
    high, low = split(mine_ref[...] + theirs_ref[...], 2)
    size = cols_ref.shape[0] // 2
    ch, cl = cols_ref[:size], cols_ref[size:]
    halves = dot(jnp.concatenate([high, low, high], 1), jnp.concatenate([ch, ch, cl], 0))
    joined = jnp.concatenate([halves[:, :tile], halves[:, tile:]], 0)
    out_ref[...] = dot(rows_ref[...], three_right(joined))


VMEM = pl.BlockSpec(memory_space=pltpu.VMEM)
SMEM = pl.BlockSpec(memory_space=pltpu.SMEM)
HBM = pl.BlockSpec(memory_space=pltpu.HBM)


def call(body, outs, specs, args, scratch=(), flops=1000000, grant=8):
    shapes = [
        shape if hasattr(shape, "dtype") else jax.ShapeDtypeStruct(shape, F32) for shape in outs
    ]
    one = len(outs) == 1
    args = [
        pltpu.with_memory_space_constraint(value, pltpu.HBM) if spec is HBM else value
        for spec, value in zip(specs, args)
    ]
    return pl.pallas_call(
        body,
        out_shape=shapes[0] if one else shapes,
        in_specs=specs,
        out_specs=VMEM if one else [VMEM] * len(outs),
        scratch_shapes=list(scratch),
        compiler_params=pltpu.CompilerParams(vmem_limit_bytes=grant * 2**20),
        cost_estimate=pl.CostEstimate(flops=flops, bytes_accessed=1000000, transcendentals=0),
    )(*args)


def partner(at, core, size):
    other = at ^ 1 if core == 0 else ((at + 1) ^ 1) - 1
    return other if 0 <= other < size else None


def swaps(mesh_shape, along):
    rows, cols, cores = mesh_shape
    out = []
    for r in range(rows):
        for c in range(cols):
            for k in range(cores):
                at, size = (r, rows) if along == 0 else (c, cols)
                other = partner(at, k, size)
                if other is not None:
                    to = (other, c, k) if along == 0 else (r, other, k)
                elif along == 0:
                    to = (r, c ^ 1, k)
                else:
                    to = (r ^ 1, c, k)
                if to[0] < rows and to[1] < cols:
                    out.append((((r * cols) + c) * cores + k, ((to[0] * cols) + to[1]) * cores + to[2]))
    return out


def shards(mesh_shape, mask, target, cond_index, kernels, dose):
    tile = mask.shape[0]
    window = tile + 2 * MARGIN
    col_table, row_table = local_tables(tile, window)
    block = (2 * BAND, 2 * HALF)
    own, send = call(
        functools.partial(local_kernel, mesh_shape), [block] * 2, [HBM] * 3,
        (mask, col_table, row_table),
        scratch=[
            pltpu.VMEM(mask.shape, F32),
            pltpu.VMEM(col_table.shape, BF),
            pltpu.VMEM(row_table.shape, BF),
            pltpu.SemaphoreType.DMA((3,)),
        ],
    )
    swap = [(0, 1), (1, 0)]
    near = lax.ppermute(send, AXES, swaps(mesh_shape, 0))

    conds = cond_index.shape[0]
    count = kernels.shape[2]
    later = (target,) + field_tables(tile, window) + adjoint_tables(tile, window)
    chosen, strength, *later = call(
        fetch_kernel,
        [(conds, count, 2, BAND * BAND), (conds, 8, tile)]
        + [jax.ShapeDtypeStruct(value.shape, value.dtype) for value in later],
        [SMEM] * 2 + [HBM] * (1 + len(later)),
        (cond_index, dose, jnp.transpose(kernels, (0, 2, 1, 3))) + later,
        scratch=[pltpu.SemaphoreType.DMA((conds + len(later),))],
    )
    near, chosen, strength, later = lax.optimization_barrier((near, chosen, strength, later))
    far = lax.ppermute(near, "cond", swap)
    real = chosen[:, :, 0].reshape(conds * count * BAND, BAND)
    imag = chosen[:, :, 1].reshape(conds * count * BAND, BAND)
    gap = jnp.zeros((real.shape[0], HALF - 2 * BAND), F32)
    arranged = jnp.concatenate([real, imag, gap] * 2, 1)
    far, arranged = lax.optimization_barrier((far, arranged))
    message = own[:BAND] + near[:BAND] + far[:BAND]
    side = lax.ppermute(message, AXES, swaps(mesh_shape, 1))
    other = lax.ppermute(side, "cond", swap)

    total = conds * count
    cotangent = call(
        functools.partial(field_kernel, mesh_shape),
        [(BAND, 2 * HALF)],
        [VMEM] * 16,
        (strength, own, near, far, side, other, arranged, *later[:-2]),
        scratch=[
            pltpu.VMEM((total * BAND, 4 * HALF), F32),
            pltpu.VMEM((total // 2, 2 * BAND, 4 * HALF), F32),
        ],
    )
    theirs = lax.ppermute(cotangent, "cond", swap)
    return call(
        adjoint_kernel, [(tile, tile)], [VMEM] * 4, (cotangent, theirs, *later[-2:])
    )


def solution(mesh):
    in_specs = (P("row", "col"), P("row", "col"), P("cond"), P(), P())
    out_specs = P("row", "col")
    shape = tuple(mesh.shape[name] for name in AXES)
    body = functools.partial(shards, shape)
    return jax.shard_map(body, mesh=mesh, in_specs=in_specs, out_specs=out_specs, check_vma=False)
```

```python
import functools
import math

import jax
import jax.numpy as jnp
import numpy as np
from jax import lax
from jax.experimental import pallas as pl
from jax.experimental.pallas import tpu as pltpu
from jax.sharding import PartitionSpec as P

MARGIN = 128
BAND = 24
STEEP = 4.0
THRESH = 0.6

HALF = 64
AXES = ("row", "col", "cond")
BF = jnp.bfloat16
F32 = jnp.float32


def pieces(table, count):
    out, rest = [], np.asarray(table, np.float32)
    for _ in range(count):
        part = rest.astype(BF)
        out.append(part)
        rest = rest - part.astype(np.float32)
    return out


def angles(left, right, period):
    left, right = np.asarray(left, np.int64), np.asarray(right, np.int64)
    return (left[:, None] * right[None, :] % period) * (2.0 * math.pi / period)


def frequencies():
    return np.arange(BAND) - BAND // 2


def lanes(*blocks):
    rows = blocks[0][1].shape[0]
    width = -(-max(at + block.shape[1] for at, block in blocks) // 128) * 128
    out = np.zeros((rows, width))
    for at, block in blocks:
        out[:, at : at + block.shape[1]] = block
    return out


def rows_at(height, *blocks):
    out = np.zeros((height, blocks[0][1].shape[1]))
    for at, block in blocks:
        out[at : at + block.shape[0]] = block
    return out


def six(table):
    high, mid, low = pieces(table, 3)
    return np.concatenate([high, high, high, mid, mid, low], 1)


def three(table):
    high, low = pieces(table, 2)
    return np.concatenate([high, high, low], 1)


def stacked(table, count):
    return np.concatenate(pieces(table, count), 0)


def local_tables(tile, window):
    places = np.arange(tile)
    cols = []
    for at, shift in ((0, 0), (HALF, 2 * MARGIN), (2 * HALF, MARGIN), (3 * HALF, MARGIN)):
        phase = angles(places + shift, frequencies(), window)
        cols += [(at, np.cos(phase)), (at + BAND, -np.sin(phase))]
    col_table = lanes(*cols) / window
    row_table = []
    for shift in (MARGIN, 0, 2 * MARGIN):
        phase = angles(frequencies(), places + shift, window)
        row_table += [np.cos(phase), -np.sin(phase)]
    return stacked(col_table, 2), three(np.concatenate(row_table, 0))


def field_tables(tile, window):
    count = 2 * BAND
    points = np.arange(count)
    phase = angles(frequencies(), points, count)
    cos, sin = np.cos(phase), np.sin(phase)
    real_rows = lanes((0, cos), (HALF, sin), (2 * HALF, -sin), (3 * HALF, cos))
    imag_rows = lanes((0, -sin), (HALF, cos), (2 * HALF, -cos), (3 * HALF, -sin))
    to_cols = rows_at(
        2 * HALF,
        (0, real_rows),
        (BAND, imag_rows),
        (HALF, imag_rows),
        (HALF + BAND, -real_rows),
    )
    to_rows = np.concatenate([cos.T, sin.T], 1)
    where = (np.arange(tile)[:, None] + MARGIN) / window - points[None, :] / count
    spread = np.ones((tile, count))
    for order in range(1, BAND):
        spread += 2.0 * np.cos(2.0 * math.pi * order * where)
    spread /= count
    spread_cols = rows_at(HALF, (0, spread.T))
    gather_cols = lanes((0, spread), (HALF, spread))
    from_rows = np.concatenate([cos, sin], 0)
    pad = np.zeros((HALF - count, BAND))
    c, s = cos.T, sin.T

    def both(real_part, imag_part):
        return lanes((0, real_part), (BAND, imag_part), (HALF, imag_part), (HALF + BAND, -real_part))

    blocks = [both(c, -s), both(s, c), both(-s, -c), both(c, -s)]
    empty = np.zeros((HALF - count, 2 * HALF))
    from_cols = np.concatenate([part for block in blocks for part in (block, empty)], 0)
    return (
        stacked(to_cols, 3),
        six(to_rows),
        stacked(spread_cols, 3),
        six(spread),
        three(spread.T),
        stacked(gather_cols, 2),
        three(from_rows),
        np.concatenate(pieces(from_cols, 2), 1),
    )


def adjoint_tables(tile, window):
    places = np.arange(tile) + MARGIN
    phase = angles(frequencies(), places, window)
    cos, sin = np.cos(phase), np.sin(phase)
    first = np.concatenate([cos, -sin], 1)
    second = np.concatenate([-sin, -cos], 1)
    cols = rows_at(
        2 * HALF, (0, first), (BAND, first), (HALF, second), (HALF + BAND, second)
    )
    rows = np.concatenate([cos.T, sin.T], 1) / window
    return stacked(cols, 2), three(rows)


def toward(at, core, size):
    onward = lax.rem(at + core, 2) == 0
    other = jnp.where(onward, at + 1, at - 1)
    return onward, (other >= 0) & (other < size)


def dot(left, right):
    return jnp.dot(left, right, preferred_element_type=F32)


def split(value, count):
    out, rest = [], value
    for step in range(count):
        part = rest.astype(BF)
        out.append(part)
        if step + 1 < count:
            rest = rest - part.astype(F32)
    return out


def lane_ids(shape):
    return lax.broadcasted_iota(jnp.int32, shape, len(shape) - 1)


def doubled(value):
    low_half = lane_ids(value.shape) < HALF
    high = value.astype(BF).astype(F32)
    rest = value - high
    mid = rest.astype(BF).astype(F32)
    first = jnp.where(low_half, high, rest).astype(BF)
    second = jnp.where(low_half, rest - mid, high).astype(BF)
    return jnp.concatenate([first, first, second], 1)


def doubled_weights(ref):
    size = ref.shape[0] // 3
    high, mid, low = ref[:size], ref[size : 2 * size], ref[2 * size :]
    return jnp.concatenate([high, high, mid, mid, high, low], 0)


def six_right(value):
    high, mid, low = split(value, 3)
    return jnp.concatenate([high, mid, low, high, mid, high], 0)


def three_right(value):
    high, low = split(value, 2)
    return jnp.concatenate([high, low, high], 0)


def fetch(sources, targets, sems):
    copies = [
        pltpu.make_async_copy(source, target, sems.at[at])
        for at, (source, target) in enumerate(zip(sources, targets))
    ]
    for copy in copies:
        copy.start()
    return copies


def local_spectrum(tile_value, col_ref, row_table):
    size = col_ref.shape[0] // 2
    high, low = split(tile_value, 2)
    ch, cl = col_ref[:size], col_ref[size:]
    partial = dot(jnp.concatenate([high, low, high], 1), jnp.concatenate([ch, ch, cl], 0))
    both = dot(row_table, three_right(partial))
    top, bottom = both[:BAND], both[BAND:]
    lane = lane_ids(top.shape) % HALF
    turned = jnp.where(
        lane < BAND,
        -pltpu.roll(bottom, top.shape[1] - BAND, 1),
        jnp.where(lane < 2 * BAND, pltpu.roll(bottom, BAND, 1), 0.0),
    )
    result = top + turned
    return jnp.concatenate([result[:, : 2 * HALF], result[:, 2 * HALF :]], 0)


def open_kernel(*refs):
    cond_hbm, dose_hbm, mask_hbm, kernels_hbm = refs[:4]
    cond_ref, dose_ref, mask_ref, sems = refs[-4:]
    count = (len(refs) - 11) // 2
    sources, targets = refs[4 : 4 + count], refs[7 + count : 7 + 2 * count]
    own_ref, chosen_ref, strength_ref = refs[4 + count : 7 + count]
    conds = cond_hbm.shape[0]
    copies = []

    def start(source, target):
        copy = pltpu.make_async_copy(source, target, sems.at[len(copies)])
        copy.start()
        copies.append(copy)
        return copy

    scalars = [start(cond_hbm, cond_ref), start(dose_hbm, dose_ref)]
    first = [start(mask_hbm, mask_ref)]
    first += [start(source, target) for source, target in zip(sources[:2], targets[:2])]
    for copy in scalars:
        copy.wait()
    rest = [start(kernels_hbm.at[cond_ref[c]], chosen_ref.at[c]) for c in range(conds)]
    rest += [start(source, target) for source, target in zip(sources[2:], targets[2:])]
    for c in range(conds):
        strength_ref[c] = jnp.full(strength_ref.shape[1:], dose_ref[cond_ref[c]], F32)
    for copy in first:
        copy.wait()
    col_ref, row_ref = targets[:2]
    own_ref[...] = local_spectrum(mask_ref[...], col_ref, row_ref[: 2 * BAND])
    for copy in rest:
        copy.wait()


def near_kernel(mesh_shape, tile_ref, col_ref, row_ref, out_ref):
    down, valid = toward(lax.axis_index("row"), lax.axis_index("cond"), mesh_shape[0])
    at = pl.multiple_of(jnp.where(down, 4 * BAND, 2 * BAND), 2 * BAND)
    share = local_spectrum(tile_ref[...], col_ref, row_ref[pl.ds(at, 2 * BAND)])
    out_ref[...] = jnp.where(valid, share, 0.0)


def field_kernel(
    mesh_shape, strength_ref, own_ref, near_ref, far_ref, side_ref, other_ref,
    kernels_ref, target_ref, to_cols_ref, to_rows_ref, spread_cols_ref, spread_ref,
    gather_rows_ref, gather_cols_ref, from_rows_ref, from_cols_ref, out_ref, cols_ref, field_ref,
):
    conds = strength_ref.shape[0]
    count = 2 * BAND
    total = kernels_ref.shape[0] // BAND
    per = total // conds
    tile = target_ref.shape[0]

    col, core = lax.axis_index("col"), lax.axis_index("cond")

    def half(value, core):
        onward, valid = toward(col, core, mesh_shape[1])
        low_half = lane_ids(value.shape) < HALF
        kept = jnp.where(onward, jnp.where(low_half, 0.0, value), jnp.where(low_half, value, 0.0))
        kept = jnp.where(valid, kept, 0.0)
        return kept + pltpu.roll(kept, HALF, 1)

    spectrum = own_ref[BAND:] + near_ref[BAND:] + far_ref[BAND:]
    spectrum += half(side_ref[...], core) + half(other_ref[...], 1 - core)
    lane = lane_ids(spectrum.shape) % HALF
    onto_next = jnp.where(lane < BAND, spectrum, 0.0)
    onto_last = jnp.where(lane >= BAND, spectrum, 0.0)
    spectrum = jnp.where(
        lane_ids(spectrum.shape) < HALF,
        onto_next + pltpu.roll(onto_next, BAND, 1),
        onto_last + pltpu.roll(onto_last, 2 * HALF - BAND, 1),
    )

    kernels = kernels_ref[...].reshape(total, BAND, 2 * HALF)
    product = (kernels * spectrum[None]).reshape(total * BAND, 2 * HALF)
    high, mid, low = split(product, 3)
    size = 2 * HALF
    wh, wm, wl = to_cols_ref[:size], to_cols_ref[size : 2 * size], to_cols_ref[2 * size :]
    cols_ref[...] = dot(
        jnp.concatenate([high, mid, low, high, mid, high], 1),
        jnp.concatenate([wh, wh, wh, wm, wm, wl], 0),
    )

    sums = [jnp.zeros((count, 2 * HALF), F32) for _ in range(conds)]
    to_rows = to_rows_ref[...]
    for pair in range(total // 2):
        rights = []
        for k in (2 * pair, 2 * pair + 1):
            block = cols_ref[k * BAND : (k + 1) * BAND, :]
            block = jnp.concatenate([block[:, : 2 * HALF], block[:, 2 * HALF :]], 0)
            rights.append(six_right(block))
        both = dot(to_rows, jnp.concatenate(rights, 1))
        field_ref[pair] = both
        squares = both * both
        for part in range(2):
            c = (2 * pair + part) // per
            sums[c] = sums[c] + squares[:, part * 2 * HALF : (part + 1) * 2 * HALF]

    coarse = jnp.concatenate([value + pltpu.roll(value, HALF, 1) for value in sums], 0)
    wide = dot(doubled(coarse), doubled_weights(spread_cols_ref))
    right = jnp.concatenate(
        [six_right(wide[c * count : (c + 1) * count]) for c in range(conds)], 1
    )
    image = dot(spread_ref[...], right)

    goal = target_ref[...].astype(F32)
    norm = 1.0 / (per * BAND * BAND)
    slopes = []
    for c in range(conds):
        strength = strength_ref[c][:1]
        intensity = image[:, c * tile : (c + 1) * tile] * norm
        resist = jax.nn.sigmoid(STEEP * (strength * intensity - THRESH))
        slope = (resist - goal) * resist * (1.0 - resist)
        slopes.append(slope * (4.0 * STEEP * norm * strength))
    back = dot(gather_rows_ref[...], three_right(jnp.concatenate(slopes, 1)))
    high, low = split(
        jnp.concatenate([back[:, c * tile : (c + 1) * tile] for c in range(conds)], 0), 2
    )
    gh, gl = gather_cols_ref[:tile], gather_cols_ref[tile:]
    slope = dot(
        jnp.concatenate([high, low, high], 1), jnp.concatenate([gh, gh, gl], 0)
    )

    from_rows = from_rows_ref[...]
    for pair in range(total // 2):
        weight = [
            slope[((2 * pair + part) // per) * count : ((2 * pair + part) // per + 1) * count]
            for part in range(2)
        ]
        scaled = field_ref[pair] * jnp.concatenate(weight, 1)
        back = dot(from_rows, three_right(scaled))
        for part in range(2):
            block = back[:, part * 2 * HALF : (part + 1) * 2 * HALF]
            k = 2 * pair + part
            cols_ref[k * BAND : (k + 1) * BAND, :] = jnp.concatenate(
                [block[:BAND], block[BAND:]], 1
            )
    high, low = split(cols_ref[...], 2)
    weights = from_cols_ref[...]
    first = dot(high, weights)
    back = first[:, : 2 * HALF] + first[:, 2 * HALF :] + dot(low, weights[:, : 2 * HALF])
    back = back.reshape(total, BAND, 2 * HALF)
    out_ref[...] = jnp.sum(kernels_ref[...].reshape(total, BAND, 2 * HALF) * back, axis=0)


def adjoint_kernel(mine_ref, theirs_ref, cols_ref, rows_ref, out_ref):
    tile = out_ref.shape[1]
    high, low = split(mine_ref[...] + theirs_ref[...], 2)
    size = cols_ref.shape[0] // 2
    ch, cl = cols_ref[:size], cols_ref[size:]
    halves = dot(jnp.concatenate([high, low, high], 1), jnp.concatenate([ch, ch, cl], 0))
    joined = jnp.concatenate([halves[:, :tile], halves[:, tile:]], 0)
    out_ref[...] = dot(rows_ref[...], three_right(joined))


VMEM = pl.BlockSpec(memory_space=pltpu.VMEM)
SMEM = pl.BlockSpec(memory_space=pltpu.SMEM)
HBM = pl.BlockSpec(memory_space=pltpu.HBM)


def call(body, outs, specs, args, scratch=(), flops=1000000, grant=8):
    shapes = [
        shape if hasattr(shape, "dtype") else jax.ShapeDtypeStruct(shape, F32) for shape in outs
    ]
    one = len(outs) == 1
    args = [
        pltpu.with_memory_space_constraint(value, pltpu.HBM) if spec is HBM else value
        for spec, value in zip(specs, args)
    ]
    return pl.pallas_call(
        body,
        out_shape=shapes[0] if one else shapes,
        in_specs=specs,
        out_specs=VMEM if one else [VMEM] * len(outs),
        scratch_shapes=list(scratch),
        compiler_params=pltpu.CompilerParams(vmem_limit_bytes=grant * 2**20),
        cost_estimate=pl.CostEstimate(flops=flops, bytes_accessed=1000000, transcendentals=0),
    )(*args)


def partner(at, core, size):
    other = at ^ 1 if core == 0 else ((at + 1) ^ 1) - 1
    return other if 0 <= other < size else None


def swaps(mesh_shape, along):
    rows, cols, cores = mesh_shape
    out = []
    for r in range(rows):
        for c in range(cols):
            for k in range(cores):
                at, size = (r, rows) if along == 0 else (c, cols)
                other = partner(at, k, size)
                if other is not None:
                    to = (other, c, k) if along == 0 else (r, other, k)
                elif along == 0:
                    to = (r, c ^ 1, k)
                else:
                    to = (r ^ 1, c, k)
                if to[0] < rows and to[1] < cols:
                    out.append((((r * cols) + c) * cores + k, ((to[0] * cols) + to[1]) * cores + to[2]))
    return out


def shards(mesh_shape, mask, target, cond_index, kernels, dose):
    tile = mask.shape[0]
    window = tile + 2 * MARGIN
    swap = [(0, 1), (1, 0)]
    conds = cond_index.shape[0]
    count = kernels.shape[2]
    block = (2 * BAND, 2 * HALF)
    beside = lax.ppermute(mask, AXES, swaps(mesh_shape, 0))
    fetched = local_tables(tile, window) + (target,)
    fetched += field_tables(tile, window) + adjoint_tables(tile, window)
    own, chosen, strength, *fetched = call(
        open_kernel,
        [block, (conds, count, 2, BAND * BAND), (conds, 8, tile)]
        + [jax.ShapeDtypeStruct(value.shape, value.dtype) for value in fetched],
        [HBM] * (4 + len(fetched)),
        (cond_index, dose, mask, jnp.transpose(kernels, (0, 2, 1, 3))) + fetched,
        scratch=[
            pltpu.SMEM(cond_index.shape, jnp.int32),
            pltpu.SMEM(dose.shape, F32),
            pltpu.VMEM(mask.shape, F32),
            pltpu.SemaphoreType.DMA((3 + conds + len(fetched),)),
        ],
    )
    beside, own, chosen, strength, fetched = lax.optimization_barrier(
        (beside, own, chosen, strength, fetched)
    )
    col_table, row_table, *later = fetched
    near = call(
        functools.partial(near_kernel, mesh_shape), [block], [VMEM] * 3,
        (beside, col_table, row_table),
    )
    far = lax.ppermute(near, "cond", swap)
    real = chosen[:, :, 0].reshape(conds * count * BAND, BAND)
    imag = chosen[:, :, 1].reshape(conds * count * BAND, BAND)
    gap = jnp.zeros((real.shape[0], HALF - 2 * BAND), F32)
    arranged = jnp.concatenate([real, imag, gap] * 2, 1)
    far, arranged = lax.optimization_barrier((far, arranged))
    message = own[:BAND] + near[:BAND] + far[:BAND]
    side = lax.ppermute(message, AXES, swaps(mesh_shape, 1))
    other = lax.ppermute(side, "cond", swap)

    total = conds * count
    cotangent = call(
        functools.partial(field_kernel, mesh_shape),
        [(BAND, 2 * HALF)],
        [VMEM] * 16,
        (strength, own, near, far, side, other, arranged, *later[:-2]),
        scratch=[
            pltpu.VMEM((total * BAND, 4 * HALF), F32),
            pltpu.VMEM((total // 2, 2 * BAND, 4 * HALF), F32),
        ],
    )
    theirs = lax.ppermute(cotangent, "cond", swap)
    return call(
        adjoint_kernel, [(tile, tile)], [VMEM] * 4, (cotangent, theirs, *later[-2:])
    )


def solution(mesh):
    in_specs = (P("row", "col"), P("row", "col"), P("cond"), P(), P())
    out_specs = P("row", "col")
    shape = tuple(mesh.shape[name] for name in AXES)
    body = functools.partial(shards, shape)
    return jax.shard_map(body, mesh=mesh, in_specs=in_specs, out_specs=out_specs, check_vma=False)
```

```python
import functools
import math

import jax
import jax.numpy as jnp
import numpy as np
from jax import lax
from jax.experimental import pallas as pl
from jax.experimental.pallas import tpu as pltpu
from jax.sharding import PartitionSpec as P

MARGIN = 128
BAND = 24
STEEP = 4.0
THRESH = 0.6

HALF = 64
AXES = ("row", "col", "cond")
BF = jnp.bfloat16
F32 = jnp.float32


def pieces(table, count):
    out, rest = [], np.asarray(table, np.float32)
    for _ in range(count):
        part = rest.astype(BF)
        out.append(part)
        rest = rest - part.astype(np.float32)
    return out


def angles(left, right, period):
    left, right = np.asarray(left, np.int64), np.asarray(right, np.int64)
    return (left[:, None] * right[None, :] % period) * (2.0 * math.pi / period)


def frequencies():
    return np.arange(BAND) - BAND // 2


def lanes(*blocks):
    rows = blocks[0][1].shape[0]
    width = -(-max(at + block.shape[1] for at, block in blocks) // 128) * 128
    out = np.zeros((rows, width))
    for at, block in blocks:
        out[:, at : at + block.shape[1]] = block
    return out


def rows_at(height, *blocks):
    out = np.zeros((height, blocks[0][1].shape[1]))
    for at, block in blocks:
        out[at : at + block.shape[0]] = block
    return out


def six(table):
    high, mid, low = pieces(table, 3)
    return np.concatenate([high, high, high, mid, mid, low], 1)


def three(table):
    high, low = pieces(table, 2)
    return np.concatenate([high, high, low], 1)


def stacked(table, count):
    return np.concatenate(pieces(table, count), 0)


def local_tables(tile, window):
    places = np.arange(tile)
    cols = []
    for at, shift in ((0, 0), (HALF, 2 * MARGIN), (2 * HALF, MARGIN), (3 * HALF, MARGIN)):
        phase = angles(places + shift, frequencies(), window)
        cols += [(at, np.cos(phase)), (at + BAND, -np.sin(phase))]
    col_table = lanes(*cols) / window
    row_table = []
    for shift in (MARGIN, 0, 2 * MARGIN):
        phase = angles(frequencies(), places + shift, window)
        row_table += [np.cos(phase), -np.sin(phase)]
    return stacked(col_table, 2), three(np.concatenate(row_table, 0))


def field_tables(tile, window):
    count = 2 * BAND
    points = np.arange(count)
    phase = angles(frequencies(), points, count)
    cos, sin = np.cos(phase), np.sin(phase)
    one = np.concatenate(
        [lanes((0, cos), (HALF, sin)), lanes((0, -sin), (HALF, cos)), np.zeros((HALF - count, 2 * HALF))]
    )
    none = np.zeros_like(one)
    to_cols = np.concatenate(
        [np.concatenate([one, none], 1), np.concatenate([none, one], 1)], 0
    )
    to_rows = np.concatenate([cos.T, -sin.T], 1)
    where = (np.arange(tile)[:, None] + MARGIN) / window - points[None, :] / count
    spread = np.ones((tile, count))
    for order in range(1, BAND):
        spread += 2.0 * np.cos(2.0 * math.pi * order * where)
    spread /= count
    spread_cols = rows_at(HALF, (0, spread.T))
    gather_cols = lanes((0, spread), (HALF, spread))
    from_rows = np.concatenate([cos, sin], 0)
    return (
        stacked(to_cols, 3),
        six(to_rows),
        stacked(spread_cols, 3),
        six(spread),
        three(spread.T),
        stacked(gather_cols, 2),
        three(from_rows),
        np.concatenate(pieces(to_cols.T, 2), 1),
    )


def adjoint_tables(tile, window):
    places = np.arange(tile) + MARGIN
    phase = angles(frequencies(), places, window)
    cos, sin = np.cos(phase), np.sin(phase)
    first = np.concatenate([cos, -sin], 1)
    second = np.concatenate([-sin, -cos], 1)
    cols = rows_at(
        2 * HALF, (0, first), (BAND, first), (HALF, second), (HALF + BAND, second)
    )
    rows = np.concatenate([cos.T, sin.T], 1) / window
    return stacked(cols, 2), three(rows)


def toward(at, core, size):
    onward = lax.rem(at + core, 2) == 0
    other = jnp.where(onward, at + 1, at - 1)
    return onward, (other >= 0) & (other < size)


def dot(left, right):
    return jnp.dot(left, right, preferred_element_type=F32)


def split(value, count):
    out, rest = [], value
    for step in range(count):
        part = rest.astype(BF)
        out.append(part)
        if step + 1 < count:
            rest = rest - part.astype(F32)
    return out


def lane_ids(shape):
    return lax.broadcasted_iota(jnp.int32, shape, len(shape) - 1)


def doubled(value):
    low_half = lane_ids(value.shape) < HALF
    high = value.astype(BF).astype(F32)
    rest = value - high
    mid = rest.astype(BF).astype(F32)
    first = jnp.where(low_half, high, rest).astype(BF)
    second = jnp.where(low_half, rest - mid, high).astype(BF)
    return jnp.concatenate([first, first, second], 1)


def doubled_weights(ref):
    size = ref.shape[0] // 3
    high, mid, low = ref[:size], ref[size : 2 * size], ref[2 * size :]
    return jnp.concatenate([high, high, mid, mid, high, low], 0)


def six_right(value):
    high, mid, low = split(value, 3)
    return jnp.concatenate([high, mid, low, high, mid, high], 0)


def three_right(value):
    high, low = split(value, 2)
    return jnp.concatenate([high, low, high], 0)


def fetch(sources, targets, sems):
    copies = [
        pltpu.make_async_copy(source, target, sems.at[at])
        for at, (source, target) in enumerate(zip(sources, targets))
    ]
    for copy in copies:
        copy.start()
    return copies


def local_spectrum(tile_value, col_ref, row_table):
    size = col_ref.shape[0] // 2
    high, low = split(tile_value, 2)
    ch, cl = col_ref[:size], col_ref[size:]
    partial = dot(jnp.concatenate([high, low, high], 1), jnp.concatenate([ch, ch, cl], 0))
    both = dot(row_table, three_right(partial))
    top, bottom = both[:BAND], both[BAND:]
    lane = lane_ids(top.shape) % HALF
    turned = jnp.where(
        lane < BAND,
        -pltpu.roll(bottom, top.shape[1] - BAND, 1),
        jnp.where(lane < 2 * BAND, pltpu.roll(bottom, BAND, 1), 0.0),
    )
    result = top + turned
    return jnp.concatenate([result[:, : 2 * HALF], result[:, 2 * HALF :]], 0)


def open_kernel(*refs):
    cond_hbm, dose_hbm, mask_hbm, kernels_hbm = refs[:4]
    cond_ref, dose_ref, mask_ref, sems = refs[-4:]
    count = (len(refs) - 11) // 2
    sources, targets = refs[4 : 4 + count], refs[7 + count : 7 + 2 * count]
    own_ref, chosen_ref, strength_ref = refs[4 + count : 7 + count]
    conds = cond_hbm.shape[0]
    copies = []

    def start(source, target):
        copy = pltpu.make_async_copy(source, target, sems.at[len(copies)])
        copy.start()
        copies.append(copy)
        return copy

    scalars = [start(cond_hbm, cond_ref), start(dose_hbm, dose_ref)]
    first = [start(mask_hbm, mask_ref)]
    first += [start(source, target) for source, target in zip(sources[:2], targets[:2])]
    for copy in scalars:
        copy.wait()
    rest = [start(kernels_hbm.at[cond_ref[c]], chosen_ref.at[c]) for c in range(conds)]
    rest += [start(source, target) for source, target in zip(sources[2:], targets[2:])]
    for c in range(conds):
        strength_ref[c] = jnp.full(strength_ref.shape[1:], dose_ref[cond_ref[c]], F32)
    for copy in first:
        copy.wait()
    col_ref, row_ref = targets[:2]
    own_ref[...] = local_spectrum(mask_ref[...], col_ref, row_ref[: 2 * BAND])
    for copy in rest:
        copy.wait()


def near_kernel(mesh_shape, tile_ref, col_ref, row_ref, out_ref):
    down, valid = toward(lax.axis_index("row"), lax.axis_index("cond"), mesh_shape[0])
    at = pl.multiple_of(jnp.where(down, 4 * BAND, 2 * BAND), 2 * BAND)
    share = local_spectrum(tile_ref[...], col_ref, row_ref[pl.ds(at, 2 * BAND)])
    out_ref[...] = jnp.where(valid, share, 0.0)


def arrange_kernel(real_ref, imag_ref, first_ref, second_ref):
    total = real_ref.shape[0] // BAND
    for pair in range(total // 2):
        first, second = 0.0, 0.0
        for part in range(2):
            at = (2 * pair + part) * BAND
            pad = jnp.zeros((BAND, 2 * HALF - BAND), F32)
            real = jnp.concatenate([real_ref[at : at + BAND, :], pad], 1)
            imag = jnp.concatenate([imag_ref[at : at + BAND, :], pad], 1)

            def moved(value, by):
                return pltpu.roll(value, part * HALF + by, 1) if part * HALF + by else value

            first = first + (moved(real, 0) + moved(imag, BAND))
            second = second + (moved(real, BAND) - moved(imag, 0))
        first_ref[:, pair * 2 * HALF : (pair + 1) * 2 * HALF] = first
        second_ref[:, pair * 2 * HALF : (pair + 1) * 2 * HALF] = second


def field_kernel(
    mesh_shape, strength_ref, own_ref, near_ref, far_ref, side_ref, other_ref,
    first_ref, second_ref, target_ref, to_cols_ref, to_rows_ref, spread_cols_ref, spread_ref,
    gather_rows_ref, gather_cols_ref, from_rows_ref, from_cols_ref, out_ref, rows_ref, field_ref,
):
    conds = strength_ref.shape[0]
    count = 2 * BAND
    pairs = first_ref.shape[1] // (2 * HALF)
    per = 2 * pairs // conds
    tile = target_ref.shape[0]
    wide = 4 * HALF
    col, core = lax.axis_index("col"), lax.axis_index("cond")

    def half(value, core):
        onward, valid = toward(col, core, mesh_shape[1])
        low_half = lane_ids(value.shape) < HALF
        kept = jnp.where(onward, jnp.where(low_half, 0.0, value), jnp.where(low_half, value, 0.0))
        kept = jnp.where(valid, kept, 0.0)
        return kept + pltpu.roll(kept, HALF, 1)

    spectrum = own_ref[BAND:] + near_ref[BAND:] + far_ref[BAND:]
    spectrum += half(side_ref[...], core) + half(other_ref[...], 1 - core)
    lane = lane_ids(spectrum.shape) % HALF
    real = jnp.where(lane < BAND, spectrum, 0.0)
    imag = jnp.where(lane >= BAND, spectrum, 0.0)
    real = real + pltpu.roll(real, BAND, 1)
    imag = imag + pltpu.roll(imag, 2 * HALF - BAND, 1)

    to_rows = to_rows_ref[...]
    for quad in range(pairs // 2):
        blocks = []
        for pair in (2 * quad, 2 * quad + 1):
            one = first_ref[:, pair * 2 * HALF : (pair + 1) * 2 * HALF]
            two = second_ref[:, pair * 2 * HALF : (pair + 1) * 2 * HALF]
            blocks.append(jnp.concatenate([one * real + two * imag, one * imag - two * real], 0))
        both = dot(to_rows, six_right(jnp.concatenate(blocks, 1)))
        for part in range(2):
            at = (2 * quad + part) * count
            rows_ref[at : at + count, :] = both[:, part * 2 * HALF : (part + 1) * 2 * HALF]

    high, mid, low = split(rows_ref[...], 3)
    size = 2 * HALF
    wh, wm, wl = to_cols_ref[:size], to_cols_ref[size : 2 * size], to_cols_ref[2 * size :]
    field_ref[...] = dot(
        jnp.concatenate([high, mid, low, high, mid, high], 1),
        jnp.concatenate([wh, wh, wh, wm, wm, wl], 0),
    )
    sums = [jnp.zeros((count, 2 * HALF), F32) for _ in range(conds)]
    for pair in range(pairs):
        both = field_ref[pair * count : (pair + 1) * count, :]
        squares = both * both
        for part in range(2):
            c = (2 * pair + part) // per
            sums[c] = sums[c] + squares[:, part * 2 * HALF : (part + 1) * 2 * HALF]

    coarse = jnp.concatenate([value + pltpu.roll(value, HALF, 1) for value in sums], 0)
    lines = dot(doubled(coarse), doubled_weights(spread_cols_ref))
    right = jnp.concatenate(
        [six_right(lines[c * count : (c + 1) * count]) for c in range(conds)], 1
    )
    image = dot(spread_ref[...], right)

    goal = target_ref[...].astype(F32)
    norm = 1.0 / (per * BAND * BAND)
    slopes = []
    for c in range(conds):
        strength = strength_ref[c][:1]
        intensity = image[:, c * tile : (c + 1) * tile] * norm
        resist = jax.nn.sigmoid(STEEP * (strength * intensity - THRESH))
        slope = (resist - goal) * resist * (1.0 - resist)
        slopes.append(slope * (4.0 * STEEP * norm * strength))
    back = dot(gather_rows_ref[...], three_right(jnp.concatenate(slopes, 1)))
    high, low = split(
        jnp.concatenate([back[:, c * tile : (c + 1) * tile] for c in range(conds)], 0), 2
    )
    gh, gl = gather_cols_ref[:tile], gather_cols_ref[tile:]
    slope = dot(jnp.concatenate([high, low, high], 1), jnp.concatenate([gh, gh, gl], 0))

    for pair in range(pairs):
        weight = []
        for k in (2 * pair, 2 * pair + 1):
            weight.append(slope[k // per * count : (k // per + 1) * count])
        at = pair * count
        field_ref[at : at + count, :] = field_ref[at : at + count, :] * jnp.concatenate(weight, 1)
    high, low = split(field_ref[...], 2)
    weights = from_cols_ref[...]
    back = dot(high, weights)
    rows_ref[...] = back[:, : 2 * HALF] + back[:, 2 * HALF :] + dot(low, weights[:, : 2 * HALF])

    from_rows = from_rows_ref[...]
    sum_one, sum_two = 0.0, 0.0
    for quad in range(pairs // 2):
        at = 2 * quad * count
        value = jnp.concatenate(
            [rows_ref[at : at + count, :], rows_ref[at + count : at + 2 * count, :]], 1
        )
        back = dot(from_rows, three_right(value))
        top, bottom = back[:BAND], back[BAND:]
        one = first_ref[:, quad * wide : (quad + 1) * wide]
        two = second_ref[:, quad * wide : (quad + 1) * wide]
        sum_one = sum_one + (one * top + two * bottom)
        sum_two = sum_two + (two * top - one * bottom)
    sum_one = sum_one[:, : 2 * HALF] + sum_one[:, 2 * HALF :]
    sum_two = sum_two[:, : 2 * HALF] + sum_two[:, 2 * HALF :]
    out_ref[...] = jnp.where(
        lane_ids(sum_one.shape) < HALF,
        sum_one + pltpu.roll(sum_one, HALF, 1),
        sum_two + pltpu.roll(sum_two, HALF, 1),
    )


def adjoint_kernel(mine_ref, theirs_ref, cols_ref, rows_ref, out_ref):
    tile = out_ref.shape[1]
    high, low = split(mine_ref[...] + theirs_ref[...], 2)
    size = cols_ref.shape[0] // 2
    ch, cl = cols_ref[:size], cols_ref[size:]
    halves = dot(jnp.concatenate([high, low, high], 1), jnp.concatenate([ch, ch, cl], 0))
    joined = jnp.concatenate([halves[:, :tile], halves[:, tile:]], 0)
    out_ref[...] = dot(rows_ref[...], three_right(joined))


VMEM = pl.BlockSpec(memory_space=pltpu.VMEM)
SMEM = pl.BlockSpec(memory_space=pltpu.SMEM)
HBM = pl.BlockSpec(memory_space=pltpu.HBM)


def call(body, outs, specs, args, scratch=(), flops=1000000, grant=8):
    shapes = [
        shape if hasattr(shape, "dtype") else jax.ShapeDtypeStruct(shape, F32) for shape in outs
    ]
    one = len(outs) == 1
    args = [
        pltpu.with_memory_space_constraint(value, pltpu.HBM) if spec is HBM else value
        for spec, value in zip(specs, args)
    ]
    return pl.pallas_call(
        body,
        out_shape=shapes[0] if one else shapes,
        in_specs=specs,
        out_specs=VMEM if one else [VMEM] * len(outs),
        scratch_shapes=list(scratch),
        compiler_params=pltpu.CompilerParams(vmem_limit_bytes=grant * 2**20),
        cost_estimate=pl.CostEstimate(flops=flops, bytes_accessed=1000000, transcendentals=0),
    )(*args)


def partner(at, core, size):
    other = at ^ 1 if core == 0 else ((at + 1) ^ 1) - 1
    return other if 0 <= other < size else None


def swaps(mesh_shape, along):
    rows, cols, cores = mesh_shape
    out = []
    for r in range(rows):
        for c in range(cols):
            for k in range(cores):
                at, size = (r, rows) if along == 0 else (c, cols)
                other = partner(at, k, size)
                if other is not None:
                    to = (other, c, k) if along == 0 else (r, other, k)
                elif along == 0:
                    to = (r, c ^ 1, k)
                else:
                    to = (r ^ 1, c, k)
                if to[0] < rows and to[1] < cols:
                    out.append((((r * cols) + c) * cores + k, ((to[0] * cols) + to[1]) * cores + to[2]))
    return out


def shards(mesh_shape, mask, target, cond_index, kernels, dose):
    tile = mask.shape[0]
    window = tile + 2 * MARGIN
    swap = [(0, 1), (1, 0)]
    conds = cond_index.shape[0]
    count = kernels.shape[2]
    block = (2 * BAND, 2 * HALF)
    beside = lax.ppermute(mask, AXES, swaps(mesh_shape, 0))
    fetched = local_tables(tile, window) + (target,)
    fetched += field_tables(tile, window) + adjoint_tables(tile, window)
    own, chosen, strength, *fetched = call(
        open_kernel,
        [block, (conds, count, 2, BAND * BAND), (conds, 8, tile)]
        + [jax.ShapeDtypeStruct(value.shape, value.dtype) for value in fetched],
        [HBM] * (4 + len(fetched)),
        (cond_index, dose, mask, jnp.transpose(kernels, (0, 2, 1, 3))) + fetched,
        scratch=[
            pltpu.SMEM(cond_index.shape, jnp.int32),
            pltpu.SMEM(dose.shape, F32),
            pltpu.VMEM(mask.shape, F32),
            pltpu.SemaphoreType.DMA((3 + conds + len(fetched),)),
        ],
    )
    beside, own, chosen, strength, fetched = lax.optimization_barrier(
        (beside, own, chosen, strength, fetched)
    )
    col_table, row_table, *later = fetched
    near = call(
        functools.partial(near_kernel, mesh_shape), [block], [VMEM] * 3,
        (beside, col_table, row_table),
    )
    far = lax.ppermute(near, "cond", swap)
    real = chosen[:, :, 0].reshape(conds * count * BAND, BAND)
    imag = chosen[:, :, 1].reshape(conds * count * BAND, BAND)
    total = conds * count
    arranged = call(arrange_kernel, [(BAND, total * HALF)] * 2, [VMEM] * 2, (real, imag))
    far, arranged = lax.optimization_barrier((far, arranged))
    message = own[:BAND] + near[:BAND] + far[:BAND]
    side = lax.ppermute(message, AXES, swaps(mesh_shape, 1))
    other = lax.ppermute(side, "cond", swap)

    cotangent = call(
        functools.partial(field_kernel, mesh_shape),
        [(BAND, 2 * HALF)],
        [VMEM] * 17,
        (strength, own, near, far, side, other, *arranged, *later[:-2]),
        scratch=[
            pltpu.VMEM((total * BAND, 2 * HALF), F32),
            pltpu.VMEM((total * BAND, 4 * HALF), F32),
        ],
    )
    theirs = lax.ppermute(cotangent, "cond", swap)
    return call(
        adjoint_kernel, [(tile, tile)], [VMEM] * 4, (cotangent, theirs, *later[-2:])
    )


def solution(mesh):
    in_specs = (P("row", "col"), P("row", "col"), P("cond"), P(), P())
    out_specs = P("row", "col")
    shape = tuple(mesh.shape[name] for name in AXES)
    body = functools.partial(shards, shape)
    return jax.shard_map(body, mesh=mesh, in_specs=in_specs, out_specs=out_specs, check_vma=False)
```

```python
import functools
import math

import jax
import jax.numpy as jnp
import numpy as np
from jax import lax
from jax.experimental import pallas as pl
from jax.experimental.pallas import tpu as pltpu
from jax.sharding import PartitionSpec as P

MARGIN = 128
BAND = 24
STEEP = 4.0
THRESH = 0.6

HALF = 64
AXES = ("row", "col", "cond")
BF = jnp.bfloat16
F32 = jnp.float32


def pieces(table, count):
    out, rest = [], np.asarray(table, np.float32)
    for _ in range(count):
        part = rest.astype(BF)
        out.append(part)
        rest = rest - part.astype(np.float32)
    return out


def angles(left, right, period):
    left, right = np.asarray(left, np.int64), np.asarray(right, np.int64)
    return (left[:, None] * right[None, :] % period) * (2.0 * math.pi / period)


def frequencies():
    return np.arange(BAND) - BAND // 2


def lanes(*blocks):
    rows = blocks[0][1].shape[0]
    width = -(-max(at + block.shape[1] for at, block in blocks) // 128) * 128
    out = np.zeros((rows, width))
    for at, block in blocks:
        out[:, at : at + block.shape[1]] = block
    return out


def rows_at(height, *blocks):
    out = np.zeros((height, blocks[0][1].shape[1]))
    for at, block in blocks:
        out[at : at + block.shape[0]] = block
    return out


def three(table):
    high, low = pieces(table, 2)
    return np.concatenate([high, high, low], 1)


def stacked(table, count):
    return np.concatenate(pieces(table, count), 0)


def local_tables(tile, window):
    places = np.arange(tile)
    cols = []
    for at, shift in ((0, 0), (HALF, 2 * MARGIN), (2 * HALF, MARGIN), (3 * HALF, MARGIN)):
        phase = angles(places + shift, frequencies(), window)
        cols += [(at, np.cos(phase)), (at + BAND, -np.sin(phase))]
    col_table = lanes(*cols) / window
    row_table = []
    for shift in (MARGIN, 0, 2 * MARGIN):
        phase = angles(frequencies(), places + shift, window)
        row_table += [np.cos(phase), -np.sin(phase)]
    return stacked(col_table, 2), three(np.concatenate(row_table, 0))


def field_tables(tile, window):
    count = 2 * BAND
    points = np.arange(count)
    phase = angles(frequencies(), points, count)
    cos, sin = np.cos(phase), np.sin(phase)
    one = np.concatenate(
        [lanes((0, cos), (HALF, sin)), lanes((0, -sin), (HALF, cos)), np.zeros((HALF - count, 2 * HALF))]
    )
    none = np.zeros_like(one)
    to_cols = np.concatenate(
        [np.concatenate([one, none], 1), np.concatenate([none, one], 1)], 0
    )
    to_rows = np.concatenate([cos.T, -sin.T], 1)
    where = (np.arange(tile)[:, None] + MARGIN) / window - points[None, :] / count
    spread = np.ones((tile, count))
    for order in range(1, BAND):
        spread += 2.0 * np.cos(2.0 * math.pi * order * where)
    spread /= count
    spread_cols = rows_at(HALF, (0, spread.T))
    gather_cols = lanes((0, spread), (HALF, spread))
    from_rows = np.concatenate([cos, sin], 0)
    return (
        stacked(to_cols, 2),
        three(to_rows),
        stacked(spread_cols, 2),
        three(spread),
        three(spread.T),
        stacked(gather_cols, 2),
        three(from_rows),
        np.concatenate(pieces(to_cols.T, 2), 1),
    )


def adjoint_tables(tile, window):
    places = np.arange(tile) + MARGIN
    phase = angles(frequencies(), places, window)
    cos, sin = np.cos(phase), np.sin(phase)
    first = np.concatenate([cos, -sin], 1)
    second = np.concatenate([-sin, -cos], 1)
    cols = rows_at(
        2 * HALF, (0, first), (BAND, first), (HALF, second), (HALF + BAND, second)
    )
    rows = np.concatenate([cos.T, sin.T], 1) / window
    return stacked(cols, 2), three(rows)


def toward(at, core, size):
    onward = lax.rem(at + core, 2) == 0
    other = jnp.where(onward, at + 1, at - 1)
    return onward, (other >= 0) & (other < size)


def dot(left, right):
    return jnp.dot(left, right, preferred_element_type=F32)


def split(value, count):
    out, rest = [], value
    for step in range(count):
        part = rest.astype(BF)
        out.append(part)
        if step + 1 < count:
            rest = rest - part.astype(F32)
    return out


def lane_ids(shape):
    return lax.broadcasted_iota(jnp.int32, shape, len(shape) - 1)


def doubled(value):
    high = value.astype(BF).astype(F32)
    part = jnp.where(lane_ids(value.shape) < HALF, high, value - high).astype(BF)
    return jnp.concatenate([part, part], 1)


def four_weights(ref):
    size = ref.shape[0] // 2
    high, low = ref[:size], ref[size:]
    return jnp.concatenate([high, high, low, low], 0)


def three_right(value):
    high, low = split(value, 2)
    return jnp.concatenate([high, low, high], 0)


def fetch(sources, targets, sems):
    copies = [
        pltpu.make_async_copy(source, target, sems.at[at])
        for at, (source, target) in enumerate(zip(sources, targets))
    ]
    for copy in copies:
        copy.start()
    return copies


def local_spectrum(tile_value, col_ref, row_table):
    size = col_ref.shape[0] // 2
    high, low = split(tile_value, 2)
    ch, cl = col_ref[:size], col_ref[size:]
    partial = dot(jnp.concatenate([high, low, high], 1), jnp.concatenate([ch, ch, cl], 0))
    both = dot(row_table, three_right(partial))
    top, bottom = both[:BAND], both[BAND:]
    lane = lane_ids(top.shape) % HALF
    turned = jnp.where(
        lane < BAND,
        -pltpu.roll(bottom, top.shape[1] - BAND, 1),
        jnp.where(lane < 2 * BAND, pltpu.roll(bottom, BAND, 1), 0.0),
    )
    result = top + turned
    return jnp.concatenate([result[:, : 2 * HALF], result[:, 2 * HALF :]], 0)


def open_kernel(*refs):
    cond_hbm, dose_hbm, mask_hbm, kernels_hbm = refs[:4]
    cond_ref, dose_ref, mask_ref, sems = refs[-4:]
    count = (len(refs) - 11) // 2
    sources, targets = refs[4 : 4 + count], refs[7 + count : 7 + 2 * count]
    own_ref, chosen_ref, strength_ref = refs[4 + count : 7 + count]
    conds = cond_hbm.shape[0]
    copies = []

    def start(source, target):
        copy = pltpu.make_async_copy(source, target, sems.at[len(copies)])
        copy.start()
        copies.append(copy)
        return copy

    scalars = [start(cond_hbm, cond_ref), start(dose_hbm, dose_ref)]
    first = [start(mask_hbm, mask_ref)]
    first += [start(source, target) for source, target in zip(sources[:2], targets[:2])]
    for copy in scalars:
        copy.wait()
    rest = [start(kernels_hbm.at[cond_ref[c]], chosen_ref.at[c]) for c in range(conds)]
    rest += [start(source, target) for source, target in zip(sources[2:], targets[2:])]
    for c in range(conds):
        strength_ref[c] = jnp.full(strength_ref.shape[1:], dose_ref[cond_ref[c]], F32)
    for copy in first:
        copy.wait()
    col_ref, row_ref = targets[:2]
    own_ref[...] = local_spectrum(mask_ref[...], col_ref, row_ref[: 2 * BAND])
    for copy in rest:
        copy.wait()


def near_kernel(mesh_shape, tile_ref, col_ref, row_ref, out_ref):
    down, valid = toward(lax.axis_index("row"), lax.axis_index("cond"), mesh_shape[0])
    at = pl.multiple_of(jnp.where(down, 4 * BAND, 2 * BAND), 2 * BAND)
    share = local_spectrum(tile_ref[...], col_ref, row_ref[pl.ds(at, 2 * BAND)])
    out_ref[...] = jnp.where(valid, share, 0.0)


def arrange_kernel(real_ref, imag_ref, first_ref, second_ref):
    total = real_ref.shape[0] // BAND
    for pair in range(total // 2):
        first, second = 0.0, 0.0
        for part in range(2):
            at = (2 * pair + part) * BAND
            pad = jnp.zeros((BAND, 2 * HALF - BAND), F32)
            real = jnp.concatenate([real_ref[at : at + BAND, :], pad], 1)
            imag = jnp.concatenate([imag_ref[at : at + BAND, :], pad], 1)

            def moved(value, by):
                return pltpu.roll(value, part * HALF + by, 1) if part * HALF + by else value

            first = first + (moved(real, 0) + moved(imag, BAND))
            second = second + (moved(real, BAND) - moved(imag, 0))
        first_ref[:, pair * 2 * HALF : (pair + 1) * 2 * HALF] = first
        second_ref[:, pair * 2 * HALF : (pair + 1) * 2 * HALF] = second


def field_kernel(
    mesh_shape, strength_ref, own_ref, near_ref, far_ref, side_ref, other_ref,
    first_ref, second_ref, target_ref, to_cols_ref, to_rows_ref, spread_cols_ref, spread_ref,
    gather_rows_ref, gather_cols_ref, from_rows_ref, from_cols_ref, out_ref, rows_ref, field_ref,
):
    conds = strength_ref.shape[0]
    count = 2 * BAND
    pairs = first_ref.shape[1] // (2 * HALF)
    per = 2 * pairs // conds
    tile = target_ref.shape[0]
    wide = 4 * HALF
    col, core = lax.axis_index("col"), lax.axis_index("cond")

    def half(value, core):
        onward, valid = toward(col, core, mesh_shape[1])
        low_half = lane_ids(value.shape) < HALF
        kept = jnp.where(onward, jnp.where(low_half, 0.0, value), jnp.where(low_half, value, 0.0))
        kept = jnp.where(valid, kept, 0.0)
        return kept + pltpu.roll(kept, HALF, 1)

    spectrum = own_ref[BAND:] + near_ref[BAND:] + far_ref[BAND:]
    spectrum += half(side_ref[...], core) + half(other_ref[...], 1 - core)
    lane = lane_ids(spectrum.shape) % HALF
    real = jnp.where(lane < BAND, spectrum, 0.0)
    imag = jnp.where(lane >= BAND, spectrum, 0.0)
    real = real + pltpu.roll(real, BAND, 1)
    imag = imag + pltpu.roll(imag, 2 * HALF - BAND, 1)

    to_rows = to_rows_ref[...]
    for quad in range(pairs // 2):
        blocks = []
        for pair in (2 * quad, 2 * quad + 1):
            one = first_ref[:, pair * 2 * HALF : (pair + 1) * 2 * HALF]
            two = second_ref[:, pair * 2 * HALF : (pair + 1) * 2 * HALF]
            blocks.append(jnp.concatenate([one * real + two * imag, one * imag - two * real], 0))
        both = dot(to_rows, three_right(jnp.concatenate(blocks, 1)))
        for part in range(2):
            at = (2 * quad + part) * count
            rows_ref[at : at + count, :] = both[:, part * 2 * HALF : (part + 1) * 2 * HALF]

    weights = four_weights(to_cols_ref)
    chunk = rows_ref.shape[0] // 2
    for at in (0, chunk):
        high, low = split(rows_ref[at : at + chunk, :], 2)
        field_ref[at : at + chunk, :] = dot(jnp.concatenate([high, low, high, low], 1), weights)
    sums = [jnp.zeros((count, 2 * HALF), F32) for _ in range(conds)]
    for pair in range(pairs):
        both = field_ref[pair * count : (pair + 1) * count, :]
        squares = both * both
        for part in range(2):
            c = (2 * pair + part) // per
            sums[c] = sums[c] + squares[:, part * 2 * HALF : (part + 1) * 2 * HALF]

    coarse = jnp.concatenate([value + pltpu.roll(value, HALF, 1) for value in sums], 0)
    lines = dot(doubled(coarse), four_weights(spread_cols_ref))
    right = jnp.concatenate(
        [three_right(lines[c * count : (c + 1) * count]) for c in range(conds)], 1
    )
    image = dot(spread_ref[...], right)

    goal = target_ref[...].astype(F32)
    norm = 1.0 / (per * BAND * BAND)
    slopes = []
    for c in range(conds):
        strength = strength_ref[c][:1]
        intensity = image[:, c * tile : (c + 1) * tile] * norm
        resist = jax.nn.sigmoid(STEEP * (strength * intensity - THRESH))
        slope = (resist - goal) * resist * (1.0 - resist)
        slopes.append(slope * (4.0 * STEEP * norm * strength))
    back = dot(gather_rows_ref[...], three_right(jnp.concatenate(slopes, 1)))
    high, low = split(
        jnp.concatenate([back[:, c * tile : (c + 1) * tile] for c in range(conds)], 0), 2
    )
    gh, gl = gather_cols_ref[:tile], gather_cols_ref[tile:]
    slope = dot(jnp.concatenate([high, low, high], 1), jnp.concatenate([gh, gh, gl], 0))

    for pair in range(pairs):
        weight = []
        for k in (2 * pair, 2 * pair + 1):
            weight.append(slope[k // per * count : (k // per + 1) * count])
        at = pair * count
        field_ref[at : at + count, :] = field_ref[at : at + count, :] * jnp.concatenate(weight, 1)
    weights = from_cols_ref[...]
    weights = jnp.concatenate(
        [
            weights,
            jnp.concatenate([weights[:, : 2 * HALF], jnp.zeros((wide, 2 * HALF), BF)], 1),
        ],
        0,
    )
    for at in (0, chunk):
        high, low = split(field_ref[at : at + chunk, :], 2)
        back = dot(jnp.concatenate([high, low], 1), weights)
        rows_ref[at : at + chunk, :] = back[:, : 2 * HALF] + back[:, 2 * HALF :]

    from_rows = from_rows_ref[...]
    sum_one, sum_two = 0.0, 0.0
    for quad in range(pairs // 2):
        at = 2 * quad * count
        value = jnp.concatenate(
            [rows_ref[at : at + count, :], rows_ref[at + count : at + 2 * count, :]], 1
        )
        back = dot(from_rows, three_right(value))
        top, bottom = back[:BAND], back[BAND:]
        one = first_ref[:, quad * wide : (quad + 1) * wide]
        two = second_ref[:, quad * wide : (quad + 1) * wide]
        sum_one = sum_one + (one * top + two * bottom)
        sum_two = sum_two + (two * top - one * bottom)
    sum_one = sum_one[:, : 2 * HALF] + sum_one[:, 2 * HALF :]
    sum_two = sum_two[:, : 2 * HALF] + sum_two[:, 2 * HALF :]
    out_ref[...] = jnp.where(
        lane_ids(sum_one.shape) < HALF,
        sum_one + pltpu.roll(sum_one, HALF, 1),
        sum_two + pltpu.roll(sum_two, HALF, 1),
    )


def adjoint_kernel(mine_ref, theirs_ref, cols_ref, rows_ref, out_ref):
    tile = out_ref.shape[1]
    high, low = split(mine_ref[...] + theirs_ref[...], 2)
    size = cols_ref.shape[0] // 2
    ch, cl = cols_ref[:size], cols_ref[size:]
    halves = dot(jnp.concatenate([high, low, high], 1), jnp.concatenate([ch, ch, cl], 0))
    joined = jnp.concatenate([halves[:, :tile], halves[:, tile:]], 0)
    out_ref[...] = dot(rows_ref[...], three_right(joined))


VMEM = pl.BlockSpec(memory_space=pltpu.VMEM)
SMEM = pl.BlockSpec(memory_space=pltpu.SMEM)
HBM = pl.BlockSpec(memory_space=pltpu.HBM)


def call(body, outs, specs, args, scratch=(), flops=1000000, grant=8):
    shapes = [
        shape if hasattr(shape, "dtype") else jax.ShapeDtypeStruct(shape, F32) for shape in outs
    ]
    one = len(outs) == 1
    args = [
        pltpu.with_memory_space_constraint(value, pltpu.HBM) if spec is HBM else value
        for spec, value in zip(specs, args)
    ]
    return pl.pallas_call(
        body,
        out_shape=shapes[0] if one else shapes,
        in_specs=specs,
        out_specs=VMEM if one else [VMEM] * len(outs),
        scratch_shapes=list(scratch),
        compiler_params=pltpu.CompilerParams(vmem_limit_bytes=grant * 2**20),
        cost_estimate=pl.CostEstimate(flops=flops, bytes_accessed=1000000, transcendentals=0),
    )(*args)


def partner(at, core, size):
    other = at ^ 1 if core == 0 else ((at + 1) ^ 1) - 1
    return other if 0 <= other < size else None


def swaps(mesh_shape, along):
    rows, cols, cores = mesh_shape
    out = []
    for r in range(rows):
        for c in range(cols):
            for k in range(cores):
                at, size = (r, rows) if along == 0 else (c, cols)
                other = partner(at, k, size)
                if other is not None:
                    to = (other, c, k) if along == 0 else (r, other, k)
                elif along == 0:
                    to = (r, c ^ 1, k)
                else:
                    to = (r ^ 1, c, k)
                if to[0] < rows and to[1] < cols:
                    out.append((((r * cols) + c) * cores + k, ((to[0] * cols) + to[1]) * cores + to[2]))
    return out


def shards(mesh_shape, mask, target, cond_index, kernels, dose):
    tile = mask.shape[0]
    window = tile + 2 * MARGIN
    swap = [(0, 1), (1, 0)]
    conds = cond_index.shape[0]
    count = kernels.shape[2]
    block = (2 * BAND, 2 * HALF)
    beside = lax.ppermute(mask, AXES, swaps(mesh_shape, 0))
    fetched = local_tables(tile, window) + (target,)
    fetched += field_tables(tile, window) + adjoint_tables(tile, window)
    own, chosen, strength, *fetched = call(
        open_kernel,
        [block, (conds, count, 2, BAND * BAND), (conds, 8, tile)]
        + [jax.ShapeDtypeStruct(value.shape, value.dtype) for value in fetched],
        [HBM] * (4 + len(fetched)),
        (cond_index, dose, mask, jnp.transpose(kernels, (0, 2, 1, 3))) + fetched,
        scratch=[
            pltpu.SMEM(cond_index.shape, jnp.int32),
            pltpu.SMEM(dose.shape, F32),
            pltpu.VMEM(mask.shape, F32),
            pltpu.SemaphoreType.DMA((3 + conds + len(fetched),)),
        ],
    )
    beside, own, chosen, strength, fetched = lax.optimization_barrier(
        (beside, own, chosen, strength, fetched)
    )
    col_table, row_table, *later = fetched
    near = call(
        functools.partial(near_kernel, mesh_shape), [block], [VMEM] * 3,
        (beside, col_table, row_table),
    )
    far = lax.ppermute(near, "cond", swap)
    real = chosen[:, :, 0].reshape(conds * count * BAND, BAND)
    imag = chosen[:, :, 1].reshape(conds * count * BAND, BAND)
    total = conds * count
    arranged = call(arrange_kernel, [(BAND, total * HALF)] * 2, [VMEM] * 2, (real, imag))
    far, arranged = lax.optimization_barrier((far, arranged))
    message = own[:BAND] + near[:BAND] + far[:BAND]
    side = lax.ppermute(message, AXES, swaps(mesh_shape, 1))
    other = lax.ppermute(side, "cond", swap)

    cotangent = call(
        functools.partial(field_kernel, mesh_shape),
        [(BAND, 2 * HALF)],
        [VMEM] * 17,
        (strength, own, near, far, side, other, *arranged, *later[:-2]),
        scratch=[
            pltpu.VMEM((total * BAND, 2 * HALF), F32),
            pltpu.VMEM((total * BAND, 4 * HALF), F32),
        ],
    )
    theirs = lax.ppermute(cotangent, "cond", swap)
    return call(
        adjoint_kernel, [(tile, tile)], [VMEM] * 4, (cotangent, theirs, *later[-2:])
    )


def solution(mesh):
    in_specs = (P("row", "col"), P("row", "col"), P("cond"), P(), P())
    out_specs = P("row", "col")
    shape = tuple(mesh.shape[name] for name in AXES)
    body = functools.partial(shards, shape)
    return jax.shard_map(body, mesh=mesh, in_specs=in_specs, out_specs=out_specs, check_vma=False)
```

```python
import functools
import math

import jax
import jax.numpy as jnp
import numpy as np
from jax import lax
from jax.experimental import pallas as pl
from jax.experimental.pallas import tpu as pltpu
from jax.sharding import PartitionSpec as P

MARGIN = 128
BAND = 24
STEEP = 4.0
THRESH = 0.6

HALF = 64
AXES = ("row", "col", "cond")
BF = jnp.bfloat16
F32 = jnp.float32


def pieces(table, count):
    out, rest = [], np.asarray(table, np.float32)
    for _ in range(count):
        part = rest.astype(BF)
        out.append(part)
        rest = rest - part.astype(np.float32)
    return out


def angles(left, right, period):
    left, right = np.asarray(left, np.int64), np.asarray(right, np.int64)
    return (left[:, None] * right[None, :] % period) * (2.0 * math.pi / period)


def frequencies():
    return np.arange(BAND) - BAND // 2


def lanes(*blocks):
    rows = blocks[0][1].shape[0]
    width = -(-max(at + block.shape[1] for at, block in blocks) // 128) * 128
    out = np.zeros((rows, width))
    for at, block in blocks:
        out[:, at : at + block.shape[1]] = block
    return out


def rows_at(height, *blocks):
    out = np.zeros((height, blocks[0][1].shape[1]))
    for at, block in blocks:
        out[at : at + block.shape[0]] = block
    return out


def three(table):
    high, low = pieces(table, 2)
    return np.concatenate([high, high, low], 1)


def stacked(table, count):
    return np.concatenate(pieces(table, count), 0)


def local_tables(tile, window):
    places = np.arange(tile)
    shifts = (MARGIN, 0, 2 * MARGIN)
    col_table, real, imag = [], [], []
    for shift in shifts:
        phase = angles(places + shift, frequencies(), window)
        block = np.concatenate([np.cos(phase), -np.sin(phase)], 1) / window
        col_table.append(stacked(lanes((0, block), (HALF, block)), 2))
        real.append(np.cos(phase.T))
        imag.append(-np.sin(phase.T))
    return np.concatenate(col_table, 0), three(np.concatenate(real + imag, 0))


def field_tables(tile, window):
    count = 2 * BAND
    points = np.arange(count)
    phase = angles(frequencies(), points, count)
    cos, sin = np.cos(phase), np.sin(phase)
    one = np.concatenate(
        [lanes((0, cos), (HALF, sin)), lanes((0, -sin), (HALF, cos)), np.zeros((HALF - count, 2 * HALF))]
    )
    none = np.zeros_like(one)
    to_cols = np.concatenate(
        [np.concatenate([one, none], 1), np.concatenate([none, one], 1)], 0
    )
    to_rows = np.concatenate([cos.T, -sin.T], 1)
    where = (np.arange(tile)[:, None] + MARGIN) / window - points[None, :] / count
    spread = np.ones((tile, count))
    for order in range(1, BAND):
        spread += 2.0 * np.cos(2.0 * math.pi * order * where)
    spread /= count
    spread_cols = rows_at(HALF, (0, spread.T))
    gather_cols = lanes((0, spread), (HALF, spread))
    from_rows = np.concatenate([cos, sin], 0)
    return (
        stacked(to_cols, 2),
        three(to_rows),
        stacked(spread_cols, 2),
        three(spread),
        three(spread.T),
        stacked(gather_cols, 2),
        three(from_rows),
        np.concatenate(pieces(to_cols.T, 2), 1),
    )


def adjoint_tables(tile, window):
    places = np.arange(tile) + MARGIN
    phase = angles(frequencies(), places, window)
    cos, sin = np.cos(phase), np.sin(phase)
    first = np.concatenate([cos, -sin], 1)
    second = np.concatenate([-sin, -cos], 1)
    cols = rows_at(
        2 * HALF, (0, first), (BAND, first), (HALF, second), (HALF + BAND, second)
    )
    rows = np.concatenate([cos.T, sin.T], 1) / window
    return stacked(cols, 2), three(rows)


def toward(at, core, size):
    onward = lax.rem(at + core, 2) == 0
    other = jnp.where(onward, at + 1, at - 1)
    return onward, (other >= 0) & (other < size)


def dot(left, right):
    return jnp.dot(left, right, preferred_element_type=F32)


def split(value, count):
    out, rest = [], value
    for step in range(count):
        part = rest.astype(BF)
        out.append(part)
        if step + 1 < count:
            rest = rest - part.astype(F32)
    return out


def lane_ids(shape):
    return lax.broadcasted_iota(jnp.int32, shape, len(shape) - 1)


def doubled(value):
    high = value.astype(BF).astype(F32)
    part = jnp.where(lane_ids(value.shape) < HALF, high, value - high).astype(BF)
    return jnp.concatenate([part, part], 1)


def four_weights(ref):
    size = ref.shape[0] // 2
    high, low = ref[:size], ref[size:]
    return jnp.concatenate([high, high, low, low], 0)


def three_right(value):
    high, low = split(value, 2)
    return jnp.concatenate([high, low, high], 0)


def fetch(sources, targets, sems):
    copies = [
        pltpu.make_async_copy(source, target, sems.at[at])
        for at, (source, target) in enumerate(zip(sources, targets))
    ]
    for copy in copies:
        copy.start()
    return copies


def local_spectrum(tile_value, col_table, row_table):
    size = col_table.shape[0] // 2
    high, low = split(tile_value, 2)
    ch, cl = col_table[:size], col_table[size:]
    partial = dot(jnp.concatenate([high, low, high], 1), jnp.concatenate([ch, ch, cl], 0))
    both = dot(row_table, three_right(partial))
    top, bottom = both[: 3 * BAND], both[3 * BAND :]
    lane = lane_ids(top.shape) % HALF
    turned = jnp.where(
        lane < BAND,
        -pltpu.roll(bottom, top.shape[1] - BAND, 1),
        jnp.where(lane < 2 * BAND, pltpu.roll(bottom, BAND, 1), 0.0),
    )
    result = top + turned
    centre, first, last = (result[at * BAND : (at + 1) * BAND] for at in range(3))
    return jnp.concatenate([jnp.where(lane_ids(first.shape) < HALF, first, last), centre], 0)


def open_kernel(*refs):
    cond_hbm, dose_hbm, mask_hbm, kernels_hbm = refs[:4]
    cond_ref, dose_ref, mask_ref, sems = refs[-4:]
    count = (len(refs) - 11) // 2
    sources, targets = refs[4 : 4 + count], refs[7 + count : 7 + 2 * count]
    own_ref, chosen_ref, strength_ref = refs[4 + count : 7 + count]
    conds = cond_hbm.shape[0]
    copies = []

    def start(source, target):
        copy = pltpu.make_async_copy(source, target, sems.at[len(copies)])
        copy.start()
        copies.append(copy)
        return copy

    scalars = [start(cond_hbm, cond_ref), start(dose_hbm, dose_ref)]
    first = [start(mask_hbm, mask_ref)]
    first += [start(source, target) for source, target in zip(sources[:2], targets[:2])]
    for copy in scalars:
        copy.wait()
    rest = [start(kernels_hbm.at[cond_ref[c]], chosen_ref.at[c]) for c in range(conds)]
    rest += [start(source, target) for source, target in zip(sources[2:], targets[2:])]
    for c in range(conds):
        strength_ref[c] = jnp.full(strength_ref.shape[1:], dose_ref[cond_ref[c]], F32)
    for copy in first:
        copy.wait()
    col_ref, row_ref = targets[:2]
    own_ref[...] = local_spectrum(
        mask_ref[...], col_ref[: 2 * mask_ref.shape[0]], row_ref[...]
    )
    for copy in rest:
        copy.wait()


def near_kernel(mesh_shape, tile_ref, col_ref, row_ref, out_ref):
    right, valid = toward(lax.axis_index("col"), lax.axis_index("cond"), mesh_shape[1])
    size = 2 * tile_ref.shape[0]
    at = pl.multiple_of(jnp.where(right, 2 * size, size), size)
    share = local_spectrum(tile_ref[...], col_ref[pl.ds(at, size)], row_ref[...])
    out_ref[...] = jnp.where(valid, share, 0.0)


def arrange_kernel(real_ref, imag_ref, first_ref, second_ref):
    total = real_ref.shape[0] // BAND
    for pair in range(total // 2):
        first, second = 0.0, 0.0
        for part in range(2):
            at = (2 * pair + part) * BAND
            pad = jnp.zeros((BAND, 2 * HALF - BAND), F32)
            real = jnp.concatenate([real_ref[at : at + BAND, :], pad], 1)
            imag = jnp.concatenate([imag_ref[at : at + BAND, :], pad], 1)

            def moved(value, by):
                return pltpu.roll(value, part * HALF + by, 1) if part * HALF + by else value

            first = first + (moved(real, 0) + moved(imag, BAND))
            second = second + (moved(real, BAND) - moved(imag, 0))
        first_ref[:, pair * 2 * HALF : (pair + 1) * 2 * HALF] = first
        second_ref[:, pair * 2 * HALF : (pair + 1) * 2 * HALF] = second


def field_kernel(
    mesh_shape, strength_ref, own_ref, near_ref, far_ref, side_ref, other_ref,
    first_ref, second_ref, target_ref, to_cols_ref, to_rows_ref, spread_cols_ref, spread_ref,
    gather_rows_ref, gather_cols_ref, from_rows_ref, from_cols_ref, out_ref, rows_ref, field_ref,
):
    conds = strength_ref.shape[0]
    count = 2 * BAND
    pairs = first_ref.shape[1] // (2 * HALF)
    per = 2 * pairs // conds
    tile = target_ref.shape[0]
    wide = 4 * HALF
    row, core = lax.axis_index("row"), lax.axis_index("cond")

    def half(value, core):
        onward, valid = toward(row, core, mesh_shape[0])
        low_half = lane_ids(value.shape) < HALF
        kept = jnp.where(onward, jnp.where(low_half, 0.0, value), jnp.where(low_half, value, 0.0))
        kept = jnp.where(valid, kept, 0.0)
        return kept + pltpu.roll(kept, HALF, 1)

    spectrum = own_ref[BAND:] + near_ref[BAND:] + far_ref[BAND:]
    spectrum += half(side_ref[...], core) + half(other_ref[...], 1 - core)
    lane = lane_ids(spectrum.shape) % HALF
    real = jnp.where(lane < BAND, spectrum, 0.0)
    imag = jnp.where(lane >= BAND, spectrum, 0.0)
    real = real + pltpu.roll(real, BAND, 1)
    imag = imag + pltpu.roll(imag, 2 * HALF - BAND, 1)

    to_rows = to_rows_ref[...]
    for quad in range(pairs // 2):
        blocks = []
        for pair in (2 * quad, 2 * quad + 1):
            one = first_ref[:, pair * 2 * HALF : (pair + 1) * 2 * HALF]
            two = second_ref[:, pair * 2 * HALF : (pair + 1) * 2 * HALF]
            blocks.append(jnp.concatenate([one * real + two * imag, one * imag - two * real], 0))
        both = dot(to_rows, three_right(jnp.concatenate(blocks, 1)))
        for part in range(2):
            at = (2 * quad + part) * count
            rows_ref[at : at + count, :] = both[:, part * 2 * HALF : (part + 1) * 2 * HALF]

    weights = four_weights(to_cols_ref)
    chunk = rows_ref.shape[0] // 2
    for at in (0, chunk):
        high, low = split(rows_ref[at : at + chunk, :], 2)
        field_ref[at : at + chunk, :] = dot(jnp.concatenate([high, low, high, low], 1), weights)
    sums = [jnp.zeros((count, 2 * HALF), F32) for _ in range(conds)]
    for pair in range(pairs):
        both = field_ref[pair * count : (pair + 1) * count, :]
        squares = both * both
        for part in range(2):
            c = (2 * pair + part) // per
            sums[c] = sums[c] + squares[:, part * 2 * HALF : (part + 1) * 2 * HALF]

    coarse = jnp.concatenate([value + pltpu.roll(value, HALF, 1) for value in sums], 0)
    lines = dot(doubled(coarse), four_weights(spread_cols_ref))
    right = jnp.concatenate(
        [three_right(lines[c * count : (c + 1) * count]) for c in range(conds)], 1
    )
    image = dot(spread_ref[...], right)

    goal = target_ref[...].astype(F32)
    norm = 1.0 / (per * BAND * BAND)
    slopes = []
    for c in range(conds):
        strength = strength_ref[c][:1]
        intensity = image[:, c * tile : (c + 1) * tile] * norm
        resist = jax.nn.sigmoid(STEEP * (strength * intensity - THRESH))
        slope = (resist - goal) * resist * (1.0 - resist)
        slopes.append(slope * (4.0 * STEEP * norm * strength))
    back = dot(gather_rows_ref[...], three_right(jnp.concatenate(slopes, 1)))
    high, low = split(
        jnp.concatenate([back[:, c * tile : (c + 1) * tile] for c in range(conds)], 0), 2
    )
    gh, gl = gather_cols_ref[:tile], gather_cols_ref[tile:]
    slope = dot(jnp.concatenate([high, low, high], 1), jnp.concatenate([gh, gh, gl], 0))

    for pair in range(pairs):
        weight = []
        for k in (2 * pair, 2 * pair + 1):
            weight.append(slope[k // per * count : (k // per + 1) * count])
        at = pair * count
        field_ref[at : at + count, :] = field_ref[at : at + count, :] * jnp.concatenate(weight, 1)
    weights = from_cols_ref[...]
    weights = jnp.concatenate(
        [
            weights,
            jnp.concatenate([weights[:, : 2 * HALF], jnp.zeros((wide, 2 * HALF), BF)], 1),
        ],
        0,
    )
    for at in (0, chunk):
        high, low = split(field_ref[at : at + chunk, :], 2)
        back = dot(jnp.concatenate([high, low], 1), weights)
        rows_ref[at : at + chunk, :] = back[:, : 2 * HALF] + back[:, 2 * HALF :]

    from_rows = from_rows_ref[...]
    sum_one, sum_two = 0.0, 0.0
    for quad in range(pairs // 2):
        at = 2 * quad * count
        value = jnp.concatenate(
            [rows_ref[at : at + count, :], rows_ref[at + count : at + 2 * count, :]], 1
        )
        back = dot(from_rows, three_right(value))
        top, bottom = back[:BAND], back[BAND:]
        one = first_ref[:, quad * wide : (quad + 1) * wide]
        two = second_ref[:, quad * wide : (quad + 1) * wide]
        sum_one = sum_one + (one * top + two * bottom)
        sum_two = sum_two + (two * top - one * bottom)
    sum_one = sum_one[:, : 2 * HALF] + sum_one[:, 2 * HALF :]
    sum_two = sum_two[:, : 2 * HALF] + sum_two[:, 2 * HALF :]
    out_ref[...] = jnp.where(
        lane_ids(sum_one.shape) < HALF,
        sum_one + pltpu.roll(sum_one, HALF, 1),
        sum_two + pltpu.roll(sum_two, HALF, 1),
    )


def adjoint_kernel(mine_ref, theirs_ref, cols_ref, rows_ref, out_hbm, out_ref, sems):
    tile = out_ref.shape[1]
    high, low = split(mine_ref[...] + theirs_ref[...], 2)
    size = cols_ref.shape[0] // 2
    ch, cl = cols_ref[:size], cols_ref[size:]
    halves = dot(jnp.concatenate([high, low, high], 1), jnp.concatenate([ch, ch, cl], 0))
    joined = three_right(jnp.concatenate([halves[:, :tile], halves[:, tile:]], 0))
    count = sems.shape[0]
    step = tile // count
    copies = []
    for at in range(count):
        rows = pl.ds(at * step, step)
        out_ref[rows] = dot(rows_ref[rows], joined)
        copies.append(pltpu.make_async_copy(out_ref.at[rows], out_hbm.at[rows], sems.at[at]))
        copies[-1].start()
    for copy in copies:
        copy.wait()


VMEM = pl.BlockSpec(memory_space=pltpu.VMEM)
SMEM = pl.BlockSpec(memory_space=pltpu.SMEM)
HBM = pl.BlockSpec(memory_space=pltpu.HBM)


def call(body, outs, specs, args, scratch=(), flops=1000000, grant=8, out_spec=None):
    shapes = [
        shape if hasattr(shape, "dtype") else jax.ShapeDtypeStruct(shape, F32) for shape in outs
    ]
    one = len(outs) == 1
    args = [
        pltpu.with_memory_space_constraint(value, pltpu.HBM) if spec is HBM else value
        for spec, value in zip(specs, args)
    ]
    return pl.pallas_call(
        body,
        out_shape=shapes[0] if one else shapes,
        in_specs=specs,
        out_specs=(out_spec or VMEM) if one else [VMEM] * len(outs),
        scratch_shapes=list(scratch),
        compiler_params=pltpu.CompilerParams(vmem_limit_bytes=grant * 2**20),
        cost_estimate=pl.CostEstimate(flops=flops, bytes_accessed=1000000, transcendentals=0),
    )(*args)


def partner(at, core, size):
    other = at ^ 1 if core == 0 else ((at + 1) ^ 1) - 1
    return other if 0 <= other < size else None


def swaps(mesh_shape, along):
    rows, cols, cores = mesh_shape
    out = []
    for r in range(rows):
        for c in range(cols):
            for k in range(cores):
                at, size = (r, rows) if along == 0 else (c, cols)
                other = partner(at, k, size)
                if other is not None:
                    to = (other, c, k) if along == 0 else (r, other, k)
                elif along == 0:
                    to = (r, c ^ 1, k)
                else:
                    to = (r ^ 1, c, k)
                if to[0] < rows and to[1] < cols:
                    out.append((((r * cols) + c) * cores + k, ((to[0] * cols) + to[1]) * cores + to[2]))
    return out


def shards(mesh_shape, mask, target, cond_index, kernels, dose):
    tile = mask.shape[0]
    window = tile + 2 * MARGIN
    swap = [(0, 1), (1, 0)]
    conds = cond_index.shape[0]
    count = kernels.shape[2]
    block = (2 * BAND, 2 * HALF)
    beside = lax.ppermute(mask, AXES, swaps(mesh_shape, 1))
    fetched = local_tables(tile, window) + (target,)
    fetched += field_tables(tile, window) + adjoint_tables(tile, window)
    own, chosen, strength, *fetched = call(
        open_kernel,
        [block, (conds, count, 2, BAND * BAND), (conds, 8, tile)]
        + [jax.ShapeDtypeStruct(value.shape, value.dtype) for value in fetched],
        [HBM] * (4 + len(fetched)),
        (cond_index, dose, mask, jnp.transpose(kernels, (0, 2, 1, 3))) + fetched,
        scratch=[
            pltpu.SMEM(cond_index.shape, jnp.int32),
            pltpu.SMEM(dose.shape, F32),
            pltpu.VMEM(mask.shape, F32),
            pltpu.SemaphoreType.DMA((3 + conds + len(fetched),)),
        ],
    )
    beside, own, chosen, strength, fetched = lax.optimization_barrier(
        (beside, own, chosen, strength, fetched)
    )
    col_table, row_table, *later = fetched
    near = call(
        functools.partial(near_kernel, mesh_shape), [block], [VMEM] * 3,
        (beside, col_table, row_table),
    )
    far = lax.ppermute(near, "cond", swap)
    real = chosen[:, :, 0].reshape(conds * count * BAND, BAND)
    imag = chosen[:, :, 1].reshape(conds * count * BAND, BAND)
    total = conds * count
    arranged = call(arrange_kernel, [(BAND, total * HALF)] * 2, [VMEM] * 2, (real, imag))
    far, arranged = lax.optimization_barrier((far, arranged))
    message = own[:BAND] + near[:BAND] + far[:BAND]
    side = lax.ppermute(message, AXES, swaps(mesh_shape, 0))
    other = lax.ppermute(side, "cond", swap)

    cotangent = call(
        functools.partial(field_kernel, mesh_shape),
        [(BAND, 2 * HALF)],
        [VMEM] * 17,
        (strength, own, near, far, side, other, *arranged, *later[:-2]),
        scratch=[
            pltpu.VMEM((total * BAND, 2 * HALF), F32),
            pltpu.VMEM((total * BAND, 4 * HALF), F32),
        ],
    )
    theirs = lax.ppermute(cotangent, "cond", swap)
    return call(
        adjoint_kernel, [(tile, tile)], [VMEM] * 4, (cotangent, theirs, *later[-2:]),
        scratch=[pltpu.VMEM((tile, tile), F32), pltpu.SemaphoreType.DMA((4,))], out_spec=HBM,
    )


def solution(mesh):
    in_specs = (P("row", "col"), P("row", "col"), P("cond"), P(), P())
    out_specs = P("row", "col")
    shape = tuple(mesh.shape[name] for name in AXES)
    body = functools.partial(shards, shape)
    return jax.shard_map(body, mesh=mesh, in_specs=in_specs, out_specs=out_specs, check_vma=False)
```

```python
import functools
import math

import jax
import jax.numpy as jnp
import numpy as np
from jax import lax
from jax.experimental import pallas as pl
from jax.experimental.pallas import tpu as pltpu
from jax.sharding import PartitionSpec as P

MARGIN = 128
BAND = 24
STEEP = 4.0
THRESH = 0.6

HALF = 64
AXES = ("row", "col", "cond")
BF = jnp.bfloat16
F32 = jnp.float32


def pieces(table, count):
    out, rest = [], np.asarray(table, np.float32)
    for _ in range(count):
        part = rest.astype(BF)
        out.append(part)
        rest = rest - part.astype(np.float32)
    return out


def angles(left, right, period):
    left, right = np.asarray(left, np.int64), np.asarray(right, np.int64)
    return (left[:, None] * right[None, :] % period) * (2.0 * math.pi / period)


def frequencies():
    return np.arange(BAND) - BAND // 2


def lanes(*blocks):
    rows = blocks[0][1].shape[0]
    width = -(-max(at + block.shape[1] for at, block in blocks) // 128) * 128
    out = np.zeros((rows, width))
    for at, block in blocks:
        out[:, at : at + block.shape[1]] = block
    return out


def rows_at(height, *blocks):
    out = np.zeros((height, blocks[0][1].shape[1]))
    for at, block in blocks:
        out[at : at + block.shape[0]] = block
    return out


def three(table):
    high, low = pieces(table, 2)
    return np.concatenate([high, high, low], 1)


def stacked(table, count):
    return np.concatenate(pieces(table, count), 0)


def local_tables(tile, window):
    places = np.arange(tile)
    shifts = (MARGIN, 0, 2 * MARGIN)
    col_table, real, imag = [], [], []
    for shift in shifts:
        phase = angles(places + shift, frequencies(), window)
        block = np.concatenate([np.cos(phase), -np.sin(phase)], 1) / window
        col_table.append(stacked(lanes((0, block), (HALF, block)), 2))
        real.append(np.cos(phase.T))
        imag.append(-np.sin(phase.T))
    return np.concatenate(col_table, 0), three(np.concatenate(real + imag, 0))


def field_tables(tile, window):
    count = 2 * BAND
    points = np.arange(count)
    phase = angles(frequencies(), points, count)
    cos, sin = np.cos(phase), np.sin(phase)
    one = np.concatenate(
        [lanes((0, cos), (HALF, sin)), lanes((0, -sin), (HALF, cos)), np.zeros((HALF - count, 2 * HALF))]
    )
    none = np.zeros_like(one)
    to_cols = np.concatenate(
        [np.concatenate([one, none], 1), np.concatenate([none, one], 1)], 0
    )
    to_rows = np.concatenate([cos.T, -sin.T], 1)
    where = (np.arange(tile)[:, None] + MARGIN) / window - points[None, :] / count
    spread = np.ones((tile, count))
    for order in range(1, BAND):
        spread += 2.0 * np.cos(2.0 * math.pi * order * where)
    spread /= count
    spread_cols = rows_at(HALF, (0, spread.T))
    gather_cols = lanes((0, spread), (HALF, spread))
    from_rows = np.concatenate([cos, sin], 0)
    return (
        stacked(to_cols, 2),
        three(to_rows),
        stacked(spread_cols, 2),
        three(spread),
        three(spread.T),
        stacked(gather_cols, 2),
        three(from_rows),
        np.concatenate(pieces(to_cols.T, 2), 1),
    )


def adjoint_tables(tile, window):
    places = np.arange(tile) + MARGIN
    phase = angles(frequencies(), places, window)
    cos, sin = np.cos(phase), np.sin(phase)
    first = np.concatenate([cos, -sin], 1)
    second = np.concatenate([-sin, -cos], 1)
    cols = rows_at(
        2 * HALF, (0, first), (BAND, first), (HALF, second), (HALF + BAND, second)
    )
    rows = np.concatenate([cos.T, sin.T], 1) / window
    return stacked(cols, 2), three(rows)


def toward(at, core, line, size):
    onward = lax.rem(core + line, 2) == 0
    other = jnp.where(onward, at + 1, at - 1)
    return onward, (other >= 0) & (other < size)


def dot(left, right):
    return jnp.dot(left, right, preferred_element_type=F32)


def split(value, count):
    out, rest = [], value
    for step in range(count):
        part = rest.astype(BF)
        out.append(part)
        if step + 1 < count:
            rest = rest - part.astype(F32)
    return out


def lane_ids(shape):
    return lax.broadcasted_iota(jnp.int32, shape, len(shape) - 1)


def doubled(value):
    high = value.astype(BF).astype(F32)
    part = jnp.where(lane_ids(value.shape) < HALF, high, value - high).astype(BF)
    return jnp.concatenate([part, part], 1)


def four_weights(ref):
    size = ref.shape[0] // 2
    high, low = ref[:size], ref[size:]
    return jnp.concatenate([high, high, low, low], 0)


def three_right(value):
    high, low = split(value, 2)
    return jnp.concatenate([high, low, high], 0)


def fetch(sources, targets, sems):
    copies = [
        pltpu.make_async_copy(source, target, sems.at[at])
        for at, (source, target) in enumerate(zip(sources, targets))
    ]
    for copy in copies:
        copy.start()
    return copies


def local_spectrum(tile_value, col_table, row_table):
    size = col_table.shape[0] // 2
    high, low = split(tile_value, 2)
    ch, cl = col_table[:size], col_table[size:]
    partial = dot(jnp.concatenate([high, low, high], 1), jnp.concatenate([ch, ch, cl], 0))
    both = dot(row_table, three_right(partial))
    top, bottom = both[: 3 * BAND], both[3 * BAND :]
    lane = lane_ids(top.shape) % HALF
    turned = jnp.where(
        lane < BAND,
        -pltpu.roll(bottom, top.shape[1] - BAND, 1),
        jnp.where(lane < 2 * BAND, pltpu.roll(bottom, BAND, 1), 0.0),
    )
    result = top + turned
    centre, first, last = (result[at * BAND : (at + 1) * BAND] for at in range(3))
    return jnp.concatenate([jnp.where(lane_ids(first.shape) < HALF, first, last), centre], 0)


def open_kernel(*refs):
    cond_hbm, dose_hbm, mask_hbm, kernels_hbm = refs[:4]
    cond_ref, dose_ref, mask_ref, sems = refs[-4:]
    count = (len(refs) - 11) // 2
    sources, targets = refs[4 : 4 + count], refs[7 + count : 7 + 2 * count]
    own_ref, chosen_ref, strength_ref = refs[4 + count : 7 + count]
    conds = cond_hbm.shape[0]
    copies = []

    def start(source, target):
        copy = pltpu.make_async_copy(source, target, sems.at[len(copies)])
        copy.start()
        copies.append(copy)
        return copy

    scalars = [start(cond_hbm, cond_ref), start(dose_hbm, dose_ref)]
    first = [start(mask_hbm, mask_ref)]
    first += [start(source, target) for source, target in zip(sources[:2], targets[:2])]
    for copy in scalars:
        copy.wait()
    rest = [start(kernels_hbm.at[cond_ref[c]], chosen_ref.at[c]) for c in range(conds)]
    rest += [start(source, target) for source, target in zip(sources[2:], targets[2:])]
    for c in range(conds):
        strength_ref[c] = jnp.full(strength_ref.shape[1:], dose_ref[cond_ref[c]], F32)
    for copy in first:
        copy.wait()
    col_ref, row_ref = targets[:2]
    own_ref[...] = local_spectrum(
        mask_ref[...], col_ref[: 2 * mask_ref.shape[0]], row_ref[...]
    )
    for copy in rest:
        copy.wait()


def near_kernel(mesh_shape, tile_ref, col_ref, row_ref, out_ref):
    row, col, core = (lax.axis_index(name) for name in AXES)
    right, valid = toward(col, core, row, mesh_shape[1])
    size = 2 * tile_ref.shape[0]
    at = pl.multiple_of(jnp.where(right, 2 * size, size), size)
    share = local_spectrum(tile_ref[...], col_ref[pl.ds(at, size)], row_ref[...])
    out_ref[...] = jnp.where(valid, share, 0.0)


def arrange_kernel(real_ref, imag_ref, first_ref, second_ref):
    total = real_ref.shape[0] // BAND
    for pair in range(total // 2):
        first, second = 0.0, 0.0
        for part in range(2):
            at = (2 * pair + part) * BAND
            pad = jnp.zeros((BAND, 2 * HALF - BAND), F32)
            real = jnp.concatenate([real_ref[at : at + BAND, :], pad], 1)
            imag = jnp.concatenate([imag_ref[at : at + BAND, :], pad], 1)

            def moved(value, by):
                return pltpu.roll(value, part * HALF + by, 1) if part * HALF + by else value

            first = first + (moved(real, 0) + moved(imag, BAND))
            second = second + (moved(real, BAND) - moved(imag, 0))
        first_ref[:, pair * 2 * HALF : (pair + 1) * 2 * HALF] = first
        second_ref[:, pair * 2 * HALF : (pair + 1) * 2 * HALF] = second


def field_kernel(
    mesh_shape, strength_ref, own_ref, near_ref, far_ref, side_ref, other_ref,
    first_ref, second_ref, target_ref, to_cols_ref, to_rows_ref, spread_cols_ref, spread_ref,
    gather_rows_ref, gather_cols_ref, from_rows_ref, from_cols_ref, out_ref, rows_ref, field_ref,
):
    conds = strength_ref.shape[0]
    count = 2 * BAND
    pairs = first_ref.shape[1] // (2 * HALF)
    per = 2 * pairs // conds
    tile = target_ref.shape[0]
    wide = 4 * HALF
    row, col, core = (lax.axis_index(name) for name in AXES)

    def half(value, core):
        onward, valid = toward(row, core, col, mesh_shape[0])
        low_half = lane_ids(value.shape) < HALF
        kept = jnp.where(onward, jnp.where(low_half, 0.0, value), jnp.where(low_half, value, 0.0))
        kept = jnp.where(valid, kept, 0.0)
        return kept + pltpu.roll(kept, HALF, 1)

    spectrum = own_ref[BAND:] + near_ref[BAND:] + far_ref[BAND:]
    spectrum += half(side_ref[...], core) + half(other_ref[...], 1 - core)
    lane = lane_ids(spectrum.shape) % HALF
    real = jnp.where(lane < BAND, spectrum, 0.0)
    imag = jnp.where(lane >= BAND, spectrum, 0.0)
    real = real + pltpu.roll(real, BAND, 1)
    imag = imag + pltpu.roll(imag, 2 * HALF - BAND, 1)

    to_rows = to_rows_ref[...]
    for quad in range(pairs // 2):
        blocks = []
        for pair in (2 * quad, 2 * quad + 1):
            one = first_ref[:, pair * 2 * HALF : (pair + 1) * 2 * HALF]
            two = second_ref[:, pair * 2 * HALF : (pair + 1) * 2 * HALF]
            blocks.append(jnp.concatenate([one * real + two * imag, one * imag - two * real], 0))
        both = dot(to_rows, three_right(jnp.concatenate(blocks, 1)))
        for part in range(2):
            at = (2 * quad + part) * count
            rows_ref[at : at + count, :] = both[:, part * 2 * HALF : (part + 1) * 2 * HALF]

    weights = four_weights(to_cols_ref)
    chunk = rows_ref.shape[0] // 2
    for at in (0, chunk):
        high, low = split(rows_ref[at : at + chunk, :], 2)
        field_ref[at : at + chunk, :] = dot(jnp.concatenate([high, low, high, low], 1), weights)
    sums = [jnp.zeros((count, 2 * HALF), F32) for _ in range(conds)]
    for pair in range(pairs):
        both = field_ref[pair * count : (pair + 1) * count, :]
        squares = both * both
        for part in range(2):
            c = (2 * pair + part) // per
            sums[c] = sums[c] + squares[:, part * 2 * HALF : (part + 1) * 2 * HALF]

    coarse = jnp.concatenate([value + pltpu.roll(value, HALF, 1) for value in sums], 0)
    lines = dot(doubled(coarse), four_weights(spread_cols_ref))
    right = jnp.concatenate(
        [three_right(lines[c * count : (c + 1) * count]) for c in range(conds)], 1
    )
    image = dot(spread_ref[...], right)

    goal = target_ref[...].astype(F32)
    norm = 1.0 / (per * BAND * BAND)
    slopes = []
    for c in range(conds):
        strength = strength_ref[c][:1]
        intensity = image[:, c * tile : (c + 1) * tile] * norm
        resist = jax.nn.sigmoid(STEEP * (strength * intensity - THRESH))
        slope = (resist - goal) * resist * (1.0 - resist)
        slopes.append(slope * (4.0 * STEEP * norm * strength))
    back = dot(gather_rows_ref[...], three_right(jnp.concatenate(slopes, 1)))
    high, low = split(
        jnp.concatenate([back[:, c * tile : (c + 1) * tile] for c in range(conds)], 0), 2
    )
    gh, gl = gather_cols_ref[:tile], gather_cols_ref[tile:]
    slope = dot(jnp.concatenate([high, low, high], 1), jnp.concatenate([gh, gh, gl], 0))

    for pair in range(pairs):
        weight = []
        for k in (2 * pair, 2 * pair + 1):
            weight.append(slope[k // per * count : (k // per + 1) * count])
        at = pair * count
        field_ref[at : at + count, :] = field_ref[at : at + count, :] * jnp.concatenate(weight, 1)
    weights = from_cols_ref[...]
    weights = jnp.concatenate(
        [
            weights,
            jnp.concatenate([weights[:, : 2 * HALF], jnp.zeros((wide, 2 * HALF), BF)], 1),
        ],
        0,
    )
    for at in (0, chunk):
        high, low = split(field_ref[at : at + chunk, :], 2)
        back = dot(jnp.concatenate([high, low], 1), weights)
        rows_ref[at : at + chunk, :] = back[:, : 2 * HALF] + back[:, 2 * HALF :]

    from_rows = from_rows_ref[...]
    sum_one, sum_two = 0.0, 0.0
    for quad in range(pairs // 2):
        at = 2 * quad * count
        value = jnp.concatenate(
            [rows_ref[at : at + count, :], rows_ref[at + count : at + 2 * count, :]], 1
        )
        back = dot(from_rows, three_right(value))
        top, bottom = back[:BAND], back[BAND:]
        one = first_ref[:, quad * wide : (quad + 1) * wide]
        two = second_ref[:, quad * wide : (quad + 1) * wide]
        sum_one = sum_one + (one * top + two * bottom)
        sum_two = sum_two + (two * top - one * bottom)
    sum_one = sum_one[:, : 2 * HALF] + sum_one[:, 2 * HALF :]
    sum_two = sum_two[:, : 2 * HALF] + sum_two[:, 2 * HALF :]
    out_ref[...] = jnp.where(
        lane_ids(sum_one.shape) < HALF,
        sum_one + pltpu.roll(sum_one, HALF, 1),
        sum_two + pltpu.roll(sum_two, HALF, 1),
    )


def adjoint_kernel(mine_ref, theirs_ref, cols_ref, rows_ref, out_hbm, out_ref, sems):
    tile = out_ref.shape[1]
    high, low = split(mine_ref[...] + theirs_ref[...], 2)
    size = cols_ref.shape[0] // 2
    ch, cl = cols_ref[:size], cols_ref[size:]
    halves = dot(jnp.concatenate([high, low, high], 1), jnp.concatenate([ch, ch, cl], 0))
    joined = three_right(jnp.concatenate([halves[:, :tile], halves[:, tile:]], 0))
    count = sems.shape[0]
    step = tile // count
    copies = []
    for at in range(count):
        rows = pl.ds(at * step, step)
        out_ref[rows] = dot(rows_ref[rows], joined)
        copies.append(pltpu.make_async_copy(out_ref.at[rows], out_hbm.at[rows], sems.at[at]))
        copies[-1].start()
    for copy in copies:
        copy.wait()


VMEM = pl.BlockSpec(memory_space=pltpu.VMEM)
SMEM = pl.BlockSpec(memory_space=pltpu.SMEM)
HBM = pl.BlockSpec(memory_space=pltpu.HBM)


def call(body, outs, specs, args, scratch=(), flops=1000000, grant=8, out_spec=None, flags=None):
    shapes = [
        shape if hasattr(shape, "dtype") else jax.ShapeDtypeStruct(shape, F32) for shape in outs
    ]
    one = len(outs) == 1
    args = [
        pltpu.with_memory_space_constraint(value, pltpu.HBM) if spec is HBM else value
        for spec, value in zip(specs, args)
    ]
    return pl.pallas_call(
        body,
        out_shape=shapes[0] if one else shapes,
        in_specs=specs,
        out_specs=(out_spec or VMEM) if one else [VMEM] * len(outs),
        scratch_shapes=list(scratch),
        compiler_params=pltpu.CompilerParams(vmem_limit_bytes=grant * 2**20, flags=flags),
        cost_estimate=pl.CostEstimate(flops=flops, bytes_accessed=1000000, transcendentals=0),
    )(*args)


def swaps(mesh_shape, along):
    rows, cols, cores = mesh_shape
    out = []
    for r in range(rows):
        for c in range(cols):
            for k in range(cores):
                at, line, size = (r, c, rows) if along == 0 else (c, r, cols)
                other = at + 1 if (k + line) % 2 == 0 else at - 1
                inside = 0 <= other < size
                at, line = (other, line) if inside else (at, line ^ 1)
                to = (at, line) if along == 0 else (line, at)
                if to[0] < rows and to[1] < cols:
                    out.append(((r * cols + c) * cores + k, (to[0] * cols + to[1]) * cores + 1 - k))
    return out


def shards(mesh_shape, mask, target, cond_index, kernels, dose):
    tile = mask.shape[0]
    window = tile + 2 * MARGIN
    swap = [(0, 1), (1, 0)]
    conds = cond_index.shape[0]
    count = kernels.shape[2]
    block = (2 * BAND, 2 * HALF)
    beside = lax.ppermute(mask, AXES, swaps(mesh_shape, 1))
    fetched = local_tables(tile, window) + (target,)
    fetched += field_tables(tile, window) + adjoint_tables(tile, window)
    own, chosen, strength, *fetched = call(
        open_kernel,
        [block, (conds, count, 2, BAND * BAND), (conds, 8, tile)]
        + [jax.ShapeDtypeStruct(value.shape, value.dtype) for value in fetched],
        [HBM] * (4 + len(fetched)),
        (cond_index, dose, mask, jnp.transpose(kernels, (0, 2, 1, 3))) + fetched,
        scratch=[
            pltpu.SMEM(cond_index.shape, jnp.int32),
            pltpu.SMEM(dose.shape, F32),
            pltpu.VMEM(mask.shape, F32),
            pltpu.SemaphoreType.DMA((3 + conds + len(fetched),)),
        ],
    )
    beside, own, chosen, strength, fetched = lax.optimization_barrier(
        (beside, own, chosen, strength, fetched)
    )
    col_table, row_table, *later = fetched
    near = call(
        functools.partial(near_kernel, mesh_shape), [block], [VMEM] * 3,
        (beside, col_table, row_table),
    )
    far = lax.ppermute(near, "cond", swap)
    real = chosen[:, :, 0].reshape(conds * count * BAND, BAND)
    imag = chosen[:, :, 1].reshape(conds * count * BAND, BAND)
    total = conds * count
    arranged = call(arrange_kernel, [(BAND, total * HALF)] * 2, [VMEM] * 2, (real, imag))
    far, arranged = lax.optimization_barrier((far, arranged))
    message = own[:BAND] + near[:BAND] + far[:BAND]
    side = lax.ppermute(message, AXES, swaps(mesh_shape, 0))
    other = lax.ppermute(side, "cond", swap)

    cotangent = call(
        functools.partial(field_kernel, mesh_shape),
        [(BAND, 2 * HALF)],
        [VMEM] * 17,
        (strength, own, near, far, side, other, *arranged, *later[:-2]),
        scratch=[
            pltpu.VMEM((total * BAND, 2 * HALF), F32),
            pltpu.VMEM((total * BAND, 4 * HALF), F32),
        ],
    )
    theirs = lax.ppermute(cotangent, "cond", swap)
    return call(
        adjoint_kernel, [(tile, tile)], [VMEM] * 4, (cotangent, theirs, *later[-2:]),
        scratch=[pltpu.VMEM((tile, tile), F32), pltpu.SemaphoreType.DMA((4,))], out_spec=HBM,
    )


def solution(mesh):
    in_specs = (P("row", "col"), P("row", "col"), P("cond"), P(), P())
    out_specs = P("row", "col")
    shape = tuple(mesh.shape[name] for name in AXES)
    body = functools.partial(shards, shape)
    return jax.shard_map(body, mesh=mesh, in_specs=in_specs, out_specs=out_specs, check_vma=False)
```

```python
import functools
import math

import jax
import jax.numpy as jnp
import numpy as np
from jax import lax
from jax.experimental import pallas as pl
from jax.experimental.pallas import tpu as pltpu
from jax.sharding import PartitionSpec as P

MARGIN = 128
BAND = 24
STEEP = 4.0
THRESH = 0.6

HALF = 64
AXES = ("row", "col", "cond")
BF = jnp.bfloat16
F32 = jnp.float32


def pieces(table, count):
    out, rest = [], np.asarray(table, np.float32)
    for _ in range(count):
        part = rest.astype(BF)
        out.append(part)
        rest = rest - part.astype(np.float32)
    return out


def angles(left, right, period):
    left, right = np.asarray(left, np.int64), np.asarray(right, np.int64)
    return (left[:, None] * right[None, :] % period) * (2.0 * math.pi / period)


def frequencies():
    return np.arange(BAND) - BAND // 2


def lanes(*blocks):
    rows = blocks[0][1].shape[0]
    width = -(-max(at + block.shape[1] for at, block in blocks) // 128) * 128
    out = np.zeros((rows, width))
    for at, block in blocks:
        out[:, at : at + block.shape[1]] = block
    return out


def rows_at(height, *blocks):
    out = np.zeros((height, blocks[0][1].shape[1]))
    for at, block in blocks:
        out[at : at + block.shape[0]] = block
    return out


def three(table):
    high, low = pieces(table, 2)
    return np.concatenate([high, high, low], 1)


def stacked(table, count):
    return np.concatenate(pieces(table, count), 0)


def local_tables(tile, window):
    places = np.arange(tile)
    col_table = []
    for shift in (MARGIN, 0, 2 * MARGIN):
        phase = angles(places + shift, frequencies(), window)
        block = np.concatenate([np.cos(phase), -np.sin(phase)], 1) / window
        col_table.append(stacked(lanes((0, block), (HALF, block)), 2))
    phase = angles(frequencies(), places + MARGIN, window)
    row_table = three(np.concatenate([np.cos(phase), -np.sin(phase)], 0))
    phase = angles(frequencies(), np.full(HALF, MARGIN), window)
    cos, sin = np.cos(phase), np.sin(phase)
    turn = np.concatenate([np.concatenate([cos, cos], 1), np.concatenate([sin, -sin], 1)], 0)
    return np.concatenate(col_table, 0), row_table, turn.astype(np.float32)


def field_tables(tile, window):
    count = 2 * BAND
    points = np.arange(count)
    phase = angles(frequencies(), points, count)
    cos, sin = np.cos(phase), np.sin(phase)
    one = np.concatenate(
        [lanes((0, cos), (HALF, sin)), lanes((0, -sin), (HALF, cos)), np.zeros((HALF - count, 2 * HALF))]
    )
    none = np.zeros_like(one)
    to_cols = np.concatenate(
        [np.concatenate([one, none], 1), np.concatenate([none, one], 1)], 0
    )
    to_rows = np.concatenate([cos.T, -sin.T], 1)
    where = (np.arange(tile)[:, None] + MARGIN) / window - points[None, :] / count
    spread = np.ones((tile, count))
    for order in range(1, BAND):
        spread += 2.0 * np.cos(2.0 * math.pi * order * where)
    spread /= count
    spread_cols = rows_at(HALF, (0, spread.T))
    gather_cols = lanes((0, spread), (HALF, spread))
    from_rows = np.concatenate([cos, sin], 0)
    return (
        stacked(to_cols, 2),
        three(to_rows),
        stacked(spread_cols, 2),
        three(spread),
        three(spread.T),
        stacked(gather_cols, 2),
        three(from_rows),
        np.concatenate(pieces(to_cols.T, 2), 1),
    )


def adjoint_tables(tile, window):
    places = np.arange(tile) + MARGIN
    phase = angles(frequencies(), places, window)
    cos, sin = np.cos(phase), np.sin(phase)
    first = np.concatenate([cos, -sin], 1)
    second = np.concatenate([-sin, -cos], 1)
    cols = rows_at(
        2 * HALF, (0, first), (BAND, first), (HALF, second), (HALF + BAND, second)
    )
    rows = np.concatenate([cos.T, sin.T], 1) / window
    return stacked(cols, 2), three(rows)


def toward(at, core, line, size):
    onward = lax.rem(core + line, 2) == 0
    other = jnp.where(onward, at + 1, at - 1)
    return onward, (other >= 0) & (other < size)


def dot(left, right):
    return jnp.dot(left, right, preferred_element_type=F32)


def split(value, count):
    out, rest = [], value
    for step in range(count):
        part = rest.astype(BF)
        out.append(part)
        if step + 1 < count:
            rest = rest - part.astype(F32)
    return out


def lane_ids(shape):
    return lax.broadcasted_iota(jnp.int32, shape, len(shape) - 1)


def doubled(value):
    high = value.astype(BF).astype(F32)
    part = jnp.where(lane_ids(value.shape) < HALF, high, value - high).astype(BF)
    return jnp.concatenate([part, part], 1)


def four_weights(ref):
    size = ref.shape[0] // 2
    high, low = ref[:size], ref[size:]
    return jnp.concatenate([high, high, low, low], 0)


def three_right(value):
    high, low = split(value, 2)
    return jnp.concatenate([high, low, high], 0)


def fetch(sources, targets, sems):
    copies = [
        pltpu.make_async_copy(source, target, sems.at[at])
        for at, (source, target) in enumerate(zip(sources, targets))
    ]
    for copy in copies:
        copy.start()
    return copies


def local_spectrum(tile_value, col_table, row_table, turn):
    size = col_table.shape[0] // 2
    high, low = split(tile_value, 2)
    ch, cl = col_table[:size], col_table[size:]
    partial = dot(jnp.concatenate([high, low, high], 1), jnp.concatenate([ch, ch, cl], 0))
    both = dot(row_table, three_right(partial))
    lane = lane_ids((BAND, both.shape[1])) % HALF

    def times_i(value):
        return jnp.where(
            lane < BAND,
            -pltpu.roll(value, value.shape[1] - BAND, 1),
            jnp.where(lane < 2 * BAND, pltpu.roll(value, BAND, 1), 0.0),
        )

    centre = both[:BAND] + times_i(both[BAND:])
    ends = turn[:BAND] * centre + turn[BAND:] * times_i(centre)
    return jnp.concatenate([ends, centre], 0)


def open_kernel(*refs):
    cond_hbm, dose_hbm, mask_hbm, kernels_hbm = refs[:4]
    cond_ref, dose_ref, mask_ref, sems = refs[-4:]
    count = (len(refs) - 11) // 2
    sources, targets = refs[4 : 4 + count], refs[7 + count : 7 + 2 * count]
    own_ref, chosen_ref, strength_ref = refs[4 + count : 7 + count]
    conds = cond_hbm.shape[0]
    copies = []

    def start(source, target):
        copy = pltpu.make_async_copy(source, target, sems.at[len(copies)])
        copy.start()
        copies.append(copy)
        return copy

    scalars = [start(cond_hbm, cond_ref), start(dose_hbm, dose_ref)]
    first = [start(mask_hbm, mask_ref)]
    first += [start(source, target) for source, target in zip(sources[:3], targets[:3])]
    for copy in scalars:
        copy.wait()
    rest = [start(kernels_hbm.at[cond_ref[c]], chosen_ref.at[c]) for c in range(conds)]
    rest += [start(source, target) for source, target in zip(sources[3:], targets[3:])]
    for c in range(conds):
        strength_ref[c] = jnp.full(strength_ref.shape[1:], dose_ref[cond_ref[c]], F32)
    for copy in first:
        copy.wait()
    col_ref, row_ref, turn_ref = targets[:3]
    own_ref[...] = local_spectrum(
        mask_ref[...], col_ref[: 2 * mask_ref.shape[0]], row_ref[...], turn_ref[...]
    )
    for copy in rest:
        copy.wait()


def near_kernel(mesh_shape, tile_ref, col_ref, row_ref, turn_ref, out_ref):
    row, col, core = (lax.axis_index(name) for name in AXES)
    right, valid = toward(col, core, row, mesh_shape[1])
    size = 2 * tile_ref.shape[0]
    at = pl.multiple_of(jnp.where(right, 2 * size, size), size)
    share = local_spectrum(tile_ref[...], col_ref[pl.ds(at, size)], row_ref[...], turn_ref[...])
    out_ref[...] = jnp.where(valid, share, 0.0)


def arrange_kernel(real_ref, imag_ref, first_ref, second_ref):
    total = real_ref.shape[0] // BAND
    for pair in range(total // 2):
        first, second = 0.0, 0.0
        for part in range(2):
            at = (2 * pair + part) * BAND
            pad = jnp.zeros((BAND, 2 * HALF - BAND), F32)
            real = jnp.concatenate([real_ref[at : at + BAND, :], pad], 1)
            imag = jnp.concatenate([imag_ref[at : at + BAND, :], pad], 1)

            def moved(value, by):
                return pltpu.roll(value, part * HALF + by, 1) if part * HALF + by else value

            first = first + (moved(real, 0) + moved(imag, BAND))
            second = second + (moved(real, BAND) - moved(imag, 0))
        first_ref[:, pair * 2 * HALF : (pair + 1) * 2 * HALF] = first
        second_ref[:, pair * 2 * HALF : (pair + 1) * 2 * HALF] = second


def field_kernel(
    mesh_shape, strength_ref, own_ref, near_ref, far_ref, side_ref, other_ref,
    first_ref, second_ref, target_ref, to_cols_ref, to_rows_ref, spread_cols_ref, spread_ref,
    gather_rows_ref, gather_cols_ref, from_rows_ref, from_cols_ref, out_ref, rows_ref, field_ref,
):
    conds = strength_ref.shape[0]
    count = 2 * BAND
    pairs = first_ref.shape[1] // (2 * HALF)
    per = 2 * pairs // conds
    tile = target_ref.shape[0]
    wide = 4 * HALF
    row, col, core = (lax.axis_index(name) for name in AXES)

    def half(value, core):
        onward, valid = toward(row, core, col, mesh_shape[0])
        low_half = lane_ids(value.shape) < HALF
        kept = jnp.where(onward, jnp.where(low_half, 0.0, value), jnp.where(low_half, value, 0.0))
        kept = jnp.where(valid, kept, 0.0)
        return kept + pltpu.roll(kept, HALF, 1)

    spectrum = own_ref[BAND:] + near_ref[BAND:] + far_ref[BAND:]
    spectrum += half(side_ref[...], core) + half(other_ref[...], 1 - core)
    lane = lane_ids(spectrum.shape) % HALF
    real = jnp.where(lane < BAND, spectrum, 0.0)
    imag = jnp.where(lane >= BAND, spectrum, 0.0)
    real = real + pltpu.roll(real, BAND, 1)
    imag = imag + pltpu.roll(imag, 2 * HALF - BAND, 1)

    to_rows = to_rows_ref[...]
    for quad in range(pairs // 2):
        blocks = []
        for pair in (2 * quad, 2 * quad + 1):
            one = first_ref[:, pair * 2 * HALF : (pair + 1) * 2 * HALF]
            two = second_ref[:, pair * 2 * HALF : (pair + 1) * 2 * HALF]
            blocks.append(jnp.concatenate([one * real + two * imag, one * imag - two * real], 0))
        both = dot(to_rows, three_right(jnp.concatenate(blocks, 1)))
        for part in range(2):
            at = (2 * quad + part) * count
            rows_ref[at : at + count, :] = both[:, part * 2 * HALF : (part + 1) * 2 * HALF]

    weights = four_weights(to_cols_ref)
    chunk = rows_ref.shape[0] // 2
    for at in (0, chunk):
        high, low = split(rows_ref[at : at + chunk, :], 2)
        field_ref[at : at + chunk, :] = dot(jnp.concatenate([high, low, high, low], 1), weights)
    sums = [jnp.zeros((count, 2 * HALF), F32) for _ in range(conds)]
    for pair in range(pairs):
        both = field_ref[pair * count : (pair + 1) * count, :]
        squares = both * both
        for part in range(2):
            c = (2 * pair + part) // per
            sums[c] = sums[c] + squares[:, part * 2 * HALF : (part + 1) * 2 * HALF]

    coarse = jnp.concatenate([value + pltpu.roll(value, HALF, 1) for value in sums], 0)
    lines = dot(doubled(coarse), four_weights(spread_cols_ref))
    right = jnp.concatenate(
        [three_right(lines[c * count : (c + 1) * count]) for c in range(conds)], 1
    )
    image = dot(spread_ref[...], right)

    goal = target_ref[...].astype(F32)
    norm = 1.0 / (per * BAND * BAND)
    slopes = []
    for c in range(conds):
        strength = strength_ref[c][:1]
        intensity = image[:, c * tile : (c + 1) * tile] * norm
        resist = jax.nn.sigmoid(STEEP * (strength * intensity - THRESH))
        slope = (resist - goal) * resist * (1.0 - resist)
        slopes.append(slope * (4.0 * STEEP * norm * strength))
    back = dot(gather_rows_ref[...], three_right(jnp.concatenate(slopes, 1)))
    high, low = split(
        jnp.concatenate([back[:, c * tile : (c + 1) * tile] for c in range(conds)], 0), 2
    )
    gh, gl = gather_cols_ref[:tile], gather_cols_ref[tile:]
    slope = dot(jnp.concatenate([high, low, high], 1), jnp.concatenate([gh, gh, gl], 0))

    for pair in range(pairs):
        weight = []
        for k in (2 * pair, 2 * pair + 1):
            weight.append(slope[k // per * count : (k // per + 1) * count])
        at = pair * count
        field_ref[at : at + count, :] = field_ref[at : at + count, :] * jnp.concatenate(weight, 1)
    weights = from_cols_ref[...]
    weights = jnp.concatenate(
        [
            weights,
            jnp.concatenate([weights[:, : 2 * HALF], jnp.zeros((wide, 2 * HALF), BF)], 1),
        ],
        0,
    )
    for at in (0, chunk):
        high, low = split(field_ref[at : at + chunk, :], 2)
        back = dot(jnp.concatenate([high, low], 1), weights)
        rows_ref[at : at + chunk, :] = back[:, : 2 * HALF] + back[:, 2 * HALF :]

    from_rows = from_rows_ref[...]
    sum_one, sum_two = 0.0, 0.0
    for quad in range(pairs // 2):
        at = 2 * quad * count
        value = jnp.concatenate(
            [rows_ref[at : at + count, :], rows_ref[at + count : at + 2 * count, :]], 1
        )
        back = dot(from_rows, three_right(value))
        top, bottom = back[:BAND], back[BAND:]
        one = first_ref[:, quad * wide : (quad + 1) * wide]
        two = second_ref[:, quad * wide : (quad + 1) * wide]
        sum_one = sum_one + (one * top + two * bottom)
        sum_two = sum_two + (two * top - one * bottom)
    sum_one = sum_one[:, : 2 * HALF] + sum_one[:, 2 * HALF :]
    sum_two = sum_two[:, : 2 * HALF] + sum_two[:, 2 * HALF :]
    out_ref[...] = jnp.where(
        lane_ids(sum_one.shape) < HALF,
        sum_one + pltpu.roll(sum_one, HALF, 1),
        sum_two + pltpu.roll(sum_two, HALF, 1),
    )


def adjoint_kernel(mine_ref, theirs_ref, cols_ref, rows_ref, out_hbm, out_ref, sems):
    tile = out_ref.shape[1]
    high, low = split(mine_ref[...] + theirs_ref[...], 2)
    size = cols_ref.shape[0] // 2
    ch, cl = cols_ref[:size], cols_ref[size:]
    halves = dot(jnp.concatenate([high, low, high], 1), jnp.concatenate([ch, ch, cl], 0))
    joined = three_right(jnp.concatenate([halves[:, :tile], halves[:, tile:]], 0))
    count = sems.shape[0]
    step = tile // count
    copies = []
    for at in range(count):
        rows = pl.ds(at * step, step)
        out_ref[rows] = dot(rows_ref[rows], joined)
        copies.append(pltpu.make_async_copy(out_ref.at[rows], out_hbm.at[rows], sems.at[at]))
        copies[-1].start()
    for copy in copies:
        copy.wait()


VMEM = pl.BlockSpec(memory_space=pltpu.VMEM)
SMEM = pl.BlockSpec(memory_space=pltpu.SMEM)
HBM = pl.BlockSpec(memory_space=pltpu.HBM)


def call(body, outs, specs, args, scratch=(), flops=1000000, grant=8, out_spec=None):
    shapes = [
        shape if hasattr(shape, "dtype") else jax.ShapeDtypeStruct(shape, F32) for shape in outs
    ]
    one = len(outs) == 1
    args = [
        pltpu.with_memory_space_constraint(value, pltpu.HBM) if spec is HBM else value
        for spec, value in zip(specs, args)
    ]
    return pl.pallas_call(
        body,
        out_shape=shapes[0] if one else shapes,
        in_specs=specs,
        out_specs=(out_spec or VMEM) if one else [VMEM] * len(outs),
        scratch_shapes=list(scratch),
        compiler_params=pltpu.CompilerParams(vmem_limit_bytes=grant * 2**20),
        cost_estimate=pl.CostEstimate(flops=flops, bytes_accessed=1000000, transcendentals=0),
    )(*args)


def swaps(mesh_shape, along):
    rows, cols, cores = mesh_shape
    out = []
    for r in range(rows):
        for c in range(cols):
            for k in range(cores):
                at, line, size = (r, c, rows) if along == 0 else (c, r, cols)
                other = at + 1 if (k + line) % 2 == 0 else at - 1
                inside = 0 <= other < size
                at, line = (other, line) if inside else (at, line ^ 1)
                to = (at, line) if along == 0 else (line, at)
                if to[0] < rows and to[1] < cols:
                    out.append(((r * cols + c) * cores + k, (to[0] * cols + to[1]) * cores + 1 - k))
    return out


def shards(mesh_shape, mask, target, cond_index, kernels, dose):
    tile = mask.shape[0]
    window = tile + 2 * MARGIN
    swap = [(0, 1), (1, 0)]
    conds = cond_index.shape[0]
    count = kernels.shape[2]
    block = (2 * BAND, 2 * HALF)
    beside = lax.ppermute(mask, AXES, swaps(mesh_shape, 1))
    fetched = local_tables(tile, window) + (target,)
    fetched += field_tables(tile, window) + adjoint_tables(tile, window)
    own, chosen, strength, *fetched = call(
        open_kernel,
        [block, (conds, count, 2, BAND * BAND), (conds, 8, tile)]
        + [jax.ShapeDtypeStruct(value.shape, value.dtype) for value in fetched],
        [HBM] * (4 + len(fetched)),
        (cond_index, dose, mask, jnp.transpose(kernels, (0, 2, 1, 3))) + fetched,
        scratch=[
            pltpu.SMEM(cond_index.shape, jnp.int32),
            pltpu.SMEM(dose.shape, F32),
            pltpu.VMEM(mask.shape, F32),
            pltpu.SemaphoreType.DMA((3 + conds + len(fetched),)),
        ],
    )
    beside, own, chosen, strength, fetched = lax.optimization_barrier(
        (beside, own, chosen, strength, fetched)
    )
    *local, later_target = fetched[:4]
    later = [later_target, *fetched[4:]]
    near = call(
        functools.partial(near_kernel, mesh_shape), [block], [VMEM] * 4, (beside, *local)
    )
    far = lax.ppermute(near, "cond", swap)
    real = chosen[:, :, 0].reshape(conds * count * BAND, BAND)
    imag = chosen[:, :, 1].reshape(conds * count * BAND, BAND)
    far, real, imag = lax.optimization_barrier((far, real, imag))
    message = own[:BAND] + near[:BAND] + far[:BAND]
    side = lax.ppermute(message, AXES, swaps(mesh_shape, 0))
    total = conds * count
    arranged = call(arrange_kernel, [(BAND, total * HALF)] * 2, [VMEM] * 2, (real, imag))
    side, arranged = lax.optimization_barrier((side, arranged))
    other = lax.ppermute(side, "cond", swap)

    cotangent = call(
        functools.partial(field_kernel, mesh_shape),
        [(BAND, 2 * HALF)],
        [VMEM] * 17,
        (strength, own, near, far, side, other, *arranged, *later[:-2]),
        scratch=[
            pltpu.VMEM((total * BAND, 2 * HALF), F32),
            pltpu.VMEM((total * BAND, 4 * HALF), F32),
        ],
    )
    theirs = lax.ppermute(cotangent, "cond", swap)
    return call(
        adjoint_kernel, [(tile, tile)], [VMEM] * 4, (cotangent, theirs, *later[-2:]),
        scratch=[pltpu.VMEM((tile, tile), F32), pltpu.SemaphoreType.DMA((4,))], out_spec=HBM,
    )


def solution(mesh):
    in_specs = (P("row", "col"), P("row", "col"), P("cond"), P(), P())
    out_specs = P("row", "col")
    shape = tuple(mesh.shape[name] for name in AXES)
    body = functools.partial(shards, shape)
    return jax.shard_map(body, mesh=mesh, in_specs=in_specs, out_specs=out_specs, check_vma=False)
```

```python
import functools
import math
from itertools import zip_longest

import jax
import jax.numpy as jnp
import numpy as np
from jax import lax
from jax.experimental import pallas as pl
from jax.experimental.pallas import tpu as pltpu
from jax.sharding import PartitionSpec as P

MARGIN = 128
BAND = 24
STEEP = 4.0
THRESH = 0.6

HALF = 64
AXES = ("row", "col", "cond")
BF = jnp.bfloat16
F32 = jnp.float32


def pieces(table, count):
    out, rest = [], np.asarray(table, np.float32)
    for _ in range(count):
        part = rest.astype(BF)
        out.append(part)
        rest = rest - part.astype(np.float32)
    return out


def angles(left, right, period):
    left, right = np.asarray(left, np.int64), np.asarray(right, np.int64)
    return (left[:, None] * right[None, :] % period) * (2.0 * math.pi / period)


def frequencies():
    return np.arange(BAND) - BAND // 2


def lanes(*blocks):
    rows = blocks[0][1].shape[0]
    width = -(-max(at + block.shape[1] for at, block in blocks) // 128) * 128
    out = np.zeros((rows, width))
    for at, block in blocks:
        out[:, at : at + block.shape[1]] = block
    return out


def rows_at(height, *blocks):
    out = np.zeros((height, blocks[0][1].shape[1]))
    for at, block in blocks:
        out[at : at + block.shape[0]] = block
    return out


def three(table):
    high, low = pieces(table, 2)
    return np.concatenate([high, high, low], 1)


def stacked(table, count):
    return np.concatenate(pieces(table, count), 0)


def local_tables(tile, window):
    places = np.arange(tile)
    col_table = []
    for shift in (MARGIN, 0, 2 * MARGIN):
        phase = angles(places + shift, frequencies(), window)
        block = np.concatenate([np.cos(phase), -np.sin(phase)], 1) / window
        col_table.append(stacked(lanes((0, block), (HALF, block)), 2))
    phase = angles(frequencies(), places + MARGIN, window)
    row_table = three(np.concatenate([np.cos(phase), -np.sin(phase)], 0))
    phase = angles(frequencies(), np.full(HALF, MARGIN), window)
    cos, sin = np.cos(phase), np.sin(phase)
    turn = np.concatenate([np.concatenate([cos, cos], 1), np.concatenate([sin, -sin], 1)], 0)
    return np.concatenate(col_table, 0), row_table, turn.astype(np.float32)


def field_tables(tile, window):
    count = 2 * BAND
    points = np.arange(count)
    phase = angles(frequencies(), points, count)
    cos, sin = np.cos(phase), np.sin(phase)
    one = np.concatenate(
        [lanes((0, cos), (HALF, sin)), lanes((0, -sin), (HALF, cos)), np.zeros((HALF - count, 2 * HALF))]
    )
    none = np.zeros_like(one)
    to_cols = np.concatenate(
        [np.concatenate([one, none], 1), np.concatenate([none, one], 1)], 0
    )
    to_rows = np.concatenate([cos.T, -sin.T], 1)
    where = (np.arange(tile)[:, None] + MARGIN) / window - points[None, :] / count
    spread = np.ones((tile, count))
    for order in range(1, BAND):
        spread += 2.0 * np.cos(2.0 * math.pi * order * where)
    spread /= count
    spread_cols = rows_at(HALF, (0, spread.T))
    gather_cols = lanes((0, spread), (HALF, spread))
    from_rows = np.concatenate([cos, sin], 0)
    return (
        stacked(to_cols, 2),
        three(to_rows),
        stacked(spread_cols, 2),
        three(spread),
        three(spread.T),
        stacked(gather_cols, 2),
        three(from_rows),
        np.concatenate(pieces(to_cols.T, 2), 1),
    )


def adjoint_tables(tile, window):
    places = np.arange(tile) + MARGIN
    phase = angles(frequencies(), places, window)
    cos, sin = np.cos(phase), np.sin(phase)
    first = np.concatenate([cos, -sin], 1)
    second = np.concatenate([-sin, -cos], 1)
    cols = rows_at(
        2 * HALF, (0, first), (BAND, first), (HALF, second), (HALF + BAND, second)
    )
    rows = np.concatenate([cos.T, sin.T], 1) / window
    return stacked(cols, 2), three(rows)


def toward(at, core, line, size):
    onward = lax.rem(core + line, 2) == 0
    other = jnp.where(onward, at + 1, at - 1)
    return onward, (other >= 0) & (other < size)


def dot(left, right):
    return jnp.dot(left, right, preferred_element_type=F32)


def split(value, count):
    out, rest = [], value
    for step in range(count):
        part = rest.astype(BF)
        out.append(part)
        if step + 1 < count:
            rest = rest - part.astype(F32)
    return out


def lane_ids(shape):
    return lax.broadcasted_iota(jnp.int32, shape, len(shape) - 1)


def doubled(value):
    high = value.astype(BF).astype(F32)
    part = jnp.where(lane_ids(value.shape) < HALF, high, value - high).astype(BF)
    return jnp.concatenate([part, part], 1)


def four_weights(ref):
    size = ref.shape[0] // 2
    high, low = ref[:size], ref[size:]
    return jnp.concatenate([high, high, low, low], 0)


def three_right(value):
    high, low = split(value, 2)
    return jnp.concatenate([high, low, high], 0)


def fetch(sources, targets, sems):
    copies = [
        pltpu.make_async_copy(source, target, sems.at[at])
        for at, (source, target) in enumerate(zip(sources, targets))
    ]
    for copy in copies:
        copy.start()
    return copies


def local_spectrum(tile_value, col_table, row_table, turn):
    size = col_table.shape[0] // 2
    high, low = split(tile_value, 2)
    ch, cl = col_table[:size], col_table[size:]
    partial = dot(jnp.concatenate([high, low], 1), jnp.concatenate([ch, ch], 0)) + dot(high, cl)
    both = dot(row_table, three_right(partial))
    lane = lane_ids((BAND, both.shape[1])) % HALF

    def times_i(value):
        return jnp.where(
            lane < BAND,
            -pltpu.roll(value, value.shape[1] - BAND, 1),
            jnp.where(lane < 2 * BAND, pltpu.roll(value, BAND, 1), 0.0),
        )

    centre = both[:BAND] + times_i(both[BAND:])
    ends = turn[:BAND] * centre + turn[BAND:] * times_i(centre)
    return jnp.concatenate([ends, centre], 0)


def open_kernel(*refs):
    cond_hbm, dose_hbm, mask_hbm, kernels_hbm = refs[:4]
    cond_ref, dose_ref, mask_ref, sems = refs[-4:]
    count = (len(refs) - 11) // 2
    sources, targets = refs[4 : 4 + count], refs[7 + count : 7 + 2 * count]
    own_ref, chosen_ref, strength_ref = refs[4 + count : 7 + count]
    conds = cond_hbm.shape[0]
    copies = []

    def start(source, target):
        copy = pltpu.make_async_copy(source, target, sems.at[len(copies)])
        copy.start()
        copies.append(copy)
        return copy

    scalars = [start(cond_hbm, cond_ref), start(dose_hbm, dose_ref)]
    first = [start(mask_hbm, mask_ref)]
    first += [start(source, target) for source, target in zip(sources[:3], targets[:3])]
    for copy in scalars:
        copy.wait()
    rest = [start(kernels_hbm.at[cond_ref[c]], chosen_ref.at[c]) for c in range(conds)]
    rest += [start(source, target) for source, target in zip(sources[3:], targets[3:])]
    for c in range(conds):
        strength_ref[c] = jnp.full(strength_ref.shape[1:], dose_ref[cond_ref[c]], F32)
    for copy in first:
        copy.wait()
    col_ref, row_ref, turn_ref = targets[:3]
    own_ref[...] = local_spectrum(
        mask_ref[...], col_ref[: 2 * mask_ref.shape[0]], row_ref[...], turn_ref[...]
    )
    for copy in rest:
        copy.wait()


def near_kernel(mesh_shape, tile_ref, col_ref, row_ref, turn_ref, out_ref):
    row, col, core = (lax.axis_index(name) for name in AXES)
    right, valid = toward(col, core, row, mesh_shape[1])
    size = 2 * tile_ref.shape[0]
    at = pl.multiple_of(jnp.where(right, 2 * size, size), size)
    share = local_spectrum(tile_ref[...], col_ref[pl.ds(at, size)], row_ref[...], turn_ref[...])
    out_ref[...] = jnp.where(valid, share, 0.0)


def arrange_kernel(real_ref, imag_ref, first_ref, second_ref):
    total = real_ref.shape[0] // BAND
    for pair in range(total // 2):
        first, second = 0.0, 0.0
        for part in range(2):
            at = (2 * pair + part) * BAND
            pad = jnp.zeros((BAND, 2 * HALF - BAND), F32)
            real = jnp.concatenate([real_ref[at : at + BAND, :], pad], 1)
            imag = jnp.concatenate([imag_ref[at : at + BAND, :], pad], 1)

            def moved(value, by):
                return pltpu.roll(value, part * HALF + by, 1) if part * HALF + by else value

            first = first + (moved(real, 0) + moved(imag, BAND))
            second = second + (moved(real, BAND) - moved(imag, 0))
        first_ref[:, pair * 2 * HALF : (pair + 1) * 2 * HALF] = first
        second_ref[:, pair * 2 * HALF : (pair + 1) * 2 * HALF] = second


def field_kernel(
    mesh_shape, strength_ref, own_ref, near_ref, far_ref, side_ref, other_ref,
    first_ref, second_ref, target_ref, to_cols_ref, to_rows_ref, spread_cols_ref, spread_ref,
    gather_rows_ref, gather_cols_ref, from_rows_ref, from_cols_ref, out_ref, rows_ref, field_ref,
):
    conds = strength_ref.shape[0]
    count = 2 * BAND
    per = first_ref.shape[1] // HALF // conds
    tile = target_ref.shape[0]
    wide = 4 * HALF
    row, col, core = (lax.axis_index(name) for name in AXES)

    def half(value, core):
        onward, valid = toward(row, core, col, mesh_shape[0])
        low_half = lane_ids(value.shape) < HALF
        kept = jnp.where(onward, jnp.where(low_half, 0.0, value), jnp.where(low_half, value, 0.0))
        kept = jnp.where(valid, kept, 0.0)
        return kept + pltpu.roll(kept, HALF, 1)

    spectrum = own_ref[BAND:] + near_ref[BAND:] + far_ref[BAND:]
    spectrum += half(side_ref[...], core) + half(other_ref[...], 1 - core)
    lane = lane_ids(spectrum.shape) % HALF
    real = jnp.where(lane < BAND, spectrum, 0.0)
    imag = jnp.where(lane >= BAND, spectrum, 0.0)
    real = real + pltpu.roll(real, BAND, 1)
    imag = imag + pltpu.roll(imag, 2 * HALF - BAND, 1)

    to_rows = to_rows_ref[...]
    to_cols = four_weights(to_cols_ref)
    spread_cols = four_weights(spread_cols_ref)
    gather_cols = gather_cols_ref[...]
    gather_cols = jnp.concatenate([gather_cols[:tile], gather_cols], 0)
    from_cols = from_cols_ref[...]
    from_cols = jnp.concatenate(
        [
            from_cols,
            jnp.concatenate([from_cols[:, : 2 * HALF], jnp.zeros((wide, 2 * HALF), BF)], 1),
        ],
        0,
    )
    from_rows = from_rows_ref[...]
    goal = target_ref[...].astype(F32)
    norm = 1.0 / (per * BAND * BAND)
    pairs = per // 2

    def pair_lanes(ref, pair, width=1):
        return ref[:, pair * 2 * HALF : (pair + width) * 2 * HALF]

    def condition(c, sums):
        first, last = c * pairs, (c + 1) * pairs
        for quad in range(first, last, 2):
            blocks = []
            for pair in (quad, quad + 1):
                one, two = pair_lanes(first_ref, pair), pair_lanes(second_ref, pair)
                blocks.append(
                    jnp.concatenate([one * real + two * imag, one * imag - two * real], 0)
                )
            both = dot(to_rows, three_right(jnp.concatenate(blocks, 1)))
            rows_ref[quad * count : (quad + 1) * count, :] = both[:, : 2 * HALF]
            rows_ref[(quad + 1) * count : (quad + 2) * count, :] = both[:, 2 * HALF :]
            yield
        total = 0.0
        rows = slice(first * count, last * count)
        high, low = split(rows_ref[rows, :], 2)
        field_ref[rows, :] = dot(jnp.concatenate([high, low, high, low], 1), to_cols)
        for pair in range(first, last):
            both = field_ref[pair * count : (pair + 1) * count, :]
            squares = both * both
            total = total + (squares[:, : 2 * HALF] + squares[:, 2 * HALF :])
        yield
        coarse = total + pltpu.roll(total, HALF, 1)
        lines = dot(doubled(coarse), spread_cols)
        yield
        intensity = dot(spread_ref[...], three_right(lines)) * norm
        strength = strength_ref[c][:1]
        resist = jax.nn.sigmoid(STEEP * (strength * intensity - THRESH))
        slope = (resist - goal) * resist * (1.0 - resist)
        slope = slope * (4.0 * STEEP * norm * strength)
        yield
        back = dot(gather_rows_ref[...], three_right(slope))
        yield
        high, low = split(back, 2)
        slope = dot(jnp.concatenate([high, low, high], 1), gather_cols)
        slope = jnp.concatenate([slope, slope], 1)
        yield
        for pair in range(first, last):
            part = slice(pair * count, (pair + 1) * count)
            field_ref[part, :] = field_ref[part, :] * slope
        back = dot(jnp.concatenate(split(field_ref[rows, :], 2), 1), from_cols)
        rows_ref[rows, :] = back[:, : 2 * HALF] + back[:, 2 * HALF :]
        yield
        for quad in range(first, last, 2):
            value = jnp.concatenate(
                [
                    rows_ref[quad * count : (quad + 1) * count, :],
                    rows_ref[(quad + 1) * count : (quad + 2) * count, :],
                ],
                1,
            )
            back = dot(from_rows, three_right(value))
            top, bottom = back[:BAND], back[BAND:]
            one, two = pair_lanes(first_ref, quad, 2), pair_lanes(second_ref, quad, 2)
            sums[0] = sums[0] + (one * top + two * bottom)
            sums[1] = sums[1] + (two * top - one * bottom)
            yield

    sums = [0.0, 0.0]
    for _ in zip_longest(*(condition(c, sums) for c in range(conds))):
        pass
    sum_one, sum_two = (value[:, : 2 * HALF] + value[:, 2 * HALF :] for value in sums)
    out_ref[...] = jnp.where(
        lane_ids(sum_one.shape) < HALF,
        sum_one + pltpu.roll(sum_one, HALF, 1),
        sum_two + pltpu.roll(sum_two, HALF, 1),
    )


def adjoint_kernel(mine_ref, theirs_ref, cols_ref, rows_ref, out_ref):
    tile = out_ref.shape[1]
    high, low = split(mine_ref[...] + theirs_ref[...], 2)
    size = cols_ref.shape[0] // 2
    ch, cl = cols_ref[:size], cols_ref[size:]
    halves = dot(jnp.concatenate([high, low, high], 1), jnp.concatenate([ch, ch, cl], 0))
    joined = jnp.concatenate([halves[:, :tile], halves[:, tile:]], 0)
    out_ref[...] = dot(rows_ref[...], three_right(joined))


VMEM = pl.BlockSpec(memory_space=pltpu.VMEM)
SMEM = pl.BlockSpec(memory_space=pltpu.SMEM)
HBM = pl.BlockSpec(memory_space=pltpu.HBM)


def call(body, outs, specs, args, scratch=(), flops=1000000, grant=8):
    shapes = [
        shape if hasattr(shape, "dtype") else jax.ShapeDtypeStruct(shape, F32) for shape in outs
    ]
    one = len(outs) == 1
    args = [
        pltpu.with_memory_space_constraint(value, pltpu.HBM) if spec is HBM else value
        for spec, value in zip(specs, args)
    ]
    return pl.pallas_call(
        body,
        out_shape=shapes[0] if one else shapes,
        in_specs=specs,
        out_specs=VMEM if one else [VMEM] * len(outs),
        scratch_shapes=list(scratch),
        compiler_params=pltpu.CompilerParams(vmem_limit_bytes=grant * 2**20),
        cost_estimate=pl.CostEstimate(flops=flops, bytes_accessed=1000000, transcendentals=0),
    )(*args)


def swaps(mesh_shape, along):
    rows, cols, cores = mesh_shape
    out = []
    for r in range(rows):
        for c in range(cols):
            for k in range(cores):
                at, line, size = (r, c, rows) if along == 0 else (c, r, cols)
                other = at + 1 if (k + line) % 2 == 0 else at - 1
                inside = 0 <= other < size
                at, line = (other, line) if inside else (at, line ^ 1)
                to = (at, line) if along == 0 else (line, at)
                if to[0] < rows and to[1] < cols:
                    out.append(((r * cols + c) * cores + k, (to[0] * cols + to[1]) * cores + 1 - k))
    return out


def shards(mesh_shape, mask, target, cond_index, kernels, dose):
    tile = mask.shape[0]
    window = tile + 2 * MARGIN
    swap = [(0, 1), (1, 0)]
    conds = cond_index.shape[0]
    count = kernels.shape[2]
    block = (2 * BAND, 2 * HALF)
    beside = lax.ppermute(mask, AXES, swaps(mesh_shape, 1))
    fetched = local_tables(tile, window) + (target,)
    fetched += field_tables(tile, window) + adjoint_tables(tile, window)
    own, chosen, strength, *fetched = call(
        open_kernel,
        [block, (conds, count, 2, BAND * BAND), (conds, 8, tile)]
        + [jax.ShapeDtypeStruct(value.shape, value.dtype) for value in fetched],
        [HBM] * (4 + len(fetched)),
        (cond_index, dose, mask, jnp.transpose(kernels, (0, 2, 1, 3))) + fetched,
        scratch=[
            pltpu.SMEM(cond_index.shape, jnp.int32),
            pltpu.SMEM(dose.shape, F32),
            pltpu.VMEM(mask.shape, F32),
            pltpu.SemaphoreType.DMA((3 + conds + len(fetched),)),
        ],
    )
    beside, own, chosen, strength, fetched = lax.optimization_barrier(
        (beside, own, chosen, strength, fetched)
    )
    *local, later_target = fetched[:4]
    later = [later_target, *fetched[4:]]
    near = call(
        functools.partial(near_kernel, mesh_shape), [block], [VMEM] * 4, (beside, *local)
    )
    far = lax.ppermute(near, "cond", swap)
    real = chosen[:, :, 0].reshape(conds * count * BAND, BAND)
    imag = chosen[:, :, 1].reshape(conds * count * BAND, BAND)
    far, real, imag = lax.optimization_barrier((far, real, imag))
    message = own[:BAND] + near[:BAND] + far[:BAND]
    side = lax.ppermute(message, AXES, swaps(mesh_shape, 0))
    total = conds * count
    arranged = call(arrange_kernel, [(BAND, total * HALF)] * 2, [VMEM] * 2, (real, imag))
    side, arranged = lax.optimization_barrier((side, arranged))
    other = lax.ppermute(side, "cond", swap)

    cotangent = call(
        functools.partial(field_kernel, mesh_shape),
        [(BAND, 2 * HALF)],
        [VMEM] * 17,
        (strength, own, near, far, side, other, *arranged, *later[:-2]),
        scratch=[
            pltpu.VMEM((total * BAND, 2 * HALF), F32),
            pltpu.VMEM((total * BAND, 4 * HALF), F32),
        ],
    )
    theirs = lax.ppermute(cotangent, "cond", swap)
    return call(
        adjoint_kernel, [(tile, tile)], [VMEM] * 4, (cotangent, theirs, *later[-2:])
    )


def solution(mesh):
    in_specs = (P("row", "col"), P("row", "col"), P("cond"), P(), P())
    out_specs = P("row", "col")
    shape = tuple(mesh.shape[name] for name in AXES)
    body = functools.partial(shards, shape)
    return jax.shard_map(body, mesh=mesh, in_specs=in_specs, out_specs=out_specs, check_vma=False)
```

```python
import functools
import math
from itertools import zip_longest

import jax
import jax.numpy as jnp
import numpy as np
from jax import lax
from jax.experimental import pallas as pl
from jax.experimental.pallas import tpu as pltpu
from jax.sharding import PartitionSpec as P

MARGIN = 128
BAND = 24
STEEP = 4.0
THRESH = 0.6

HALF = 64
AXES = ("row", "col", "cond")
BF = jnp.bfloat16
F32 = jnp.float32


def pieces(table, count):
    out, rest = [], np.asarray(table, np.float32)
    for _ in range(count):
        part = rest.astype(BF)
        out.append(part)
        rest = rest - part.astype(np.float32)
    return out


def angles(left, right, period):
    left, right = np.asarray(left, np.int64), np.asarray(right, np.int64)
    return (left[:, None] * right[None, :] % period) * (2.0 * math.pi / period)


def frequencies():
    return np.arange(BAND) - BAND // 2


def lanes(*blocks):
    rows = blocks[0][1].shape[0]
    width = -(-max(at + block.shape[1] for at, block in blocks) // 128) * 128
    out = np.zeros((rows, width))
    for at, block in blocks:
        out[:, at : at + block.shape[1]] = block
    return out


def rows_at(height, *blocks):
    out = np.zeros((height, blocks[0][1].shape[1]))
    for at, block in blocks:
        out[at : at + block.shape[0]] = block
    return out


def three(table):
    high, low = pieces(table, 2)
    return np.concatenate([high, high, low], 1)


def stacked(table, count):
    return np.concatenate(pieces(table, count), 0)


def local_tables(tile, window):
    places = np.arange(tile)
    col_table = []
    for shift in (MARGIN, 0, 2 * MARGIN):
        phase = angles(places + shift, frequencies(), window)
        block = np.concatenate([np.cos(phase), -np.sin(phase)], 1) / window
        col_table.append(stacked(lanes((0, block), (HALF, block)), 2))
    phase = angles(frequencies(), places + MARGIN, window)
    row_table = three(np.concatenate([np.cos(phase), -np.sin(phase)], 0))
    phase = angles(frequencies(), np.full(HALF, MARGIN), window)
    cos, sin = np.cos(phase), np.sin(phase)
    turn = np.concatenate([np.concatenate([cos, cos], 1), np.concatenate([sin, -sin], 1)], 0)
    return np.concatenate(col_table, 0), row_table, turn.astype(np.float32)


def field_tables(tile, window):
    count = 2 * BAND
    points = np.arange(count)
    phase = angles(frequencies(), points, count)
    cos, sin = np.cos(phase), np.sin(phase)
    one = np.concatenate(
        [lanes((0, cos), (HALF, sin)), lanes((0, -sin), (HALF, cos)), np.zeros((HALF - count, 2 * HALF))]
    )
    none = np.zeros_like(one)
    to_cols = np.concatenate(
        [np.concatenate([one, none], 1), np.concatenate([none, one], 1)], 0
    )
    to_rows = np.concatenate([cos.T, -sin.T], 1)
    where = (np.arange(tile)[:, None] + MARGIN) / window - points[None, :] / count
    spread = np.ones((tile, count))
    for order in range(1, BAND):
        spread += 2.0 * np.cos(2.0 * math.pi * order * where)
    spread /= count
    spread_cols = rows_at(HALF, (0, spread.T))
    gather_cols = lanes((0, spread), (HALF, spread))
    from_rows = np.concatenate([cos, sin], 0)
    return (
        stacked(to_cols, 2),
        three(to_rows),
        stacked(spread_cols, 2),
        three(spread),
        three(spread.T),
        stacked(gather_cols, 2),
        three(from_rows),
        np.concatenate(pieces(to_cols.T, 2), 1),
    )


def adjoint_tables(tile, window):
    places = np.arange(tile) + MARGIN
    phase = angles(frequencies(), places, window)
    cos, sin = np.cos(phase), np.sin(phase)
    first = np.concatenate([cos, -sin], 1)
    second = np.concatenate([-sin, -cos], 1)
    cols = rows_at(
        2 * HALF, (0, first), (BAND, first), (HALF, second), (HALF + BAND, second)
    )
    rows = np.concatenate([cos.T, sin.T], 1) / window
    return stacked(cols, 2), three(rows)


def toward(at, core, line, size):
    onward = lax.rem(core + line, 2) == 0
    other = jnp.where(onward, at + 1, at - 1)
    return onward, (other >= 0) & (other < size)


def dot(left, right):
    return jnp.dot(left, right, preferred_element_type=F32)


def split(value, count):
    out, rest = [], value
    for step in range(count):
        part = rest.astype(BF)
        out.append(part)
        if step + 1 < count:
            rest = rest - part.astype(F32)
    return out


def lane_ids(shape):
    return lax.broadcasted_iota(jnp.int32, shape, len(shape) - 1)


def doubled(value):
    high = value.astype(BF).astype(F32)
    part = jnp.where(lane_ids(value.shape) < HALF, high, value - high).astype(BF)
    return jnp.concatenate([part, part], 1)


def four_weights(ref):
    size = ref.shape[0] // 2
    high, low = ref[:size], ref[size:]
    return jnp.concatenate([high, high, low, low], 0)


def three_right(value):
    high, low = split(value, 2)
    return jnp.concatenate([high, low, high], 0)


def fetch(sources, targets, sems):
    copies = [
        pltpu.make_async_copy(source, target, sems.at[at])
        for at, (source, target) in enumerate(zip(sources, targets))
    ]
    for copy in copies:
        copy.start()
    return copies


def local_spectrum(tile_value, col_table, row_table, turn):
    size = col_table.shape[0] // 2
    high, low = split(tile_value, 2)
    ch, cl = col_table[:size], col_table[size:]
    partial = dot(jnp.concatenate([high, low], 1), jnp.concatenate([ch, ch], 0)) + dot(high, cl)
    both = dot(row_table, three_right(partial))
    lane = lane_ids((BAND, both.shape[1])) % HALF

    def times_i(value):
        return jnp.where(
            lane < BAND,
            -pltpu.roll(value, value.shape[1] - BAND, 1),
            jnp.where(lane < 2 * BAND, pltpu.roll(value, BAND, 1), 0.0),
        )

    centre = both[:BAND] + times_i(both[BAND:])
    ends = turn[:BAND] * centre + turn[BAND:] * times_i(centre)
    return jnp.concatenate([ends, centre], 0)


def open_kernel(*refs):
    cond_hbm, dose_hbm, mask_hbm, kernels_hbm = refs[:4]
    cond_ref, dose_ref, mask_ref, sems = refs[-4:]
    count = (len(refs) - 11) // 2
    sources, targets = refs[4 : 4 + count], refs[7 + count : 7 + 2 * count]
    own_ref, chosen_ref, strength_ref = refs[4 + count : 7 + count]
    conds = cond_hbm.shape[0]
    copies = []

    def start(source, target):
        copy = pltpu.make_async_copy(source, target, sems.at[len(copies)])
        copy.start()
        copies.append(copy)
        return copy

    scalars = [start(cond_hbm, cond_ref), start(dose_hbm, dose_ref)]
    first = [start(mask_hbm, mask_ref)]
    first += [start(source, target) for source, target in zip(sources[:3], targets[:3])]
    for copy in scalars:
        copy.wait()
    rest = [start(kernels_hbm.at[cond_ref[c]], chosen_ref.at[c]) for c in range(conds)]
    rest += [start(source, target) for source, target in zip(sources[3:], targets[3:])]
    for c in range(conds):
        strength_ref[c] = jnp.full(strength_ref.shape[1:], dose_ref[cond_ref[c]], F32)
    for copy in first:
        copy.wait()
    col_ref, row_ref, turn_ref = targets[:3]
    own_ref[...] = local_spectrum(
        mask_ref[...], col_ref[: 2 * mask_ref.shape[0]], row_ref[...], turn_ref[...]
    )
    for copy in rest:
        copy.wait()


def near_kernel(mesh_shape, tile_ref, col_ref, row_ref, turn_ref, out_ref):
    row, col, core = (lax.axis_index(name) for name in AXES)
    right, valid = toward(col, core, row, mesh_shape[1])
    size = 2 * tile_ref.shape[0]
    at = pl.multiple_of(jnp.where(right, 2 * size, size), size)
    share = local_spectrum(tile_ref[...], col_ref[pl.ds(at, size)], row_ref[...], turn_ref[...])
    out_ref[...] = jnp.where(valid, share, 0.0)


def arrange_kernel(real_ref, imag_ref, first_ref, second_ref):
    total = real_ref.shape[0] // BAND
    for pair in range(total // 2):
        first, second = 0.0, 0.0
        for part in range(2):
            at = (2 * pair + part) * BAND
            pad = jnp.zeros((BAND, 2 * HALF - BAND), F32)
            real = jnp.concatenate([real_ref[at : at + BAND, :], pad], 1)
            imag = jnp.concatenate([imag_ref[at : at + BAND, :], pad], 1)

            def moved(value, by):
                return pltpu.roll(value, part * HALF + by, 1) if part * HALF + by else value

            first = first + (moved(real, 0) + moved(imag, BAND))
            second = second + (moved(real, BAND) - moved(imag, 0))
        first_ref[:, pair * 2 * HALF : (pair + 1) * 2 * HALF] = first
        second_ref[:, pair * 2 * HALF : (pair + 1) * 2 * HALF] = second


def row_block(mesh_shape, value, core):
    row, col, _ = (lax.axis_index(name) for name in AXES)
    onward, valid = toward(row, core, col, mesh_shape[0])
    low_half = lane_ids(value.shape) < HALF
    kept = jnp.where(onward, jnp.where(low_half, 0.0, value), jnp.where(low_half, value, 0.0))
    kept = jnp.where(valid, kept, 0.0)
    return kept + pltpu.roll(kept, HALF, 1)


def spread_lanes(value):
    lane = lane_ids(value.shape) % HALF
    real = jnp.where(lane < BAND, value, 0.0)
    imag = jnp.where(lane >= BAND, value, 0.0)
    return real + pltpu.roll(real, BAND, 1), imag + pltpu.roll(imag, 2 * HALF - BAND, 1)


def base_kernel(mesh_shape, own_ref, near_ref, far_ref, side_ref, out_ref):
    value = own_ref[BAND:] + near_ref[BAND:] + far_ref[BAND:]
    value += row_block(mesh_shape, side_ref[...], lax.axis_index("cond"))
    out_ref[:BAND], out_ref[BAND:] = spread_lanes(value)


def field_kernel(
    mesh_shape, strength_ref, base_ref, other_ref,
    first_ref, second_ref, target_ref, to_cols_ref, to_rows_ref, spread_cols_ref, spread_ref,
    gather_rows_ref, gather_cols_ref, from_rows_ref, from_cols_ref, out_ref, rows_ref, field_ref,
):
    conds = strength_ref.shape[0]
    count = 2 * BAND
    per = first_ref.shape[1] // HALF // conds
    tile = target_ref.shape[0]
    wide = 4 * HALF
    core = lax.axis_index("cond")
    real, imag = spread_lanes(row_block(mesh_shape, other_ref[...], 1 - core))
    real, imag = base_ref[:BAND] + real, base_ref[BAND:] + imag

    to_rows = to_rows_ref[...]
    th, tl = to_cols_ref[: 2 * HALF], to_cols_ref[2 * HALF :]
    to_cols = jnp.concatenate([th, th, tl], 0)
    spread_cols = four_weights(spread_cols_ref)
    gather_cols = gather_cols_ref[...]
    gather_cols = jnp.concatenate([gather_cols[:tile], gather_cols], 0)
    from_cols = from_cols_ref[...]
    from_cols = jnp.concatenate(
        [
            from_cols,
            jnp.concatenate([from_cols[:, : 2 * HALF], jnp.zeros((wide, 2 * HALF), BF)], 1),
        ],
        0,
    )
    from_rows = from_rows_ref[...]
    goal = target_ref[...].astype(F32)
    norm = 1.0 / (per * BAND * BAND)
    pairs = per // 2

    def pair_lanes(ref, pair, width=1):
        return ref[:, pair * 2 * HALF : (pair + width) * 2 * HALF]

    def condition(c, sums):
        first, last = c * pairs, (c + 1) * pairs
        for quad in range(first, last, 2):
            blocks = []
            for pair in (quad, quad + 1):
                one, two = pair_lanes(first_ref, pair), pair_lanes(second_ref, pair)
                blocks.append(
                    jnp.concatenate([one * real + two * imag, one * imag - two * real], 0)
                )
            both = dot(to_rows, three_right(jnp.concatenate(blocks, 1)))
            rows_ref[quad * count : (quad + 1) * count, :] = both[:, : 2 * HALF]
            rows_ref[(quad + 1) * count : (quad + 2) * count, :] = both[:, 2 * HALF :]
            yield
        total = 0.0
        rows = slice(first * count, last * count)
        high, low = split(rows_ref[rows, :], 2)
        field_ref[rows, :] = dot(jnp.concatenate([high, low, high], 1), to_cols)
        for pair in range(first, last):
            both = field_ref[pair * count : (pair + 1) * count, :]
            squares = both * both
            total = total + (squares[:, : 2 * HALF] + squares[:, 2 * HALF :])
        yield
        coarse = total + pltpu.roll(total, HALF, 1)
        lines = dot(doubled(coarse), spread_cols)
        yield
        intensity = dot(spread_ref[...], three_right(lines)) * norm
        strength = strength_ref[c][:1]
        resist = jax.nn.sigmoid(STEEP * (strength * intensity - THRESH))
        slope = (resist - goal) * resist * (1.0 - resist)
        slope = slope * (4.0 * STEEP * norm * strength)
        yield
        back = dot(gather_rows_ref[...], three_right(slope))
        yield
        high, low = split(back, 2)
        slope = dot(jnp.concatenate([high, low, high], 1), gather_cols)
        slope = jnp.concatenate([slope, slope], 1)
        yield
        for pair in range(first, last):
            part = slice(pair * count, (pair + 1) * count)
            field_ref[part, :] = field_ref[part, :] * slope
        back = dot(jnp.concatenate(split(field_ref[rows, :], 2), 1), from_cols)
        rows_ref[rows, :] = back[:, : 2 * HALF] + back[:, 2 * HALF :]
        yield
        for quad in range(first, last, 2):
            value = jnp.concatenate(
                [
                    rows_ref[quad * count : (quad + 1) * count, :],
                    rows_ref[(quad + 1) * count : (quad + 2) * count, :],
                ],
                1,
            )
            back = dot(from_rows, three_right(value))
            top, bottom = back[:BAND], back[BAND:]
            one, two = pair_lanes(first_ref, quad, 2), pair_lanes(second_ref, quad, 2)
            sums[0] = sums[0] + (one * top + two * bottom)
            sums[1] = sums[1] + (two * top - one * bottom)
            yield

    sums = [0.0, 0.0]
    for _ in zip_longest(*(condition(c, sums) for c in range(conds))):
        pass
    sum_one, sum_two = (value[:, : 2 * HALF] + value[:, 2 * HALF :] for value in sums)
    out_ref[...] = jnp.where(
        lane_ids(sum_one.shape) < HALF,
        sum_one + pltpu.roll(sum_one, HALF, 1),
        sum_two + pltpu.roll(sum_two, HALF, 1),
    )


def adjoint_kernel(mine_ref, theirs_ref, cols_ref, rows_ref, out_ref):
    tile = out_ref.shape[1]
    high, low = split(mine_ref[...] + theirs_ref[...], 2)
    size = cols_ref.shape[0] // 2
    ch, cl = cols_ref[:size], cols_ref[size:]
    halves = dot(jnp.concatenate([high, low, high], 1), jnp.concatenate([ch, ch, cl], 0))
    joined = jnp.concatenate([halves[:, :tile], halves[:, tile:]], 0)
    out_ref[...] = dot(rows_ref[...], three_right(joined))


VMEM = pl.BlockSpec(memory_space=pltpu.VMEM)
SMEM = pl.BlockSpec(memory_space=pltpu.SMEM)
HBM = pl.BlockSpec(memory_space=pltpu.HBM)


def call(body, outs, specs, args, scratch=(), flops=1000000, grant=8):
    shapes = [
        shape if hasattr(shape, "dtype") else jax.ShapeDtypeStruct(shape, F32) for shape in outs
    ]
    one = len(outs) == 1
    args = [
        pltpu.with_memory_space_constraint(value, pltpu.HBM) if spec is HBM else value
        for spec, value in zip(specs, args)
    ]
    return pl.pallas_call(
        body,
        out_shape=shapes[0] if one else shapes,
        in_specs=specs,
        out_specs=VMEM if one else [VMEM] * len(outs),
        scratch_shapes=list(scratch),
        compiler_params=pltpu.CompilerParams(vmem_limit_bytes=grant * 2**20),
        cost_estimate=pl.CostEstimate(flops=flops, bytes_accessed=1000000, transcendentals=0),
    )(*args)


def swaps(mesh_shape, along):
    rows, cols, cores = mesh_shape
    out = []
    for r in range(rows):
        for c in range(cols):
            for k in range(cores):
                at, line, size = (r, c, rows) if along == 0 else (c, r, cols)
                other = at + 1 if (k + line) % 2 == 0 else at - 1
                inside = 0 <= other < size
                at, line = (other, line) if inside else (at, line ^ 1)
                to = (at, line) if along == 0 else (line, at)
                if to[0] < rows and to[1] < cols:
                    out.append(((r * cols + c) * cores + k, (to[0] * cols + to[1]) * cores + 1 - k))
    return out


def shards(mesh_shape, mask, target, cond_index, kernels, dose):
    tile = mask.shape[0]
    window = tile + 2 * MARGIN
    swap = [(0, 1), (1, 0)]
    conds = cond_index.shape[0]
    count = kernels.shape[2]
    block = (2 * BAND, 2 * HALF)
    beside = lax.ppermute(mask, AXES, swaps(mesh_shape, 1))
    fetched = local_tables(tile, window) + (target,)
    fetched += field_tables(tile, window) + adjoint_tables(tile, window)
    own, chosen, strength, *fetched = call(
        open_kernel,
        [block, (conds, count, 2, BAND * BAND), (conds, 8, tile)]
        + [jax.ShapeDtypeStruct(value.shape, value.dtype) for value in fetched],
        [HBM] * (4 + len(fetched)),
        (cond_index, dose, mask, jnp.transpose(kernels, (0, 2, 1, 3))) + fetched,
        scratch=[
            pltpu.SMEM(cond_index.shape, jnp.int32),
            pltpu.SMEM(dose.shape, F32),
            pltpu.VMEM(mask.shape, F32),
            pltpu.SemaphoreType.DMA((3 + conds + len(fetched),)),
        ],
    )
    beside, own, chosen, strength, fetched = lax.optimization_barrier(
        (beside, own, chosen, strength, fetched)
    )
    *local, later_target = fetched[:4]
    later = [later_target, *fetched[4:]]
    near = call(
        functools.partial(near_kernel, mesh_shape), [block], [VMEM] * 4, (beside, *local)
    )
    far = lax.ppermute(near, "cond", swap)
    real = chosen[:, :, 0].reshape(conds * count * BAND, BAND)
    imag = chosen[:, :, 1].reshape(conds * count * BAND, BAND)
    far, real, imag = lax.optimization_barrier((far, real, imag))
    message = own[:BAND] + near[:BAND] + far[:BAND]
    side = lax.ppermute(message, AXES, swaps(mesh_shape, 0))
    total = conds * count
    arranged = call(arrange_kernel, [(BAND, total * HALF)] * 2, [VMEM] * 2, (real, imag))
    side, arranged = lax.optimization_barrier((side, arranged))
    other = lax.ppermute(side, "cond", swap)
    base = call(
        functools.partial(base_kernel, mesh_shape), [block], [VMEM] * 4, (own, near, far, side)
    )
    other, base = lax.optimization_barrier((other, base))

    cotangent = call(
        functools.partial(field_kernel, mesh_shape),
        [(BAND, 2 * HALF)],
        [VMEM] * 14,
        (strength, base, other, *arranged, *later[:-2]),
        scratch=[
            pltpu.VMEM((total * BAND, 2 * HALF), F32),
            pltpu.VMEM((total * BAND, 4 * HALF), F32),
        ],
    )
    theirs = lax.ppermute(cotangent, "cond", swap)
    return call(
        adjoint_kernel, [(tile, tile)], [VMEM] * 4, (cotangent, theirs, *later[-2:])
    )


def solution(mesh):
    in_specs = (P("row", "col"), P("row", "col"), P("cond"), P(), P())
    out_specs = P("row", "col")
    shape = tuple(mesh.shape[name] for name in AXES)
    body = functools.partial(shards, shape)
    return jax.shard_map(body, mesh=mesh, in_specs=in_specs, out_specs=out_specs, check_vma=False)
```

```python
import functools
import math
from itertools import zip_longest

import jax
import jax.numpy as jnp
import numpy as np
from jax import lax
from jax.experimental import pallas as pl
from jax.experimental.pallas import tpu as pltpu
from jax.sharding import PartitionSpec as P

MARGIN = 128
BAND = 24
STEEP = 4.0
THRESH = 0.6

HALF = 64
AXES = ("row", "col", "cond")
BF = jnp.bfloat16
F32 = jnp.float32


def pieces(table, count):
    out, rest = [], np.asarray(table, np.float32)
    for _ in range(count):
        part = rest.astype(BF)
        out.append(part)
        rest = rest - part.astype(np.float32)
    return out


def angles(left, right, period):
    left, right = np.asarray(left, np.int64), np.asarray(right, np.int64)
    return (left[:, None] * right[None, :] % period) * (2.0 * math.pi / period)


def frequencies():
    return np.arange(BAND) - BAND // 2


def lanes(*blocks):
    rows = blocks[0][1].shape[0]
    width = -(-max(at + block.shape[1] for at, block in blocks) // 128) * 128
    out = np.zeros((rows, width))
    for at, block in blocks:
        out[:, at : at + block.shape[1]] = block
    return out


def rows_at(height, *blocks):
    out = np.zeros((height, blocks[0][1].shape[1]))
    for at, block in blocks:
        out[at : at + block.shape[0]] = block
    return out


def three(table):
    high, low = pieces(table, 2)
    return np.concatenate([high, high, low], 1)


def stacked(table, count):
    return np.concatenate(pieces(table, count), 0)


def local_tables(tile, window):
    places = np.arange(tile)
    col_table = []
    for shift in (MARGIN, 0, 2 * MARGIN):
        phase = angles(places + shift, frequencies(), window)
        block = np.concatenate([np.cos(phase), -np.sin(phase)], 1) / window
        col_table.append(stacked(lanes((0, block), (HALF, block)), 2))
    phase = angles(frequencies(), places + MARGIN, window)
    row_table = three(np.concatenate([np.cos(phase), -np.sin(phase)], 0))
    phase = angles(frequencies(), np.full(HALF, MARGIN), window)
    cos, sin = np.cos(phase), np.sin(phase)
    turn = np.concatenate([np.concatenate([cos, cos], 1), np.concatenate([sin, -sin], 1)], 0)
    return np.concatenate(col_table, 0), row_table, turn.astype(np.float32)


def field_tables(tile, window):
    count = 2 * BAND
    points = np.arange(count)
    phase = angles(frequencies(), points, count)
    cos, sin = np.cos(phase), np.sin(phase)
    one = np.concatenate(
        [lanes((0, cos), (HALF, sin)), lanes((0, -sin), (HALF, cos)), np.zeros((HALF - count, 2 * HALF))]
    )
    none = np.zeros_like(one)
    to_cols = np.concatenate(
        [np.concatenate([one, none], 1), np.concatenate([none, one], 1)], 0
    )
    to_rows = np.concatenate([cos.T, -sin.T], 1)
    where = (np.arange(tile)[:, None] + MARGIN) / window - points[None, :] / count
    spread = np.ones((tile, count))
    for order in range(1, BAND):
        spread += 2.0 * np.cos(2.0 * math.pi * order * where)
    spread /= count
    spread_cols = rows_at(HALF, (0, spread.T))
    gather_cols = lanes((0, spread), (HALF, spread))
    from_rows = np.concatenate([cos, sin], 0)
    return (
        stacked(to_cols, 2),
        three(to_rows),
        stacked(spread_cols, 2),
        three(spread),
        three(spread.T),
        stacked(gather_cols, 2),
        three(from_rows),
        np.concatenate(pieces(to_cols.T, 2), 1),
    )


def adjoint_tables(tile, window):
    places = np.arange(tile) + MARGIN
    phase = angles(frequencies(), places, window)
    cos, sin = np.cos(phase), np.sin(phase)
    first = np.concatenate([cos, -sin], 1)
    second = np.concatenate([-sin, -cos], 1)
    cols = rows_at(
        2 * HALF, (0, first), (BAND, first), (HALF, second), (HALF + BAND, second)
    )
    rows = np.concatenate([cos.T, sin.T], 1) / window
    return stacked(cols, 2), three(rows)


def toward(at, core, line, size):
    onward = lax.rem(core + line, 2) == 0
    other = jnp.where(onward, at + 1, at - 1)
    return onward, (other >= 0) & (other < size)


def dot(left, right):
    return jnp.dot(left, right, preferred_element_type=F32)


def split(value, count):
    out, rest = [], value
    for step in range(count):
        part = rest.astype(BF)
        out.append(part)
        if step + 1 < count:
            rest = rest - part.astype(F32)
    return out


def lane_ids(shape):
    return lax.broadcasted_iota(jnp.int32, shape, len(shape) - 1)


def doubled(value):
    high = value.astype(BF).astype(F32)
    part = jnp.where(lane_ids(value.shape) < HALF, high, value - high).astype(BF)
    return jnp.concatenate([part, part], 1)


def four_weights(ref):
    size = ref.shape[0] // 2
    high, low = ref[:size], ref[size:]
    return jnp.concatenate([high, high, low, low], 0)


def three_right(value):
    high, low = split(value, 2)
    return jnp.concatenate([high, low, high], 0)


def fetch(sources, targets, sems):
    copies = [
        pltpu.make_async_copy(source, target, sems.at[at])
        for at, (source, target) in enumerate(zip(sources, targets))
    ]
    for copy in copies:
        copy.start()
    return copies


def local_spectrum(tile_value, col_table, row_table, turn):
    size = col_table.shape[0] // 2
    high, low = split(tile_value, 2)
    ch, cl = col_table[:size], col_table[size:]
    partial = dot(jnp.concatenate([high, low], 1), jnp.concatenate([ch, ch], 0)) + dot(high, cl)
    both = dot(row_table, three_right(partial))
    lane = lane_ids((BAND, both.shape[1])) % HALF

    def times_i(value):
        return jnp.where(
            lane < BAND,
            -pltpu.roll(value, value.shape[1] - BAND, 1),
            jnp.where(lane < 2 * BAND, pltpu.roll(value, BAND, 1), 0.0),
        )

    centre = both[:BAND] + times_i(both[BAND:])
    ends = turn[:BAND] * centre + turn[BAND:] * times_i(centre)
    return jnp.concatenate([ends, centre], 0)


def open_kernel(*refs):
    cond_hbm, dose_hbm, mask_hbm, kernels_hbm = refs[:4]
    cond_ref, dose_ref, mask_ref, sems = refs[-4:]
    count = (len(refs) - 11) // 2
    sources, targets = refs[4 : 4 + count], refs[7 + count : 7 + 2 * count]
    own_ref, chosen_ref, strength_ref = refs[4 + count : 7 + count]
    conds = cond_hbm.shape[0]
    copies = []

    def start(source, target):
        copy = pltpu.make_async_copy(source, target, sems.at[len(copies)])
        copy.start()
        copies.append(copy)
        return copy

    scalars = [start(cond_hbm, cond_ref), start(dose_hbm, dose_ref)]
    first = [start(mask_hbm, mask_ref)]
    first += [start(source, target) for source, target in zip(sources[:3], targets[:3])]
    for copy in scalars:
        copy.wait()
    rest = [start(kernels_hbm.at[cond_ref[c]], chosen_ref.at[c]) for c in range(conds)]
    rest += [start(source, target) for source, target in zip(sources[3:], targets[3:])]
    for c in range(conds):
        strength_ref[c] = jnp.full(strength_ref.shape[1:], dose_ref[cond_ref[c]], F32)
    for copy in first:
        copy.wait()
    col_ref, row_ref, turn_ref = targets[:3]
    own_ref[...] = local_spectrum(
        mask_ref[...], col_ref[: 2 * mask_ref.shape[0]], row_ref[...], turn_ref[...]
    )
    for copy in rest:
        copy.wait()


def near_kernel(mesh_shape, tile_ref, col_ref, row_ref, turn_ref, out_ref):
    row, col, core = (lax.axis_index(name) for name in AXES)
    right, valid = toward(col, core, row, mesh_shape[1])
    size = 2 * tile_ref.shape[0]
    at = pl.multiple_of(jnp.where(right, 2 * size, size), size)
    share = local_spectrum(tile_ref[...], col_ref[pl.ds(at, size)], row_ref[...], turn_ref[...])
    out_ref[...] = jnp.where(valid, share, 0.0)


def arrange_kernel(real_ref, imag_ref, first_ref, second_ref):
    total = real_ref.shape[0] // BAND
    for pair in range(total // 2):
        first, second = 0.0, 0.0
        for part in range(2):
            at = (2 * pair + part) * BAND
            pad = jnp.zeros((BAND, 2 * HALF - BAND), F32)
            real = jnp.concatenate([real_ref[at : at + BAND, :], pad], 1)
            imag = jnp.concatenate([imag_ref[at : at + BAND, :], pad], 1)

            def moved(value, by):
                return pltpu.roll(value, part * HALF + by, 1) if part * HALF + by else value

            first = first + (moved(real, 0) + moved(imag, BAND))
            second = second + (moved(real, BAND) - moved(imag, 0))
        first_ref[:, pair * 2 * HALF : (pair + 1) * 2 * HALF] = first
        second_ref[:, pair * 2 * HALF : (pair + 1) * 2 * HALF] = second


def row_block(mesh_shape, value, core):
    row, col, _ = (lax.axis_index(name) for name in AXES)
    onward, valid = toward(row, core, col, mesh_shape[0])
    low_half = lane_ids(value.shape) < HALF
    kept = jnp.where(onward, jnp.where(low_half, 0.0, value), jnp.where(low_half, value, 0.0))
    kept = jnp.where(valid, kept, 0.0)
    return kept + pltpu.roll(kept, HALF, 1)


def spread_lanes(value):
    lane = lane_ids(value.shape) % HALF
    real = jnp.where(lane < BAND, value, 0.0)
    imag = jnp.where(lane >= BAND, value, 0.0)
    return real + pltpu.roll(real, BAND, 1), imag + pltpu.roll(imag, 2 * HALF - BAND, 1)


def base_kernel(mesh_shape, own_ref, near_ref, far_ref, side_ref, out_ref):
    value = own_ref[BAND:] + near_ref[BAND:] + far_ref[BAND:]
    value += row_block(mesh_shape, side_ref[...], lax.axis_index("cond"))
    out_ref[:BAND], out_ref[BAND:] = spread_lanes(value)


def field_kernel(
    mesh_shape, strength_ref, base_ref, other_ref,
    first_ref, second_ref, target_ref, to_cols_ref, to_rows_ref, spread_cols_ref, spread_ref,
    gather_rows_ref, gather_cols_ref, from_rows_ref, from_cols_ref, out_ref, rows_ref, field_ref,
):
    conds = strength_ref.shape[0]
    count = 2 * BAND
    per = first_ref.shape[1] // HALF // conds
    tile = target_ref.shape[0]
    wide = 4 * HALF
    core = lax.axis_index("cond")
    real, imag = spread_lanes(row_block(mesh_shape, other_ref[...], 1 - core))
    real, imag = base_ref[:BAND] + real, base_ref[BAND:] + imag

    to_rows = to_rows_ref[...]
    th, tl = to_cols_ref[: 2 * HALF], to_cols_ref[2 * HALF :]
    to_cols = jnp.concatenate([th, th, tl], 0)
    spread_cols = four_weights(spread_cols_ref)
    gather_cols = gather_cols_ref[...]
    gather_cols = jnp.concatenate([gather_cols[:tile], gather_cols], 0)
    from_cols = from_cols_ref[...]
    from_cols = jnp.concatenate(
        [
            from_cols,
            jnp.concatenate([from_cols[:, : 2 * HALF], jnp.zeros((wide, 2 * HALF), BF)], 1),
        ],
        0,
    )
    from_rows = from_rows_ref[...]
    goal = target_ref[...].astype(F32)
    norm = 1.0 / (per * BAND * BAND)
    pairs = per // 2

    def pair_lanes(ref, pair, width=1):
        return ref[:, pair * 2 * HALF : (pair + width) * 2 * HALF]

    def condition(c, sums):
        first, last = c * pairs, (c + 1) * pairs
        for quad in range(first, last, 2):
            blocks = []
            for pair in (quad, quad + 1):
                one, two = pair_lanes(first_ref, pair), pair_lanes(second_ref, pair)
                blocks.append(
                    jnp.concatenate([one * real + two * imag, one * imag - two * real], 0)
                )
            both = dot(to_rows, three_right(jnp.concatenate(blocks, 1)))
            rows_ref[quad * count : (quad + 1) * count, :] = both[:, : 2 * HALF]
            rows_ref[(quad + 1) * count : (quad + 2) * count, :] = both[:, 2 * HALF :]
            yield
        total = 0.0
        rows = slice(first * count, last * count)
        high, low = split(rows_ref[rows, :], 2)
        field_ref[rows, :] = dot(jnp.concatenate([high, low, high], 1), to_cols)
        for pair in range(first, last):
            both = field_ref[pair * count : (pair + 1) * count, :]
            squares = both * both
            total = total + (squares[:, : 2 * HALF] + squares[:, 2 * HALF :])
        yield
        coarse = total + pltpu.roll(total, HALF, 1)
        lines = dot(doubled(coarse), spread_cols)
        yield
        intensity = dot(spread_ref[...], three_right(lines)) * norm
        strength = strength_ref[c][:1]
        resist = jax.nn.sigmoid(STEEP * (strength * intensity - THRESH))
        slope = (resist - goal) * resist * (1.0 - resist)
        slope = slope * (4.0 * STEEP * norm * strength)
        yield
        back = dot(gather_rows_ref[...], three_right(slope))
        yield
        high, low = split(back, 2)
        slope = dot(jnp.concatenate([high, low, high], 1), gather_cols)
        slope = jnp.concatenate([slope, slope], 1)
        yield
        for pair in range(first, last):
            part = slice(pair * count, (pair + 1) * count)
            field_ref[part, :] = field_ref[part, :] * slope
        back = dot(jnp.concatenate(split(field_ref[rows, :], 2), 1), from_cols)
        rows_ref[rows, :] = back[:, : 2 * HALF] + back[:, 2 * HALF :]
        yield
        for quad in range(first, last, 2):
            value = jnp.concatenate(
                [
                    rows_ref[quad * count : (quad + 1) * count, :],
                    rows_ref[(quad + 1) * count : (quad + 2) * count, :],
                ],
                1,
            )
            back = dot(from_rows, three_right(value))
            top, bottom = back[:BAND], back[BAND:]
            one, two = pair_lanes(first_ref, quad, 2), pair_lanes(second_ref, quad, 2)
            sums[0] = sums[0] + (one * top + two * bottom)
            sums[1] = sums[1] + (two * top - one * bottom)
            yield

    sums = [0.0, 0.0]
    steps = [condition(c, sums) for c in range(conds)]
    for step in steps:
        for _ in range(pairs // 2):
            next(step)
    for _ in zip_longest(*steps):
        pass
    sum_one, sum_two = (value[:, : 2 * HALF] + value[:, 2 * HALF :] for value in sums)
    out_ref[...] = jnp.where(
        lane_ids(sum_one.shape) < HALF,
        sum_one + pltpu.roll(sum_one, HALF, 1),
        sum_two + pltpu.roll(sum_two, HALF, 1),
    )


def adjoint_kernel(mine_ref, theirs_ref, cols_ref, rows_ref, out_ref):
    tile = out_ref.shape[1]
    high, low = split(mine_ref[...] + theirs_ref[...], 2)
    size = cols_ref.shape[0] // 2
    ch, cl = cols_ref[:size], cols_ref[size:]
    halves = dot(jnp.concatenate([high, low, high], 1), jnp.concatenate([ch, ch, cl], 0))
    joined = jnp.concatenate([halves[:, :tile], halves[:, tile:]], 0)
    out_ref[...] = dot(rows_ref[...], three_right(joined))


VMEM = pl.BlockSpec(memory_space=pltpu.VMEM)
SMEM = pl.BlockSpec(memory_space=pltpu.SMEM)
HBM = pl.BlockSpec(memory_space=pltpu.HBM)


def call(body, outs, specs, args, scratch=(), flops=1000000, grant=8):
    shapes = [
        shape if hasattr(shape, "dtype") else jax.ShapeDtypeStruct(shape, F32) for shape in outs
    ]
    one = len(outs) == 1
    args = [
        pltpu.with_memory_space_constraint(value, pltpu.HBM) if spec is HBM else value
        for spec, value in zip(specs, args)
    ]
    return pl.pallas_call(
        body,
        out_shape=shapes[0] if one else shapes,
        in_specs=specs,
        out_specs=VMEM if one else [VMEM] * len(outs),
        scratch_shapes=list(scratch),
        compiler_params=pltpu.CompilerParams(vmem_limit_bytes=grant * 2**20),
        cost_estimate=pl.CostEstimate(flops=flops, bytes_accessed=1000000, transcendentals=0),
    )(*args)


def swaps(mesh_shape, along):
    rows, cols, cores = mesh_shape
    out = []
    for r in range(rows):
        for c in range(cols):
            for k in range(cores):
                at, line, size = (r, c, rows) if along == 0 else (c, r, cols)
                other = at + 1 if (k + line) % 2 == 0 else at - 1
                inside = 0 <= other < size
                at, line = (other, line) if inside else (at, line ^ 1)
                to = (at, line) if along == 0 else (line, at)
                if to[0] < rows and to[1] < cols:
                    out.append(((r * cols + c) * cores + k, (to[0] * cols + to[1]) * cores + 1 - k))
    return out


def shards(mesh_shape, mask, target, cond_index, kernels, dose):
    tile = mask.shape[0]
    window = tile + 2 * MARGIN
    swap = [(0, 1), (1, 0)]
    conds = cond_index.shape[0]
    count = kernels.shape[2]
    block = (2 * BAND, 2 * HALF)
    beside = lax.ppermute(mask, AXES, swaps(mesh_shape, 1))
    fetched = local_tables(tile, window) + (target,)
    fetched += field_tables(tile, window) + adjoint_tables(tile, window)
    own, chosen, strength, *fetched = call(
        open_kernel,
        [block, (conds, count, 2, BAND * BAND), (conds, 8, tile)]
        + [jax.ShapeDtypeStruct(value.shape, value.dtype) for value in fetched],
        [HBM] * (4 + len(fetched)),
        (cond_index, dose, mask, jnp.transpose(kernels, (0, 2, 1, 3))) + fetched,
        scratch=[
            pltpu.SMEM(cond_index.shape, jnp.int32),
            pltpu.SMEM(dose.shape, F32),
            pltpu.VMEM(mask.shape, F32),
            pltpu.SemaphoreType.DMA((3 + conds + len(fetched),)),
        ],
    )
    beside, own, chosen, strength, fetched = lax.optimization_barrier(
        (beside, own, chosen, strength, fetched)
    )
    *local, later_target = fetched[:4]
    later = [later_target, *fetched[4:]]
    near = call(
        functools.partial(near_kernel, mesh_shape), [block], [VMEM] * 4, (beside, *local)
    )
    far = lax.ppermute(near, "cond", swap)
    real = chosen[:, :, 0].reshape(conds * count * BAND, BAND)
    imag = chosen[:, :, 1].reshape(conds * count * BAND, BAND)
    far, real, imag = lax.optimization_barrier((far, real, imag))
    message = own[:BAND] + near[:BAND] + far[:BAND]
    side = lax.ppermute(message, AXES, swaps(mesh_shape, 0))
    total = conds * count
    arranged = call(arrange_kernel, [(BAND, total * HALF)] * 2, [VMEM] * 2, (real, imag))
    side, arranged = lax.optimization_barrier((side, arranged))
    other = lax.ppermute(side, "cond", swap)
    base = call(
        functools.partial(base_kernel, mesh_shape), [block], [VMEM] * 4, (own, near, far, side)
    )
    other, base = lax.optimization_barrier((other, base))

    cotangent = call(
        functools.partial(field_kernel, mesh_shape),
        [(BAND, 2 * HALF)],
        [VMEM] * 14,
        (strength, base, other, *arranged, *later[:-2]),
        scratch=[
            pltpu.VMEM((total * BAND, 2 * HALF), F32),
            pltpu.VMEM((total * BAND, 4 * HALF), F32),
        ],
    )
    theirs = lax.ppermute(cotangent, "cond", swap)
    return call(
        adjoint_kernel, [(tile, tile)], [VMEM] * 4, (cotangent, theirs, *later[-2:])
    )


def solution(mesh):
    in_specs = (P("row", "col"), P("row", "col"), P("cond"), P(), P())
    out_specs = P("row", "col")
    shape = tuple(mesh.shape[name] for name in AXES)
    body = functools.partial(shards, shape)
    return jax.shard_map(body, mesh=mesh, in_specs=in_specs, out_specs=out_specs, check_vma=False)
```
